32 devices in a mesh: rep: 4 (over z), shard: 4 (over y, x), seq: 2 (over core).
Axes of the slice: x: 2, y: 2, z: 4, core: 2. Of those that a mesh axis runs over, the one named last changes fastest.
Arguments:
- tokens_in: bfloat16 [4096, 1024], P(('rep', 'shard', 'seq')), may hold values from -6 to 6
- doc_lengths: int32 [4, 4], P('rep'), may hold values from 1 to 512, 1024 in all within a row
- attn_gain: float32 [1024], replicated, may hold values from 0.25 to 1.75
- w_query: bfloat16 [1024, 1024], P('shard'), may hold values from -0.1875 to 0.1875
- key_weight: bfloat16 [1024, 512], P('shard'), may hold values from -0.1875 to 0.1875
- value_weight: bfloat16 [1024, 512], P('shard'), may hold values from -0.1875 to 0.1875
- w_output: bfloat16 [1024, 1024], P('shard'), may hold values from -2 to 2
- query_norm_gain: float32 [64], replicated, may hold values from 0.5 to 2
- key_norm_gain: float32 [64], replicated, may hold values from 0.5 to 2
- mlp_gain: float32 [1024], replicated, may hold values from 0.25 to 1.75
- w_gate: bfloat16 [4608, 1024], P('shard'), may hold values from -0.1875 to 0.1875
- w_up: bfloat16 [4608, 1024], P('shard'), may hold values from -0.1875 to 0.1875
- w_down: bfloat16 [4608, 1024], P('shard'), may hold values from -0.09375 to 0.09375
- out_grad: bfloat16 [4096, 1024], P(('rep', 'shard', 'seq')), may hold values from -6 to 6
Outputs:
- act_out: float32 [4096, 1024], P(('rep', 'shard', 'seq'))
- in_grad: float32 [4096, 1024], P(('rep', 'shard', 'seq'))
- grad_attn_gain: float32 [1024], replicated
- grad_query: float32 [1024, 1024], P(('shard', 'seq'))
- grad_key: float32 [1024, 512], P(('shard', 'seq'))
- grad_value: float32 [1024, 512], P(('shard', 'seq'))
- grad_output: float32 [1024, 1024], P(('shard', 'seq'))
- grad_query_gain: float32 [64], replicated
- grad_key_gain: float32 [64], replicated
- grad_mlp_gain: float32 [1024], replicated
- grad_gate: float32 [4608, 1024], P(('shard', 'seq'))
- grad_up: float32 [4608, 1024], P(('shard', 'seq'))
- grad_down: float32 [4608, 1024], P(('shard', 'seq'))
The draws below stay inside these ranges and needn't reach their ends.
Inputs may be any that keep to these rules, and one draw needn't show every extreme that they name: `doc_lengths`: each row sums to 1024, and its largest entry is exactly 512.
All inputs are finite; a program needn't handle non-finite values.
Results may differ from the reference program's by a relative error of at most 0.014.
The reference program's roundings to bfloat16 on the way count: a program that leaves them out, or rounds other values in their place, can miss the bound.
Values may be sent and summed in bfloat16 or wider, within the bound.
No kernel may reach another device: no remote copies, remote signals or barrier semaphores. Data moves between devices by JAX's collectives and lax.ppermute only.
A program may use at most 256 MiB of HBM per device.

```python
import math
import jax
import jax.numpy as jnp
import numpy as np
from jax import lax

MODEL_DIMENSION = 1024
QUERY_HEADS = 16
KEY_VALUE_HEADS = 8
HEAD_SIZE = 64
FEEDFORWARD_SIZE = 4608
REPLICA_TOKENS = 1024
TOKENS = 4096
LENGTH = 512
DOCS = 4
N_REP = 4


def block_levels(rng, dims, pieces, low, top_value):
    level = 1.0
    for position, blocks in pieces:
        draws = jax.random.uniform(jax.random.fold_in(jax.random.fold_in(rng, 6), position), (blocks,), jnp.float32, low / len(pieces), top_value / len(pieces))
        level = level * jnp.repeat(jnp.exp(draws), dims[position] // blocks).reshape((-1,) + (1,) * (len(dims) - 1 - position))
    return level


def profile(amount, total, bound, slope):
    portions = [(1 << 20) // math.isqrt(standing ** slope) + 1 for standing in range(2, amount + 1)]
    rest, holding = total - bound - (amount - 1), [1] * (amount - 1)
    while rest > 0:
        candidates = [i for i in range(amount - 1) if holding[i] < bound]
        whole, remaining = sum([portions[i] for i in candidates]), rest
        for i in candidates:
            extra = min(bound - holding[i], max(1, remaining * portions[i] // whole), rest)
            holding[i] = holding[i] + extra
            rest = rest - extra
    return np.array([bound] + holding)


def ragged_sizes(key, number_of, total, reach, slope):
    if number_of == 2:
        one = jax.random.randint(key, (), max(1, total - reach), min(reach, total - 1) + 1)
        return jnp.stack([one, total - one])
    tallies = jnp.asarray(profile(number_of, total, reach, slope), jnp.int32)
    couples = (number_of - 1) // 2
    donor, taker = tallies[1:1 + 2 * couples:2], tallies[2:2 + 2 * couples:2]
    room = jnp.minimum(donor - 1, reach - taker)
    shifted = jax.random.randint(jax.random.fold_in(key, 1), (couples,), 0, 1 << 20) % (room + 1)
    tallies = tallies.at[1:1 + 2 * couples:2].set(donor - shifted).at[2:2 + 2 * couples:2].set(taker + shifted)
    return tallies[jax.random.permutation(jax.random.fold_in(key, 2), number_of)]


def scatter_about(own_key, extent, spread, most, split=(), kind=jnp.bfloat16):
    level = block_levels(own_key, extent, split, -0.22, 0.18) if split else 1.0
    result = jax.random.normal(own_key, extent, jnp.float32) * spread * level
    return jnp.minimum(jnp.maximum(result, -most), most).astype(kind)


def setup_inputs(seed: int = 0) -> dict:
    arg_keys = jax.random.split(jax.random.key(seed), 15)
    return {
        "tokens_in": scatter_about(arg_keys[0], (TOKENS, MODEL_DIMENSION), 1.0, 6.0, ((0, 32),)),
        "doc_lengths": jax.vmap(lambda own: ragged_sizes(own, DOCS, REPLICA_TOKENS, LENGTH, 2))(jax.random.split(arg_keys[1], N_REP)).reshape((N_REP, DOCS)).astype(jnp.int32),
        "attn_gain": jnp.clip(1.0 + 0.15 * jax.random.normal(arg_keys[2], (MODEL_DIMENSION,), jnp.float32), 0.25, 1.75),
        "w_query": scatter_about(arg_keys[3], (MODEL_DIMENSION, QUERY_HEADS * HEAD_SIZE), MODEL_DIMENSION ** -0.5, 0.1875, ((0, 4),)),
        "key_weight": scatter_about(arg_keys[4], (MODEL_DIMENSION, KEY_VALUE_HEADS * HEAD_SIZE), MODEL_DIMENSION ** -0.5, 0.1875, ((0, 4),)),
        "value_weight": scatter_about(arg_keys[5], (MODEL_DIMENSION, KEY_VALUE_HEADS * HEAD_SIZE), MODEL_DIMENSION ** -0.5, 0.1875, ((0, 4),)),
        "w_output": scatter_about(arg_keys[6], (MODEL_DIMENSION, QUERY_HEADS * HEAD_SIZE), (max(2, QUERY_HEADS * HEAD_SIZE // 128)) ** -0.5, 2.0, ((0, 4),)),
        "query_norm_gain": jnp.clip(jnp.exp(jax.random.uniform(arg_keys[7], (HEAD_SIZE,), jnp.float32, math.log(0.5), math.log(2.0))), 0.5, 2.0),
        "key_norm_gain": jnp.clip(jnp.exp(jax.random.uniform(arg_keys[8], (HEAD_SIZE,), jnp.float32, math.log(0.5), math.log(2.0))), 0.5, 2.0),
        "mlp_gain": jnp.clip(1.0 + 0.15 * jax.random.normal(arg_keys[9], (MODEL_DIMENSION,), jnp.float32), 0.25, 1.75),
        "w_gate": scatter_about(arg_keys[10], (FEEDFORWARD_SIZE, MODEL_DIMENSION), MODEL_DIMENSION ** -0.5, 0.1875, ((0, 4),)),
        "w_up": scatter_about(arg_keys[11], (FEEDFORWARD_SIZE, MODEL_DIMENSION), MODEL_DIMENSION ** -0.5, 0.1875, ((0, 4),)),
        "w_down": scatter_about(arg_keys[12], (FEEDFORWARD_SIZE, MODEL_DIMENSION), FEEDFORWARD_SIZE ** -0.5, 0.09375, ((0, 4),)),
        "out_grad": scatter_about(arg_keys[13], (TOKENS, MODEL_DIMENSION), 1.0, 6.0, ((0, 32),)),
    }


norm_eps = 1e-05
rope_base = 1000000.0
very_low = -1e+30

def rms_scale(values):
    return lax.rsqrt(lax.optimization_barrier(jnp.mean(values * values, axis=-1, keepdims=True)) + norm_eps)

def root_mean_backward(normed, factor, gain, upstream):
    scaled = upstream * gain
    return factor * (scaled - normed * lax.optimization_barrier(jnp.mean(scaled * normed, axis=-1, keepdims=True)))

def rope_tables(positions, head_dim):
    half_dim = head_dim // 2
    inverse_freq = rope_base ** (-(jnp.arange(half_dim, dtype=jnp.float32) * 2.0 / head_dim))
    angles = positions.astype(jnp.float32)[:, None] * inverse_freq[None, :]
    return (jnp.cos(angles)[:, None, :], jnp.sin(angles)[:, None, :])

def rotate_pairs(values, cosine_table, sine_values):
    half_dim = values.shape[-1] // 2
    lower_half = values[..., :half_dim]
    upper_half = values[..., half_dim:]
    return jnp.concatenate([lower_half * cosine_table - upper_half * sine_values, upper_half * cosine_table + lower_half * sine_values], axis=-1)

def rotate_back(grads, cosine_table, sine_values):
    half_dim = grads.shape[-1] // 2
    lower_half = grads[..., :half_dim]
    upper_half = grads[..., half_dim:]
    return jnp.concatenate([lower_half * cosine_table + upper_half * sine_values, upper_half * cosine_table - lower_half * sine_values], axis=-1)

def doc_info(lengths, positions):
    doc_ends = jnp.cumsum(lengths).astype(jnp.int32)
    finished = doc_ends[None, :] <= positions[:, None]
    doc_ids = lax.optimization_barrier(jnp.sum(finished.astype(jnp.int32), axis=1)).astype(jnp.int32)
    doc_first = lax.optimization_barrier(jnp.sum(jnp.where(finished, lengths[None, :], 0), axis=1)).astype(jnp.int32)
    return (doc_ids, (positions - doc_first).astype(jnp.int32))

def rounded_values(values):
    return lax.optimization_barrier(values.astype(jnp.bfloat16))

def reference(tokens_in, doc_lengths, attn_gain, w_query, key_weight, value_weight, w_output, query_norm_gain, key_norm_gain, mlp_gain, w_gate, w_up, w_down, out_grad):
    score_scale = HEAD_SIZE ** (-0.5)
    q_block = min(512, REPLICA_TOKENS)
    window = min(LENGTH + q_block, REPLICA_TOKENS)
    block_count = REPLICA_TOKENS // q_block
    head_grouping = QUERY_HEADS // KEY_VALUE_HEADS
    block_ids = jnp.arange(block_count, dtype=jnp.int32)

    def group_pass(totals, inputs):
        x_rows, lengths, grad_rows = inputs
        positions = jnp.arange(REPLICA_TOKENS, dtype=jnp.int32)
        doc_ids, offsets = doc_info(lengths, positions)
        cosine_table, sine_values = rope_tables(offsets, HEAD_SIZE)
        x_float = x_rows.astype(jnp.float32)
        norm_one = rms_scale(x_float)
        x_hat = x_float * norm_one
        normalized_input = (x_hat * attn_gain).astype(jnp.bfloat16)
        queries = jnp.dot(normalized_input, w_query, preferred_element_type=jnp.float32).reshape(REPLICA_TOKENS, QUERY_HEADS, HEAD_SIZE)
        key_head_rows = jnp.dot(normalized_input, key_weight, preferred_element_type=jnp.float32).reshape(REPLICA_TOKENS, KEY_VALUE_HEADS, HEAD_SIZE)
        value_head_rows = rounded_values(jnp.dot(normalized_input, value_weight, preferred_element_type=jnp.float32)).astype(jnp.float32).reshape(REPLICA_TOKENS, KEY_VALUE_HEADS, HEAD_SIZE)
        query_norm = rms_scale(queries)
        query_normalized = queries * query_norm
        query_rotated = rounded_values(rotate_pairs(query_normalized * query_norm_gain, cosine_table, sine_values)).astype(jnp.float32).reshape(REPLICA_TOKENS, KEY_VALUE_HEADS, head_grouping, HEAD_SIZE)
        key_head_norm = rms_scale(key_head_rows)
        key_normalized = key_head_rows * key_head_norm
        key_rot = rounded_values(rotate_pairs(key_normalized * key_norm_gain, cosine_table, sine_values)).astype(jnp.float32)

        def block_parts(block_id):
            query_first = (block_id * q_block).astype(jnp.int32)
            key_first = jnp.clip(query_first + q_block - window, 0, REPLICA_TOKENS - window).astype(jnp.int32)
            query_docs = lax.dynamic_slice_in_dim(doc_ids, query_first, q_block)
            key_docs = lax.dynamic_slice_in_dim(doc_ids, key_first, window)
            query_index = query_first + jnp.arange(q_block, dtype=jnp.int32)
            key_index = key_first + jnp.arange(window, dtype=jnp.int32)
            allowed = (query_docs[:, None] == key_docs[None, :]) & (key_index[None, :] <= query_index[:, None])
            query_part = lax.dynamic_slice_in_dim(query_rotated, query_first, q_block, 0)
            key_part = lax.dynamic_slice_in_dim(key_rot, key_first, window, 0)
            value_part = lax.dynamic_slice_in_dim(value_head_rows, key_first, window, 0)
            scores = jnp.einsum('tgjd,rgd->gjtr', query_part, key_part) * score_scale
            scores = jnp.where(allowed, scores, very_low)
            return (query_first, key_first, allowed, query_part, key_part, value_part, scores)

        def attend(block_id):
            query_first, key_first, allowed, query_part, key_part, value_part, scores = block_parts(block_id)
            row_high = lax.optimization_barrier(jnp.max(scores, axis=-1, keepdims=True))
            row_total = lax.optimization_barrier(jnp.sum(jnp.where(allowed, jnp.exp(scores - row_high), 0.0), axis=-1, keepdims=True))
            log_total = row_high + jnp.log(row_total)
            attn_prob = rounded_values(jnp.where(allowed, jnp.exp(scores - log_total), 0.0)).astype(jnp.float32)
            mixed_rows = jnp.einsum('gjtr,rgd->tgjd', attn_prob, value_part)
            return (rounded_values(mixed_rows.reshape(q_block, QUERY_HEADS * HEAD_SIZE)), log_total[..., 0])
        head_mixture, log_totals = lax.map(attend, block_ids)
        head_mixture = head_mixture.reshape(REPLICA_TOKENS, QUERY_HEADS * HEAD_SIZE)
        attn_part = jnp.dot(head_mixture, w_output.T, preferred_element_type=jnp.float32)
        residual = x_float + attn_part
        norm_two = rms_scale(residual)
        resid_hat = residual * norm_two
        normed_mid = (resid_hat * mlp_gain).astype(jnp.bfloat16)
        gate_part = jnp.dot(normed_mid, w_gate.T, preferred_element_type=jnp.float32)
        up_part = jnp.dot(normed_mid, w_up.T, preferred_element_type=jnp.float32)
        gate_sig = jax.nn.sigmoid(gate_part)
        hidden_rows = (gate_part * gate_sig * up_part).astype(jnp.bfloat16)
        act_out = residual + jnp.dot(hidden_rows, w_down, preferred_element_type=jnp.float32)
        grad_float = grad_rows.astype(jnp.float32)
        grad_hidden = jnp.dot(grad_rows, w_down.T, preferred_element_type=jnp.float32)
        gate_grad = (grad_hidden * up_part * gate_sig * (1.0 + gate_part * (1.0 - gate_sig))).astype(jnp.bfloat16)
        up_grad = (grad_hidden * gate_part * gate_sig).astype(jnp.bfloat16)
        grad_mid = jnp.dot(gate_grad, w_gate, preferred_element_type=jnp.float32) + jnp.dot(up_grad, w_up, preferred_element_type=jnp.float32)
        grad_resid = grad_float + root_mean_backward(resid_hat, norm_two, mlp_gain, grad_mid)
        grad_resid_b = grad_resid.astype(jnp.bfloat16)
        mixing_gradient = rounded_values(jnp.dot(grad_resid_b, w_output, preferred_element_type=jnp.float32))
        mixture_float = mixing_gradient.astype(jnp.float32).reshape(REPLICA_TOKENS, KEY_VALUE_HEADS, head_grouping, HEAD_SIZE)
        delta_row_values = lax.optimization_barrier(jnp.sum(mixture_float * head_mixture.astype(jnp.float32).reshape(REPLICA_TOKENS, KEY_VALUE_HEADS, head_grouping, HEAD_SIZE), axis=-1)).transpose(1, 2, 0)

        def attend_back(grads, block_id):
            key_sums, value_totals = grads
            query_first, key_first, allowed, query_part, key_part, value_part, scores = block_parts(block_id)
            log_total = log_totals[block_id]
            mix_part = lax.dynamic_slice_in_dim(mixture_float, query_first, q_block, 0)
            delta_part = lax.dynamic_slice_in_dim(delta_row_values, query_first, q_block, 2)
            attn_prob = jnp.where(allowed, jnp.exp(scores - log_total[..., None]), 0.0)
            grad_prob = jnp.einsum('tgjd,rgd->gjtr', mix_part, value_part)
            grad_score = rounded_values(attn_prob * (grad_prob - delta_part[..., None])).astype(jnp.float32)
            query_grad = score_scale * jnp.einsum('gjtr,rgd->tgjd', grad_score, key_part)
            key_grad = score_scale * jnp.einsum('gjtr,tgjd->rgd', grad_score, query_part)
            value_grad = jnp.einsum('gjtr,tgjd->rgd', rounded_values(attn_prob).astype(jnp.float32), mix_part)
            key_sums = lax.dynamic_update_slice_in_dim(key_sums, lax.dynamic_slice_in_dim(key_sums, key_first, window, 0) + key_grad, key_first, 0)
            value_totals = lax.dynamic_update_slice_in_dim(value_totals, lax.dynamic_slice_in_dim(value_totals, key_first, window, 0) + value_grad, key_first, 0)
            return ((key_sums, value_totals), query_grad)
        zeroed_keys = jnp.zeros((REPLICA_TOKENS, KEY_VALUE_HEADS, HEAD_SIZE), jnp.float32)
        (key_sums, value_totals), query_grads = lax.scan(attend_back, (zeroed_keys, zeroed_keys), block_ids)
        query_unrot = rotate_back(query_grads.reshape(REPLICA_TOKENS, QUERY_HEADS, HEAD_SIZE), cosine_table, sine_values)
        key_unrotated = rotate_back(key_sums, cosine_table, sine_values)
        query_gain_part = lax.optimization_barrier(jnp.sum(query_unrot * query_normalized, axis=(0, 1)))
        key_gain_part = lax.optimization_barrier(jnp.sum(key_unrotated * key_normalized, axis=(0, 1)))
        grad_query_rows = root_mean_backward(query_normalized, query_norm, query_norm_gain, query_unrot).reshape(REPLICA_TOKENS, QUERY_HEADS * HEAD_SIZE).astype(jnp.bfloat16)
        key_row_gradient = root_mean_backward(key_normalized, key_head_norm, key_norm_gain, key_unrotated).reshape(REPLICA_TOKENS, KEY_VALUE_HEADS * HEAD_SIZE).astype(jnp.bfloat16)
        value_row_gradient = value_totals.reshape(REPLICA_TOKENS, KEY_VALUE_HEADS * HEAD_SIZE).astype(jnp.bfloat16)
        grad_in_norm = jnp.dot(grad_query_rows, w_query.T, preferred_element_type=jnp.float32) + jnp.dot(key_row_gradient, key_weight.T, preferred_element_type=jnp.float32) + jnp.dot(value_row_gradient, value_weight.T, preferred_element_type=jnp.float32)
        in_grad = grad_resid + root_mean_backward(x_hat, norm_one, attn_gain, grad_in_norm)
        new_totals = (totals[0] + lax.optimization_barrier(jnp.sum(grad_in_norm * x_hat, axis=0)), totals[1] + jnp.dot(normalized_input.T, grad_query_rows, preferred_element_type=jnp.float32), totals[2] + jnp.dot(normalized_input.T, key_row_gradient, preferred_element_type=jnp.float32), totals[3] + jnp.dot(normalized_input.T, value_row_gradient, preferred_element_type=jnp.float32), totals[4] + jnp.dot(grad_resid_b.T, head_mixture, preferred_element_type=jnp.float32), totals[5] + query_gain_part, totals[6] + key_gain_part, totals[7] + lax.optimization_barrier(jnp.sum(grad_mid * resid_hat, axis=0)), totals[8] + jnp.dot(gate_grad.T, normed_mid, preferred_element_type=jnp.float32), totals[9] + jnp.dot(up_grad.T, normed_mid, preferred_element_type=jnp.float32), totals[10] + jnp.dot(hidden_rows.T, grad_rows, preferred_element_type=jnp.float32))
        return (new_totals, (act_out, in_grad))
    initial_state = (jnp.zeros((MODEL_DIMENSION,), jnp.float32), jnp.zeros((MODEL_DIMENSION, QUERY_HEADS * HEAD_SIZE), jnp.float32), jnp.zeros((MODEL_DIMENSION, KEY_VALUE_HEADS * HEAD_SIZE), jnp.float32), jnp.zeros((MODEL_DIMENSION, KEY_VALUE_HEADS * HEAD_SIZE), jnp.float32), jnp.zeros((MODEL_DIMENSION, QUERY_HEADS * HEAD_SIZE), jnp.float32), jnp.zeros((HEAD_SIZE,), jnp.float32), jnp.zeros((HEAD_SIZE,), jnp.float32), jnp.zeros((MODEL_DIMENSION,), jnp.float32), jnp.zeros((FEEDFORWARD_SIZE, MODEL_DIMENSION), jnp.float32), jnp.zeros((FEEDFORWARD_SIZE, MODEL_DIMENSION), jnp.float32), jnp.zeros((FEEDFORWARD_SIZE, MODEL_DIMENSION), jnp.float32))
    totals, (act_rows, grad_in_rows) = lax.scan(group_pass, initial_state, (tokens_in.reshape(N_REP, REPLICA_TOKENS, MODEL_DIMENSION), doc_lengths, out_grad.reshape(N_REP, REPLICA_TOKENS, MODEL_DIMENSION)))
    return (act_rows.reshape(TOKENS, MODEL_DIMENSION), grad_in_rows.reshape(TOKENS, MODEL_DIMENSION), totals[0], totals[1], totals[2], totals[3], totals[4], totals[5], totals[6], totals[7], totals[8], totals[9], totals[10])
```

```python
import jax
import jax.numpy as jnp
from jax import lax
from jax.experimental import pallas as pl
from jax.experimental.pallas import tpu as pltpu
from jax.sharding import PartitionSpec as P

norm_eps = 1e-05
rope_base = 1000000.0
very_low = -1e30
contract_last = (((1,), (1,)), ((), ()))
contract_first = (((0,), (0,)), ((), ()))


def rms_scale(values):
    return lax.rsqrt(jnp.mean(values * values, axis=-1, keepdims=True) + norm_eps)


def root_mean_backward(normed, factor, gain, upstream):
    scaled = upstream * gain
    return factor * (scaled - normed * jnp.mean(scaled * normed, axis=-1, keepdims=True))


def rope_tables(positions, head_dim):
    half_dim = head_dim // 2
    inverse_freq = rope_base ** (-(jnp.arange(half_dim, dtype=jnp.float32) * 2.0 / head_dim))
    angles = positions.astype(jnp.float32)[:, None] * inverse_freq[None, :]
    return (jnp.cos(angles)[:, None, :], jnp.sin(angles)[:, None, :])


def rotate_pairs(values, cosine_table, sine_values):
    half_dim = values.shape[-1] // 2
    lower_half = values[..., :half_dim]
    upper_half = values[..., half_dim:]
    return jnp.concatenate(
        [
            lower_half * cosine_table - upper_half * sine_values,
            upper_half * cosine_table + lower_half * sine_values,
        ],
        axis=-1,
    )


def rotate_back(grads, cosine_table, sine_values):
    half_dim = grads.shape[-1] // 2
    lower_half = grads[..., :half_dim]
    upper_half = grads[..., half_dim:]
    return jnp.concatenate(
        [
            lower_half * cosine_table + upper_half * sine_values,
            upper_half * cosine_table - lower_half * sine_values,
        ],
        axis=-1,
    )


def doc_info(lengths, positions):
    doc_ends = jnp.cumsum(lengths)
    finished = doc_ends[None, :] <= positions[:, None]
    doc_ids = jnp.sum(finished.astype(jnp.int32), axis=1)
    doc_first = jnp.sum(jnp.where(finished, lengths[None, :], 0), axis=1)
    return (doc_ids, positions - doc_first)


def local(
    tokens_in,
    doc_lengths,
    attn_gain,
    w_query,
    key_weight,
    value_weight,
    w_output,
    query_norm_gain,
    key_norm_gain,
    mlp_gain,
    w_gate,
    w_up,
    w_down,
    out_grad,
):
    row_count = tokens_in.shape[0]
    model_width = tokens_in.shape[1]
    head_dim = query_norm_gain.shape[0]
    query_width = w_query.shape[1]
    kv_width = key_weight.shape[1]
    kv_heads = kv_width // head_dim
    head_grouping = query_width // kv_width
    score_scale = head_dim ** (-0.5)
    rank_count = lax.axis_size("shard") * lax.axis_size("seq")
    group_rows = row_count * rank_count
    first_row = lax.axis_index(("shard", "seq")) * row_count
    key_block = min(512, group_rows)
    block_count = group_rows // key_block
    key_index = jnp.arange(group_rows, dtype=jnp.int32)
    key_docs, key_offset = doc_info(doc_lengths[0], key_index)
    query_index = first_row + jnp.arange(row_count, dtype=jnp.int32)
    query_docs = lax.dynamic_slice_in_dim(key_docs, first_row, row_count)
    query_offset = lax.dynamic_slice_in_dim(key_offset, first_row, row_count)
    cosine_table, sine_values = rope_tables(query_offset, head_dim)
    x_float = tokens_in.astype(jnp.float32)
    norm_one = rms_scale(x_float)
    x_hat = x_float * norm_one
    normalized_input = (x_hat * attn_gain).astype(jnp.bfloat16)
    pieces = (
        lax.all_gather(w_query, "shard", axis=0, tiled=True),
        lax.all_gather(key_weight, "shard", axis=0, tiled=True),
        lax.all_gather(value_weight, "shard", axis=0, tiled=True),
    )
    in_cols = normalized_input
    queries, key_proj, value_proj = tuple(
        (jnp.dot(in_cols, weight, preferred_element_type=jnp.float32) for weight in pieces)
    )
    query_heads = queries.reshape(row_count, query_width // head_dim, head_dim)
    query_norm = rms_scale(query_heads)
    query_normalized = query_heads * query_norm
    query_rotated = rotate_pairs(
        query_normalized * query_norm_gain, cosine_table, sine_values
    ).astype(jnp.bfloat16)
    key_head_rows = key_proj.reshape(row_count, kv_heads, head_dim)
    key_head_norm = rms_scale(key_head_rows)
    key_normalized = key_head_rows * key_head_norm
    key_rot = rotate_pairs(key_normalized * key_norm_gain, cosine_table, sine_values).astype(
        jnp.bfloat16
    )
    value_rows = value_proj.astype(jnp.bfloat16)
    key_all, value_all = (
        lax.all_gather(key_rot.reshape(row_count, kv_width), ("shard", "seq"), axis=0, tiled=True),
        lax.all_gather(value_rows, ("shard", "seq"), axis=0, tiled=True),
    )
    query_grouped = query_rotated.reshape(row_count, kv_heads, head_grouping, head_dim)

    def block_mask(offset, span_rows):
        docs_here = lax.dynamic_slice_in_dim(key_docs, offset, span_rows)
        index_here = offset + jnp.arange(span_rows, dtype=jnp.int32)
        return (query_docs[:, None] == docs_here[None, :]) & (
            index_here[None, :] <= query_index[:, None]
        )

    def block_scores(offset, span_rows, allowed):
        key_rows = lax.dynamic_slice_in_dim(key_all, offset, span_rows, 0).reshape(
            span_rows, kv_heads, head_dim
        )
        value_block = lax.dynamic_slice_in_dim(value_all, offset, span_rows, 0).reshape(
            span_rows, kv_heads, head_dim
        )
        scores = (
            jnp.einsum(
                "tgjd,rgd->gjtr", query_grouped, key_rows, preferred_element_type=jnp.float32
            )
            * score_scale
        )
        return (jnp.where(allowed, scores, very_low), key_rows, value_block)

    def total_block(block_index, running):
        offset = block_index * key_block
        allowed = block_mask(offset, key_block)

        def total_accumulate(softmax_state):
            row_high, row_total = softmax_state
            scores, key_rows, value_block = block_scores(offset, key_block, allowed)
            new_high = jnp.maximum(row_high, jnp.max(scores, axis=-1))
            exp_scores = jnp.where(allowed, jnp.exp(scores - new_high[..., None]), 0.0)
            row_total = row_total * jnp.exp(row_high - new_high) + jnp.sum(exp_scores, axis=-1)
            return (new_high, row_total)

        return lax.cond(
            jnp.any(allowed), total_accumulate, lambda softmax_state: softmax_state, running
        )

    softmax_init = (
        jnp.full((kv_heads, head_grouping, row_count), very_low, jnp.float32),
        jnp.zeros((kv_heads, head_grouping, row_count), jnp.float32),
    )
    row_high, row_total = lax.fori_loop(0, block_count, total_block, softmax_init)
    log_total = row_high + jnp.log(row_total)

    def mix_block(block_index, weighted):
        offset = block_index * key_block
        allowed = block_mask(offset, key_block)

        def mix_accumulate(current):
            scores, key_rows, value_block = block_scores(offset, key_block, allowed)
            attn_prob = jnp.where(allowed, jnp.exp(scores - log_total[..., None]), 0.0).astype(
                jnp.bfloat16
            )
            return current + jnp.einsum(
                "gjtr,rgd->gjtd", attn_prob, value_block, preferred_element_type=jnp.float32
            )

        return lax.cond(jnp.any(allowed), mix_accumulate, lambda current: current, weighted)

    weighted = lax.fori_loop(
        0,
        block_count,
        mix_block,
        jnp.zeros((kv_heads, head_grouping, row_count, head_dim), jnp.float32),
    )
    head_mixture = (
        weighted.transpose(2, 0, 1, 3).reshape(row_count, query_width).astype(jnp.bfloat16)
    )
    attn_part = lax.dot_general(
        head_mixture,
        lax.all_gather(w_output, "shard", axis=0, tiled=True),
        contract_last,
        preferred_element_type=jnp.float32,
    )
    residual = x_float + attn_part
    norm_two = rms_scale(residual)
    resid_hat = residual * norm_two
    normed_mid = (resid_hat * mlp_gain).astype(jnp.bfloat16)
    gate_rows = lax.all_gather(w_gate, "shard", axis=0, tiled=True)
    up_rows = lax.all_gather(w_up, "shard", axis=0, tiled=True)
    down_rows = lax.all_gather(w_down, "shard", axis=0, tiled=True)
    gate_part = lax.dot_general(
        normed_mid, gate_rows, contract_last, preferred_element_type=jnp.float32
    )
    up_part = lax.dot_general(
        normed_mid, up_rows, contract_last, preferred_element_type=jnp.float32
    )
    hidden_part = (gate_part * jax.nn.sigmoid(gate_part) * up_part).astype(jnp.bfloat16)
    mlp_sum = jnp.dot(hidden_part, down_rows, preferred_element_type=jnp.float32)
    mlp_gate_store = gate_part
    mlp_up_store = up_part
    hidden_store = hidden_part
    mlp_sum, gate_store, up_store, hidden_store = (
        mlp_sum,
        mlp_gate_store,
        mlp_up_store,
        hidden_store,
    )
    act_out = residual + mlp_sum
    grad_float = out_grad.astype(jnp.float32)
    gate_rows = lax.all_gather(w_gate, "shard", axis=0, tiled=True)
    up_rows = lax.all_gather(w_up, "shard", axis=0, tiled=True)
    down_rows = lax.all_gather(w_down, "shard", axis=0, tiled=True)
    span_rows = gate_rows.shape[0]
    gate_part = gate_store
    up_part = up_store
    grad_hidden = lax.dot_general(
        out_grad, down_rows, contract_last, preferred_element_type=jnp.float32
    )
    gate_sig = jax.nn.sigmoid(gate_part)
    gate_grad = (grad_hidden * up_part * gate_sig * (1.0 + gate_part * (1.0 - gate_sig))).astype(
        jnp.bfloat16
    )
    up_grad = (grad_hidden * gate_part * gate_sig).astype(jnp.bfloat16)
    grad_mid = jnp.dot(gate_grad, gate_rows, preferred_element_type=jnp.float32) + jnp.dot(
        up_grad, up_rows, preferred_element_type=jnp.float32
    )
    gate_grad_store = gate_grad
    up_grad_store = up_grad
    grad_mid, gate_grad_store, up_grad_store = (grad_mid, gate_grad_store, up_grad_store)
    grad_resid = grad_float + root_mean_backward(resid_hat, norm_two, mlp_gain, grad_mid)
    mlp_gain_part = jnp.sum(grad_mid * resid_hat, axis=0)
    grad_resid_b = grad_resid.astype(jnp.bfloat16)
    resid_cols = grad_resid_b
    mixing_gradient = jnp.dot(
        resid_cols,
        lax.all_gather(w_output, "shard", axis=0, tiled=True),
        preferred_element_type=jnp.float32,
    ).astype(jnp.bfloat16)
    mix_grouped = mixing_gradient.reshape(row_count, kv_heads, head_grouping, head_dim)
    delta_row_values = jnp.sum(
        (mixing_gradient.astype(jnp.float32) * head_mixture.astype(jnp.float32)).reshape(
            row_count, kv_heads, head_grouping, head_dim
        ),
        axis=-1,
    ).transpose(1, 2, 0)

    def score_grads(offset, span_rows, allowed):
        scores, key_rows, value_block = block_scores(offset, span_rows, allowed)
        attn_prob = jnp.where(allowed, jnp.exp(scores - log_total[..., None]), 0.0)
        grad_prob = jnp.einsum(
            "tgjd,rgd->gjtr", mix_grouped, value_block, preferred_element_type=jnp.float32
        )
        grad_score = (attn_prob * (grad_prob - delta_row_values[..., None])).astype(jnp.bfloat16)
        return (attn_prob, grad_score, key_rows)

    def query_pass(block_index, grad_sum):
        offset = block_index * key_block
        allowed = block_mask(offset, key_block)

        def query_accumulate(current):
            attn_prob, grad_score, key_rows = score_grads(offset, key_block, allowed)
            return current + score_scale * jnp.einsum(
                "gjtr,rgd->tgjd", grad_score, key_rows, preferred_element_type=jnp.float32
            )

        return lax.cond(jnp.any(allowed), query_accumulate, lambda current: current, grad_sum)

    query_rot_grad = lax.fori_loop(
        0,
        block_count,
        query_pass,
        jnp.zeros((row_count, kv_heads, head_grouping, head_dim), jnp.float32),
    )

    def one_block(start_row):
        allowed = block_mask(start_row, key_block)

        def compute(unused):
            attn_prob, grad_score, key_rows = score_grads(start_row, key_block, allowed)
            key_grad = score_scale * jnp.einsum(
                "gjtr,tgjd->rgd", grad_score, query_grouped, preferred_element_type=jnp.float32
            )
            value_grad = jnp.einsum(
                "gjtr,tgjd->rgd",
                attn_prob.astype(jnp.bfloat16),
                mix_grouped,
                preferred_element_type=jnp.float32,
            )
            return jnp.concatenate(
                [key_grad.reshape(key_block, kv_width), value_grad.reshape(key_block, kv_width)],
                axis=1,
            )

        return lax.cond(
            jnp.any(allowed),
            compute,
            lambda unused: jnp.zeros((key_block, 2 * kv_width), jnp.float32),
            0,
        )

    starts = key_block * jnp.arange(
        row_count * lax.axis_size(("shard", "seq")) // key_block, dtype=jnp.int32
    )
    kv_summed = lax.psum_scatter(
        lax.map(one_block, starts).reshape(
            row_count * lax.axis_size(("shard", "seq")), 2 * kv_width
        ),
        ("shard", "seq"),
        scatter_dimension=0,
        tiled=True,
    )
    key_rot_grad = kv_summed[:, :kv_width].reshape(row_count, kv_heads, head_dim)
    value_grad_b = kv_summed[:, kv_width:].astype(jnp.bfloat16)
    key_unrotated = rotate_back(key_rot_grad, cosine_table, sine_values)
    key_gain_part = jnp.sum(key_unrotated * key_normalized, axis=(0, 1))
    key_row_gradient = (
        root_mean_backward(key_normalized, key_head_norm, key_norm_gain, key_unrotated)
        .reshape(row_count, kv_width)
        .astype(jnp.bfloat16)
    )
    query_unrot = rotate_back(
        query_rot_grad.reshape(row_count, query_width // head_dim, head_dim),
        cosine_table,
        sine_values,
    )
    query_gain_part = jnp.sum(query_unrot * query_normalized, axis=(0, 1))
    grad_query_rows = (
        root_mean_backward(query_normalized, query_norm, query_norm_gain, query_unrot)
        .reshape(row_count, query_width)
        .astype(jnp.bfloat16)
    )
    query_rows, key_rows, value_rows_w = lax.all_gather(
        (w_query, key_weight, value_weight), "shard", axis=0, tiled=True
    )
    grad_in_norm = (
        lax.dot_general(
            grad_query_rows, query_rows, contract_last, preferred_element_type=jnp.float32
        )
        + lax.dot_general(
            key_row_gradient, key_rows, contract_last, preferred_element_type=jnp.float32
        )
        + lax.dot_general(
            value_grad_b, value_rows_w, contract_last, preferred_element_type=jnp.float32
        )
    )
    in_grad = grad_resid + root_mean_backward(x_hat, norm_one, attn_gain, grad_in_norm)
    attn_gain_part = jnp.sum(grad_in_norm * x_hat, axis=0)
    grad_attn_gain, grad_mlp_gain, grad_query_gain, grad_key_gain = lax.psum(
        (attn_gain_part, mlp_gain_part, query_gain_part, key_gain_part), ("rep", "shard", "seq")
    )
    attn_grads = jnp.concatenate([grad_query_rows, key_row_gradient, value_grad_b], axis=1)
    d_share = model_width // rank_count
    in_own, resid_own, gate_own, up_own, hidden_own = (
        lax.all_to_all(normalized_input, ("shard", "seq"), split_axis=1, concat_axis=0, tiled=True),
        lax.all_to_all(grad_resid_b, ("shard", "seq"), split_axis=1, concat_axis=0, tiled=True),
        lax.all_to_all(gate_grad_store, ("shard", "seq"), split_axis=1, concat_axis=0, tiled=True),
        lax.all_to_all(up_grad_store, ("shard", "seq"), split_axis=1, concat_axis=0, tiled=True),
        lax.all_to_all(hidden_store, ("shard", "seq"), split_axis=1, concat_axis=0, tiled=True),
    )
    attn_piece = lax.all_gather(attn_grads, ("shard", "seq"), axis=0, tiled=True)
    mix_piece = lax.all_gather(head_mixture, ("shard", "seq"), axis=0, tiled=True)
    mid_piece = lax.all_gather(normed_mid, ("shard", "seq"), axis=0, tiled=True)
    grad_piece = lax.all_gather(out_grad, ("shard", "seq"), axis=0, tiled=True)
    span_rows = attn_piece.shape[0]
    in_cols = in_own
    resid_cols = resid_own
    attn_rows = jnp.concatenate(
        [
            lax.dot_general(
                in_cols, attn_piece, contract_first, preferred_element_type=jnp.float32
            ),
            lax.dot_general(
                resid_cols, mix_piece, contract_first, preferred_element_type=jnp.float32
            ),
        ],
        axis=1,
    )
    mlp_rows = jnp.concatenate(
        [
            lax.dot_general(
                gate_own, mid_piece, contract_first, preferred_element_type=jnp.float32
            ),
            lax.dot_general(up_own, mid_piece, contract_first, preferred_element_type=jnp.float32),
            lax.dot_general(
                hidden_own, grad_piece, contract_first, preferred_element_type=jnp.float32
            ),
        ],
        axis=1,
    )
    group_grads = jnp.concatenate([attn_rows, mlp_rows], axis=0)
    own_grads = lax.psum(group_grads, "rep")
    attn_block_grads = own_grads[:d_share]
    mlp_block_grads = own_grads[d_share:]
    grad_query = attn_block_grads[:, :query_width]
    grad_key = attn_block_grads[:, query_width : query_width + kv_width]
    grad_value = attn_block_grads[:, query_width + kv_width : query_width + 2 * kv_width]
    grad_output = attn_block_grads[:, query_width + 2 * kv_width :]
    grad_gate = mlp_block_grads[:, :model_width]
    grad_up = mlp_block_grads[:, model_width : 2 * model_width]
    grad_down = mlp_block_grads[:, 2 * model_width :]
    return (
        act_out,
        in_grad,
        grad_attn_gain,
        grad_query,
        grad_key,
        grad_value,
        grad_output,
        grad_query_gain,
        grad_key_gain,
        grad_mlp_gain,
        grad_gate,
        grad_up,
        grad_down,
    )


group_axes = ("shard", "seq")


def group_swap(values, mask):
    return lax.ppermute(values, group_axes, [(rank, rank ^ mask) for rank in range(8)])


def rep_swap(values, mask):
    return lax.ppermute(values, "rep", [(rank, rank ^ mask) for rank in range(4)])


def rep_shift(values, step):
    pairs = [(rank, rank + step) for rank in range(4) if 0 <= rank + step < 4]
    return lax.ppermute(values, "rep", pairs)


def gather_pieces(own):
    same_core = [own] + [group_swap(own, mask) for mask in (2, 4, 6)]
    other_core = [group_swap(piece, 1) for piece in same_core]
    return [piece for pair in zip(same_core, other_core) for piece in pair]


def place_pieces(pieces, rank, axis):
    shape = list(pieces[0].shape)
    width = shape[axis]
    shape[axis] = width * len(pieces)
    whole = jnp.zeros(shape, pieces[0].dtype)
    for mask, piece in enumerate(pieces):
        whole = lax.dynamic_update_slice_in_dim(whole, piece, (rank ^ mask) * width, axis)
    return whole


def add_rounded(left, right):
    return (left.astype(jnp.float32) + right.astype(jnp.float32)).astype(jnp.bfloat16)


def scatter_sum(partial, rank, axis=0):
    width = partial.shape[axis] // 8

    def block(mask):
        return lax.dynamic_slice_in_dim(partial, (rank ^ mask) * width, width, axis)

    halves = [
        add_rounded(block(mask), group_swap(block(mask ^ 1).astype(jnp.bfloat16), 1))
        for mask in (0, 2, 4, 6)
    ]
    moved = [group_swap(half, mask) for mask, half in zip((2, 4, 6), halves[1:])]
    total = halves[0].astype(jnp.float32)
    for piece in moved:
        total = total + piece.astype(jnp.float32)
    return total


def rep_chain_sum(values, chunk_count):
    place = lax.axis_index("rep")
    rows = values.shape[0] // chunk_count
    chunks = values.reshape(chunk_count, rows, values.shape[1])

    def own(index):
        return lax.dynamic_index_in_dim(
            chunks, jnp.clip(index, 0, chunk_count - 1), 0, keepdims=False
        )

    last = 3
    from_left = []
    from_right = []
    for tick in range(chunk_count + 2):
        up = own(tick - place)
        down = own(tick - (last - place))
        if tick:
            up = add_rounded(up, from_left[-1])
            down = add_rounded(down, from_right[-1])
        from_left.append(rep_shift(up, 1))
        from_right.append(rep_shift(down, -1))
    left = jnp.stack(from_left)
    right = jnp.stack(from_right)
    left = lax.dynamic_slice_in_dim(left, jnp.maximum(place - 1, 0), chunk_count)
    right = lax.dynamic_slice_in_dim(right, jnp.maximum(last - place - 1, 0), chunk_count)
    total = (
        chunks.astype(jnp.float32) + left.astype(jnp.float32) + right.astype(jnp.float32)
    )
    return total.reshape(values.shape)


def rep_halving_sum(values):
    place = lax.axis_index("rep")
    low = place % 2
    high = place // 2
    half = values.shape[0] // 2
    quarter = half // 2
    kept = lax.dynamic_slice_in_dim(values, low * half, half)
    sent = lax.dynamic_slice_in_dim(values, (1 - low) * half, half)
    part = add_rounded(kept, rep_swap(sent, 1))
    kept = lax.dynamic_slice_in_dim(part, high * quarter, quarter)
    sent = lax.dynamic_slice_in_dim(part, (1 - high) * quarter, quarter)
    part = add_rounded(kept, rep_swap(sent, 2))
    other = rep_swap(part, 2)
    part = jnp.where(
        high == 0, jnp.concatenate([part, other]), jnp.concatenate([other, part])
    )
    other = rep_swap(part, 1)
    return jnp.where(low == 0, jnp.concatenate([part, other]), jnp.concatenate([other, part]))


def sum_everywhere(values):
    for mask in (1, 2, 4):
        values = values + group_swap(values, mask)
    for mask in (1, 2):
        values = values + rep_swap(values, mask)
    return values


def lower_lanes(shape, width):
    return lax.broadcasted_iota(jnp.int32, shape, 1) % (2 * width) < width


def pair_scale(values, head_dim):
    lower = lower_lanes(values.shape, head_dim)
    low = jnp.sum(jnp.where(lower, values, 0.0), axis=1, keepdims=True)
    high = jnp.sum(jnp.where(lower, 0.0, values), axis=1, keepdims=True)
    return jnp.where(lower, low, high) * (1.0 / head_dim)


def swap_halves(values, head_dim):
    width = values.shape[1]
    half = head_dim // 2
    return jnp.where(
        lower_lanes(values.shape, half),
        pltpu.roll(values, width - half, 1),
        pltpu.roll(values, half, 1),
    )


def rotated_heads(raw, query_gain, key_gain, cosine, sine, head_dim):
    width = 2 * head_dim
    queries = raw[:, :width]
    keys = raw[:, width:]
    query_norm = lax.rsqrt(pair_scale(queries * queries, head_dim) + norm_eps)
    key_norm = lax.rsqrt(pair_scale(keys * keys, head_dim) + norm_eps)
    query_hat = queries * query_norm
    key_hat = keys * key_norm
    scaled = query_hat * query_gain
    query_rot = scaled * cosine + swap_halves(scaled, head_dim) * sine
    scaled = key_hat * key_gain
    key_rot = scaled * cosine + swap_halves(scaled, head_dim) * sine
    lower = lower_lanes(keys.shape, head_dim)
    key_twice = jnp.where(lower, key_rot, pltpu.roll(key_rot, head_dim, 1))
    value_twice = jnp.where(lower, pltpu.roll(keys, head_dim, 1), keys)
    return query_hat, query_norm, key_hat, key_norm, query_rot, key_twice, value_twice


def stack_heads(values, head_dim):
    lower = lower_lanes(values.shape, head_dim)
    zero = jnp.zeros_like(values)
    return jnp.concatenate(
        [jnp.where(lower, values, zero), jnp.where(lower, zero, values)], axis=0
    )


def join_heads(stacked, head_dim):
    rows = stacked.shape[0] // 2
    lower = lower_lanes((rows, stacked.shape[1]), head_dim)
    return jnp.where(lower, stacked[:rows], stacked[rows:])


def allowed_pairs(doc_column, doc_row, first, rows, span):
    row_index = first + lax.broadcasted_iota(jnp.int32, (rows, span), 0)
    key_index = lax.broadcasted_iota(jnp.int32, (rows, span), 1)
    return (doc_column == doc_row) & (key_index <= row_index)


def dot_last(left, right):
    return lax.dot_general(left, right, contract_last, preferred_element_type=jnp.float32)


def dot_first(left, right):
    return lax.dot_general(left, right, contract_first, preferred_element_type=jnp.float32)


def dot_plain(left, right):
    return jnp.dot(left, right, preferred_element_type=jnp.float32)


def attention_forward(head_dim, block):
    score_scale = head_dim ** (-0.5)
    width = 2 * head_dim

    def kernel(
        x_ref, gain_ref, weight_ref, query_gain_ref, key_gain_ref, cos_ref, sin_ref,
        doc_col_ref, doc_row_ref, mix_ref, normed_ref, raw_ref, lse_ref,
        query_scr, key_scr, value_scr,
    ):
        total = x_ref.shape[0]
        for first in range(0, total, block):
            rows = pl.ds(first, block)
            x = x_ref[rows, :].astype(jnp.float32)
            normed = (x * rms_scale(x) * gain_ref[...]).astype(jnp.bfloat16)
            normed_ref[rows, :] = normed
            raw = dot_plain(normed, weight_ref[...])
            raw_ref[rows, :] = raw
            parts = rotated_heads(
                raw, query_gain_ref[...], key_gain_ref[...], cos_ref[rows, :], sin_ref[rows, :],
                head_dim,
            )
            query_scr[rows, :] = parts[4].astype(jnp.bfloat16)
            key_scr[rows, :] = parts[5].astype(jnp.bfloat16)
            value_scr[rows, :] = parts[6].astype(jnp.bfloat16)
        for first in range(0, total, block):
            rows = pl.ds(first, block)
            span = first + block
            stacked = stack_heads(query_scr[rows, :], head_dim)
            allowed = allowed_pairs(
                doc_col_ref[rows, :], doc_row_ref[:, :span], first, block, span
            )
            allowed = jnp.concatenate([allowed, allowed], axis=0)
            scores = dot_last(stacked, key_scr[:span, :]) * score_scale
            scores = jnp.where(allowed, scores, very_low)
            high = jnp.max(scores, axis=1, keepdims=True)
            powers = jnp.exp(scores - high)
            row_total = jnp.sum(powers, axis=1, keepdims=True)
            probs = (powers * (1.0 / row_total)).astype(jnp.bfloat16)
            mixed = dot_plain(probs, value_scr[:span, :])
            mix_ref[rows, :] = join_heads(mixed, head_dim).astype(jnp.bfloat16)
            lse_ref[pl.ds(2 * first, 2 * block), :] = high + jnp.log(row_total)

    def call(x, gain, weight, query_gain, key_gain, cosine, sine, doc_column, doc_row):
        total, model = x.shape
        return pl.pallas_call(
            kernel,
            name="attention_forward",
            out_shape=(
                jax.ShapeDtypeStruct((total, width), jnp.bfloat16),
                jax.ShapeDtypeStruct((total, model), jnp.bfloat16),
                jax.ShapeDtypeStruct((total, 2 * width), jnp.float32),
                jax.ShapeDtypeStruct((2 * total, 1), jnp.float32),
            ),
            scratch_shapes=[pltpu.VMEM((total, width), jnp.bfloat16)] * 3,
        )(x, gain, weight, query_gain, key_gain, cosine, sine, doc_column, doc_row)

    return call


def attention_backward(head_dim, block):
    score_scale = head_dim ** (-0.5)
    width = 2 * head_dim

    def kernel(
        raw_ref, mix_ref, resid_ref, out_cols_ref, lse_ref, query_gain_ref, key_gain_ref,
        cos_ref, sin_ref, doc_col_ref, doc_row_ref, grads_ref, query_part_ref, key_part_ref,
        query_scr, key_scr, value_scr, key_sum, value_sum,
    ):
        total = raw_ref.shape[0]
        query_gain = query_gain_ref[...]
        key_gain = key_gain_ref[...]

        def heads_of(rows):
            return rotated_heads(
                raw_ref[rows, :], query_gain, key_gain, cos_ref[rows, :], sin_ref[rows, :],
                head_dim,
            )

        def unrotated(grad, rows):
            return grad * cos_ref[rows, :] - swap_halves(grad, head_dim) * sin_ref[rows, :]

        def norm_back(upstream, hat, norm, gain):
            scaled = upstream * gain
            return norm * (scaled - hat * pair_scale(scaled * hat, head_dim))

        for first in range(0, total, block):
            rows = pl.ds(first, block)
            parts = heads_of(rows)
            query_scr[rows, :] = parts[4].astype(jnp.bfloat16)
            key_scr[rows, :] = parts[5].astype(jnp.bfloat16)
            value_scr[rows, :] = parts[6].astype(jnp.bfloat16)
        key_sum[...] = jnp.zeros_like(key_sum)
        value_sum[...] = jnp.zeros_like(value_sum)
        query_part = jnp.zeros((1, width), jnp.float32)
        for first in range(0, total, block):
            rows = pl.ds(first, block)
            span = first + block
            stacked = stack_heads(query_scr[rows, :], head_dim)
            mix_grad = dot_plain(resid_ref[rows, :], out_cols_ref[...]).astype(jnp.bfloat16)
            stacked_grad = stack_heads(mix_grad, head_dim)
            mixed = mix_ref[rows, :].astype(jnp.float32)
            delta = jnp.sum(
                stacked_grad.astype(jnp.float32) * jnp.concatenate([mixed, mixed], axis=0),
                axis=1,
                keepdims=True,
            )
            allowed = allowed_pairs(
                doc_col_ref[rows, :], doc_row_ref[:, :span], first, block, span
            )
            allowed = jnp.concatenate([allowed, allowed], axis=0)
            scores = dot_last(stacked, key_scr[:span, :]) * score_scale
            lse = lse_ref[pl.ds(2 * first, 2 * block), :]
            probs = jnp.exp(jnp.where(allowed, scores - lse, very_low))
            prob_grad = dot_last(stacked_grad, value_scr[:span, :])
            score_grad = (probs * (prob_grad - delta)).astype(jnp.bfloat16)
            rotated = join_heads(dot_plain(score_grad, key_scr[:span, :]), head_dim)
            key_sum[:span, :] += dot_first(score_grad, stacked)
            value_sum[:span, :] += dot_first(probs.astype(jnp.bfloat16), stacked_grad)
            query_hat, query_norm = heads_of(rows)[:2]
            straight = unrotated(rotated * score_scale, rows)
            query_part = query_part + jnp.sum(straight * query_hat, axis=0, keepdims=True)
            grads_ref[rows, :width] = norm_back(
                straight, query_hat, query_norm, query_gain
            ).astype(jnp.bfloat16)
        key_part = jnp.zeros((1, width), jnp.float32)
        for first in range(0, total, block):
            rows = pl.ds(first, block)
            key_hat, key_norm = heads_of(rows)[2:4]
            summed = key_sum[rows, :]
            summed = (summed + pltpu.roll(summed, head_dim, 1)) * score_scale
            values = value_sum[rows, :]
            values = values + pltpu.roll(values, head_dim, 1)
            straight = unrotated(summed, rows)
            key_part = key_part + jnp.sum(straight * key_hat, axis=0, keepdims=True)
            key_grad = norm_back(straight, key_hat, key_norm, key_gain)
            lower = lower_lanes(key_grad.shape, head_dim)
            grads_ref[rows, width:] = jnp.where(lower, key_grad, values).astype(jnp.bfloat16)
        query_part_ref[...] = query_part
        key_part_ref[...] = key_part

    def call(raw, mix, resid, out_cols, lse, query_gain, key_gain, cosine, sine, doc_col, doc_row):
        total = raw.shape[0]
        return pl.pallas_call(
            kernel,
            name="attention_backward",
            out_shape=(
                jax.ShapeDtypeStruct((total, 2 * width), jnp.bfloat16),
                jax.ShapeDtypeStruct((1, width), jnp.float32),
                jax.ShapeDtypeStruct((1, width), jnp.float32),
            ),
            scratch_shapes=[pltpu.VMEM((total, width), jnp.bfloat16)] * 3
            + [pltpu.VMEM((total, width), jnp.float32)] * 2,
        )(raw, mix, resid, out_cols, lse, query_gain, key_gain, cosine, sine, doc_col, doc_row)

    return call


def local_by_heads(
    tokens_in,
    doc_lengths,
    attn_gain,
    w_query,
    key_weight,
    value_weight,
    w_output,
    query_norm_gain,
    key_norm_gain,
    mlp_gain,
    w_gate,
    w_up,
    w_down,
    out_grad,
):
    row_count, model_width = tokens_in.shape
    head_dim = query_norm_gain.shape[0]
    query_width = w_query.shape[1]
    kv_width = key_weight.shape[1]
    rank_count = 8
    pair_width = 2 * head_dim
    total = row_count * rank_count
    block = 256
    core = lax.axis_index("seq")
    shard = lax.axis_index("shard")
    rank = shard * 2 + core

    x_all = place_pieces(gather_pieces(tokens_in), rank, 0)

    shard_rows = w_query.shape[0]
    by_head = jnp.concatenate(
        [
            w_query.reshape(shard_rows, rank_count, pair_width),
            key_weight.reshape(shard_rows, rank_count, head_dim),
            value_weight.reshape(shard_rows, rank_count, head_dim),
        ],
        axis=2,
    )

    def head_columns(mask):
        picked = lax.dynamic_index_in_dim(by_head, rank ^ mask, 1, keepdims=False)
        return picked if mask == 0 else group_swap(picked, mask)

    head_weight = jnp.zeros((model_width, 2 * pair_width), jnp.bfloat16)
    for mask in (0, 2, 4, 6):
        head_weight = lax.dynamic_update_slice_in_dim(
            head_weight, head_columns(mask), (shard ^ (mask // 2)) * shard_rows, 0
        )

    out_part = lax.dynamic_slice_in_dim(w_output, core * row_count, row_count)
    out_weight = place_pieces(gather_pieces(out_part), rank, 0)
    grad_all = place_pieces(gather_pieces(out_grad), rank, 0)

    index = jnp.arange(total, dtype=jnp.int32)
    docs, offsets = doc_info(doc_lengths[0], index)
    half_dim = head_dim // 2
    inverse_freq = rope_base ** (-(jnp.arange(half_dim, dtype=jnp.float32) * 2.0 / head_dim))
    angles = offsets.astype(jnp.float32)[:, None] * inverse_freq[None, :]
    cosine = jnp.cos(angles)
    sine = jnp.sin(angles)
    cosine = jnp.concatenate([cosine] * 4, axis=1)
    sine = jnp.concatenate([-sine, sine, -sine, sine], axis=1)
    doc_column = docs[:, None]
    doc_row = docs[None, :]
    query_gain = jnp.concatenate([query_norm_gain] * 2)[None, :]
    key_gain = jnp.concatenate([key_norm_gain] * 2)[None, :]

    mix, normed, raw, lse = attention_forward(head_dim, block)(
        x_all, attn_gain[None, :], head_weight, query_gain, key_gain, cosine, sine,
        doc_column, doc_row,
    )
    mix_all = place_pieces(gather_pieces(mix), rank, 1)

    x_float = x_all.astype(jnp.float32)
    residual = x_float + dot_last(mix_all, out_weight)
    norm_two = rms_scale(residual)
    resid_hat = residual * norm_two
    normed_mid = (resid_hat * mlp_gain).astype(jnp.bfloat16)

    hidden_rows = w_gate.shape[0] // 2

    def own_rows(weight):
        return lax.dynamic_slice_in_dim(weight, core * hidden_rows, hidden_rows)

    gate_rows = own_rows(w_gate)
    up_rows = own_rows(w_up)
    down_rows = own_rows(w_down)
    gate = dot_last(normed_mid, gate_rows)
    up = dot_last(normed_mid, up_rows)
    grad_hidden = dot_last(grad_all, down_rows)
    gate_sig = jax.nn.sigmoid(gate)
    hidden = (gate * gate_sig * up).astype(jnp.bfloat16)
    gate_grad = (grad_hidden * up * gate_sig * (1.0 + gate * (1.0 - gate_sig))).astype(jnp.bfloat16)
    up_grad = (grad_hidden * gate * gate_sig).astype(jnp.bfloat16)
    mid_part = dot_plain(gate_grad, gate_rows) + dot_plain(up_grad, up_rows)
    grad_mid = scatter_sum(mid_part, rank)

    own_first = rank * row_count

    def own_tokens(values):
        return lax.dynamic_slice_in_dim(values, own_first, row_count)

    own_hat = own_tokens(resid_hat)
    grad_resid = out_grad.astype(jnp.float32) + root_mean_backward(
        own_hat, own_tokens(norm_two), mlp_gain, grad_mid
    )
    mlp_gain_part = jnp.sum(grad_mid * own_hat, axis=0)
    resid_all = place_pieces(gather_pieces(grad_resid.astype(jnp.bfloat16)), rank, 0)

    act_out = own_tokens(residual) + scatter_sum(dot_plain(hidden, down_rows), rank)

    mlp_grads = jnp.concatenate(
        [
            dot_first(gate_grad, normed_mid).astype(jnp.bfloat16),
            dot_first(up_grad, normed_mid).astype(jnp.bfloat16),
            dot_first(hidden, grad_all).astype(jnp.bfloat16),
        ],
        axis=0,
    )
    mlp_sums = rep_chain_sum(mlp_grads, 6)

    out_cols = lax.dynamic_slice_in_dim(out_weight, rank * pair_width, pair_width, 1)
    head_grads, query_part, key_part = attention_backward(head_dim, block)(
        raw, mix, resid_all, out_cols, lse, query_gain, key_gain, cosine, sine,
        doc_column, doc_row,
    )
    in_part = dot_last(head_grads, head_weight)
    x_norm = rms_scale(x_float)
    attn_gain_part = jnp.sum(in_part * (x_float * x_norm), axis=0)
    query_gain_part = query_part[0, :head_dim] + query_part[0, head_dim:]
    gains = sum_everywhere(
        jnp.concatenate(
            [attn_gain_part, mlp_gain_part, query_gain_part, key_part[0, :head_dim]]
        )[None, :]
    )[0]

    weight_part = dot_first(normed, head_grads).astype(jnp.bfloat16)
    resid_own = lax.dynamic_slice_in_dim(resid_all, own_first, row_count, 1)
    out_grads = dot_first(resid_own, mix_all).astype(jnp.bfloat16)

    def weight_block(mask):
        piece = lax.dynamic_slice_in_dim(weight_part, (rank ^ mask) * row_count, row_count)
        return piece if mask == 0 else group_swap(piece, mask)

    attn_grads = place_pieces([weight_block(mask) for mask in range(rank_count)], rank, 1)
    attn_grads = jnp.concatenate([attn_grads, out_grads], axis=1)
    attn_grads = rep_halving_sum(attn_grads).astype(jnp.float32)

    grad_in_norm = scatter_sum(in_part, rank)
    own_x = tokens_in.astype(jnp.float32)
    own_norm = rms_scale(own_x)
    in_grad = grad_resid + root_mean_backward(own_x * own_norm, own_norm, attn_gain, grad_in_norm)

    by_rank = attn_grads[:, : 2 * query_width].reshape(row_count, rank_count, 2 * pair_width)
    grad_query = by_rank[:, :, :pair_width].reshape(row_count, query_width)
    grad_key = by_rank[:, :, pair_width : pair_width + head_dim].reshape(row_count, kv_width)
    grad_value = by_rank[:, :, pair_width + head_dim :].reshape(row_count, kv_width)
    grad_output = attn_grads[:, 2 * query_width :]
    return (
        act_out,
        in_grad,
        gains[:model_width],
        grad_query,
        grad_key,
        grad_value,
        grad_output,
        gains[2 * model_width : 2 * model_width + head_dim],
        gains[2 * model_width + head_dim :],
        gains[model_width : 2 * model_width],
        mlp_sums[:hidden_rows],
        mlp_sums[hidden_rows : 2 * hidden_rows],
        mlp_sums[2 * hidden_rows :],
    )


def solution(mesh):
    placed = (
        P(("rep", "shard", "seq"), None),
        P("rep", None),
        P(),
        P("shard", None),
        P("shard", None),
        P("shard", None),
        P("shard", None),
        P(),
        P(),
        P(),
        P("shard", None),
        P("shard", None),
        P("shard", None),
        P(("rep", "shard", "seq"), None),
    )
    sizes = dict(mesh.shape)
    by_heads = sizes["rep"] == 4 and sizes["shard"] == 4 and sizes["seq"] == 2
    return jax.shard_map(
        local_by_heads if by_heads else local,
        mesh=mesh,
        in_specs=placed,
        out_specs=(
            P(("rep", "shard", "seq"), None),
            P(("rep", "shard", "seq"), None),
            P(),
            P(("shard", "seq"), None),
            P(("shard", "seq"), None),
            P(("shard", "seq"), None),
            P(("shard", "seq"), None),
            P(),
            P(),
            P(),
            P(("shard", "seq"), None),
            P(("shard", "seq"), None),
            P(("shard", "seq"), None),
        ),
        check_vma=False,
    )
```

```python
import jax
import jax.numpy as jnp
from jax import lax
from jax.experimental import pallas as pl
from jax.experimental.pallas import tpu as pltpu
from jax.sharding import PartitionSpec as P

norm_eps = 1e-05
rope_base = 1000000.0
very_low = -1e30
contract_last = (((1,), (1,)), ((), ()))
contract_first = (((0,), (0,)), ((), ()))


def rms_scale(values):
    return lax.rsqrt(jnp.mean(values * values, axis=-1, keepdims=True) + norm_eps)


def root_mean_backward(normed, factor, gain, upstream):
    scaled = upstream * gain
    return factor * (scaled - normed * jnp.mean(scaled * normed, axis=-1, keepdims=True))


def rope_tables(positions, head_dim):
    half_dim = head_dim // 2
    inverse_freq = rope_base ** (-(jnp.arange(half_dim, dtype=jnp.float32) * 2.0 / head_dim))
    angles = positions.astype(jnp.float32)[:, None] * inverse_freq[None, :]
    return (jnp.cos(angles)[:, None, :], jnp.sin(angles)[:, None, :])


def rotate_pairs(values, cosine_table, sine_values):
    half_dim = values.shape[-1] // 2
    lower_half = values[..., :half_dim]
    upper_half = values[..., half_dim:]
    return jnp.concatenate(
        [
            lower_half * cosine_table - upper_half * sine_values,
            upper_half * cosine_table + lower_half * sine_values,
        ],
        axis=-1,
    )


def rotate_back(grads, cosine_table, sine_values):
    half_dim = grads.shape[-1] // 2
    lower_half = grads[..., :half_dim]
    upper_half = grads[..., half_dim:]
    return jnp.concatenate(
        [
            lower_half * cosine_table + upper_half * sine_values,
            upper_half * cosine_table - lower_half * sine_values,
        ],
        axis=-1,
    )


def doc_info(lengths, positions):
    doc_ends = jnp.cumsum(lengths)
    finished = doc_ends[None, :] <= positions[:, None]
    doc_ids = jnp.sum(finished.astype(jnp.int32), axis=1)
    doc_first = jnp.sum(jnp.where(finished, lengths[None, :], 0), axis=1)
    return (doc_ids, positions - doc_first)


def local(
    tokens_in,
    doc_lengths,
    attn_gain,
    w_query,
    key_weight,
    value_weight,
    w_output,
    query_norm_gain,
    key_norm_gain,
    mlp_gain,
    w_gate,
    w_up,
    w_down,
    out_grad,
):
    row_count = tokens_in.shape[0]
    model_width = tokens_in.shape[1]
    head_dim = query_norm_gain.shape[0]
    query_width = w_query.shape[1]
    kv_width = key_weight.shape[1]
    kv_heads = kv_width // head_dim
    head_grouping = query_width // kv_width
    score_scale = head_dim ** (-0.5)
    rank_count = lax.axis_size("shard") * lax.axis_size("seq")
    group_rows = row_count * rank_count
    first_row = lax.axis_index(("shard", "seq")) * row_count
    key_block = min(512, group_rows)
    block_count = group_rows // key_block
    key_index = jnp.arange(group_rows, dtype=jnp.int32)
    key_docs, key_offset = doc_info(doc_lengths[0], key_index)
    query_index = first_row + jnp.arange(row_count, dtype=jnp.int32)
    query_docs = lax.dynamic_slice_in_dim(key_docs, first_row, row_count)
    query_offset = lax.dynamic_slice_in_dim(key_offset, first_row, row_count)
    cosine_table, sine_values = rope_tables(query_offset, head_dim)
    x_float = tokens_in.astype(jnp.float32)
    norm_one = rms_scale(x_float)
    x_hat = x_float * norm_one
    normalized_input = (x_hat * attn_gain).astype(jnp.bfloat16)
    pieces = (
        lax.all_gather(w_query, "shard", axis=0, tiled=True),
        lax.all_gather(key_weight, "shard", axis=0, tiled=True),
        lax.all_gather(value_weight, "shard", axis=0, tiled=True),
    )
    in_cols = normalized_input
    queries, key_proj, value_proj = tuple(
        (jnp.dot(in_cols, weight, preferred_element_type=jnp.float32) for weight in pieces)
    )
    query_heads = queries.reshape(row_count, query_width // head_dim, head_dim)
    query_norm = rms_scale(query_heads)
    query_normalized = query_heads * query_norm
    query_rotated = rotate_pairs(
        query_normalized * query_norm_gain, cosine_table, sine_values
    ).astype(jnp.bfloat16)
    key_head_rows = key_proj.reshape(row_count, kv_heads, head_dim)
    key_head_norm = rms_scale(key_head_rows)
    key_normalized = key_head_rows * key_head_norm
    key_rot = rotate_pairs(key_normalized * key_norm_gain, cosine_table, sine_values).astype(
        jnp.bfloat16
    )
    value_rows = value_proj.astype(jnp.bfloat16)
    key_all, value_all = (
        lax.all_gather(key_rot.reshape(row_count, kv_width), ("shard", "seq"), axis=0, tiled=True),
        lax.all_gather(value_rows, ("shard", "seq"), axis=0, tiled=True),
    )
    query_grouped = query_rotated.reshape(row_count, kv_heads, head_grouping, head_dim)

    def block_mask(offset, span_rows):
        docs_here = lax.dynamic_slice_in_dim(key_docs, offset, span_rows)
        index_here = offset + jnp.arange(span_rows, dtype=jnp.int32)
        return (query_docs[:, None] == docs_here[None, :]) & (
            index_here[None, :] <= query_index[:, None]
        )

    def block_scores(offset, span_rows, allowed):
        key_rows = lax.dynamic_slice_in_dim(key_all, offset, span_rows, 0).reshape(
            span_rows, kv_heads, head_dim
        )
        value_block = lax.dynamic_slice_in_dim(value_all, offset, span_rows, 0).reshape(
            span_rows, kv_heads, head_dim
        )
        scores = (
            jnp.einsum(
                "tgjd,rgd->gjtr", query_grouped, key_rows, preferred_element_type=jnp.float32
            )
            * score_scale
        )
        return (jnp.where(allowed, scores, very_low), key_rows, value_block)

    def total_block(block_index, running):
        offset = block_index * key_block
        allowed = block_mask(offset, key_block)

        def total_accumulate(softmax_state):
            row_high, row_total = softmax_state
            scores, key_rows, value_block = block_scores(offset, key_block, allowed)
            new_high = jnp.maximum(row_high, jnp.max(scores, axis=-1))
            exp_scores = jnp.where(allowed, jnp.exp(scores - new_high[..., None]), 0.0)
            row_total = row_total * jnp.exp(row_high - new_high) + jnp.sum(exp_scores, axis=-1)
            return (new_high, row_total)

        return lax.cond(
            jnp.any(allowed), total_accumulate, lambda softmax_state: softmax_state, running
        )

    softmax_init = (
        jnp.full((kv_heads, head_grouping, row_count), very_low, jnp.float32),
        jnp.zeros((kv_heads, head_grouping, row_count), jnp.float32),
    )
    row_high, row_total = lax.fori_loop(0, block_count, total_block, softmax_init)
    log_total = row_high + jnp.log(row_total)

    def mix_block(block_index, weighted):
        offset = block_index * key_block
        allowed = block_mask(offset, key_block)

        def mix_accumulate(current):
            scores, key_rows, value_block = block_scores(offset, key_block, allowed)
            attn_prob = jnp.where(allowed, jnp.exp(scores - log_total[..., None]), 0.0).astype(
                jnp.bfloat16
            )
            return current + jnp.einsum(
                "gjtr,rgd->gjtd", attn_prob, value_block, preferred_element_type=jnp.float32
            )

        return lax.cond(jnp.any(allowed), mix_accumulate, lambda current: current, weighted)

    weighted = lax.fori_loop(
        0,
        block_count,
        mix_block,
        jnp.zeros((kv_heads, head_grouping, row_count, head_dim), jnp.float32),
    )
    head_mixture = (
        weighted.transpose(2, 0, 1, 3).reshape(row_count, query_width).astype(jnp.bfloat16)
    )
    attn_part = lax.dot_general(
        head_mixture,
        lax.all_gather(w_output, "shard", axis=0, tiled=True),
        contract_last,
        preferred_element_type=jnp.float32,
    )
    residual = x_float + attn_part
    norm_two = rms_scale(residual)
    resid_hat = residual * norm_two
    normed_mid = (resid_hat * mlp_gain).astype(jnp.bfloat16)
    gate_rows = lax.all_gather(w_gate, "shard", axis=0, tiled=True)
    up_rows = lax.all_gather(w_up, "shard", axis=0, tiled=True)
    down_rows = lax.all_gather(w_down, "shard", axis=0, tiled=True)
    gate_part = lax.dot_general(
        normed_mid, gate_rows, contract_last, preferred_element_type=jnp.float32
    )
    up_part = lax.dot_general(
        normed_mid, up_rows, contract_last, preferred_element_type=jnp.float32
    )
    hidden_part = (gate_part * jax.nn.sigmoid(gate_part) * up_part).astype(jnp.bfloat16)
    mlp_sum = jnp.dot(hidden_part, down_rows, preferred_element_type=jnp.float32)
    mlp_gate_store = gate_part
    mlp_up_store = up_part
    hidden_store = hidden_part
    mlp_sum, gate_store, up_store, hidden_store = (
        mlp_sum,
        mlp_gate_store,
        mlp_up_store,
        hidden_store,
    )
    act_out = residual + mlp_sum
    grad_float = out_grad.astype(jnp.float32)
    gate_rows = lax.all_gather(w_gate, "shard", axis=0, tiled=True)
    up_rows = lax.all_gather(w_up, "shard", axis=0, tiled=True)
    down_rows = lax.all_gather(w_down, "shard", axis=0, tiled=True)
    span_rows = gate_rows.shape[0]
    gate_part = gate_store
    up_part = up_store
    grad_hidden = lax.dot_general(
        out_grad, down_rows, contract_last, preferred_element_type=jnp.float32
    )
    gate_sig = jax.nn.sigmoid(gate_part)
    gate_grad = (grad_hidden * up_part * gate_sig * (1.0 + gate_part * (1.0 - gate_sig))).astype(
        jnp.bfloat16
    )
    up_grad = (grad_hidden * gate_part * gate_sig).astype(jnp.bfloat16)
    grad_mid = jnp.dot(gate_grad, gate_rows, preferred_element_type=jnp.float32) + jnp.dot(
        up_grad, up_rows, preferred_element_type=jnp.float32
    )
    gate_grad_store = gate_grad
    up_grad_store = up_grad
    grad_mid, gate_grad_store, up_grad_store = (grad_mid, gate_grad_store, up_grad_store)
    grad_resid = grad_float + root_mean_backward(resid_hat, norm_two, mlp_gain, grad_mid)
    mlp_gain_part = jnp.sum(grad_mid * resid_hat, axis=0)
    grad_resid_b = grad_resid.astype(jnp.bfloat16)
    resid_cols = grad_resid_b
    mixing_gradient = jnp.dot(
        resid_cols,
        lax.all_gather(w_output, "shard", axis=0, tiled=True),
        preferred_element_type=jnp.float32,
    ).astype(jnp.bfloat16)
    mix_grouped = mixing_gradient.reshape(row_count, kv_heads, head_grouping, head_dim)
    delta_row_values = jnp.sum(
        (mixing_gradient.astype(jnp.float32) * head_mixture.astype(jnp.float32)).reshape(
            row_count, kv_heads, head_grouping, head_dim
        ),
        axis=-1,
    ).transpose(1, 2, 0)

    def score_grads(offset, span_rows, allowed):
        scores, key_rows, value_block = block_scores(offset, span_rows, allowed)
        attn_prob = jnp.where(allowed, jnp.exp(scores - log_total[..., None]), 0.0)
        grad_prob = jnp.einsum(
            "tgjd,rgd->gjtr", mix_grouped, value_block, preferred_element_type=jnp.float32
        )
        grad_score = (attn_prob * (grad_prob - delta_row_values[..., None])).astype(jnp.bfloat16)
        return (attn_prob, grad_score, key_rows)

    def query_pass(block_index, grad_sum):
        offset = block_index * key_block
        allowed = block_mask(offset, key_block)

        def query_accumulate(current):
            attn_prob, grad_score, key_rows = score_grads(offset, key_block, allowed)
            return current + score_scale * jnp.einsum(
                "gjtr,rgd->tgjd", grad_score, key_rows, preferred_element_type=jnp.float32
            )

        return lax.cond(jnp.any(allowed), query_accumulate, lambda current: current, grad_sum)

    query_rot_grad = lax.fori_loop(
        0,
        block_count,
        query_pass,
        jnp.zeros((row_count, kv_heads, head_grouping, head_dim), jnp.float32),
    )

    def one_block(start_row):
        allowed = block_mask(start_row, key_block)

        def compute(unused):
            attn_prob, grad_score, key_rows = score_grads(start_row, key_block, allowed)
            key_grad = score_scale * jnp.einsum(
                "gjtr,tgjd->rgd", grad_score, query_grouped, preferred_element_type=jnp.float32
            )
            value_grad = jnp.einsum(
                "gjtr,tgjd->rgd",
                attn_prob.astype(jnp.bfloat16),
                mix_grouped,
                preferred_element_type=jnp.float32,
            )
            return jnp.concatenate(
                [key_grad.reshape(key_block, kv_width), value_grad.reshape(key_block, kv_width)],
                axis=1,
            )

        return lax.cond(
            jnp.any(allowed),
            compute,
            lambda unused: jnp.zeros((key_block, 2 * kv_width), jnp.float32),
            0,
        )

    starts = key_block * jnp.arange(
        row_count * lax.axis_size(("shard", "seq")) // key_block, dtype=jnp.int32
    )
    kv_summed = lax.psum_scatter(
        lax.map(one_block, starts).reshape(
            row_count * lax.axis_size(("shard", "seq")), 2 * kv_width
        ),
        ("shard", "seq"),
        scatter_dimension=0,
        tiled=True,
    )
    key_rot_grad = kv_summed[:, :kv_width].reshape(row_count, kv_heads, head_dim)
    value_grad_b = kv_summed[:, kv_width:].astype(jnp.bfloat16)
    key_unrotated = rotate_back(key_rot_grad, cosine_table, sine_values)
    key_gain_part = jnp.sum(key_unrotated * key_normalized, axis=(0, 1))
    key_row_gradient = (
        root_mean_backward(key_normalized, key_head_norm, key_norm_gain, key_unrotated)
        .reshape(row_count, kv_width)
        .astype(jnp.bfloat16)
    )
    query_unrot = rotate_back(
        query_rot_grad.reshape(row_count, query_width // head_dim, head_dim),
        cosine_table,
        sine_values,
    )
    query_gain_part = jnp.sum(query_unrot * query_normalized, axis=(0, 1))
    grad_query_rows = (
        root_mean_backward(query_normalized, query_norm, query_norm_gain, query_unrot)
        .reshape(row_count, query_width)
        .astype(jnp.bfloat16)
    )
    query_rows, key_rows, value_rows_w = lax.all_gather(
        (w_query, key_weight, value_weight), "shard", axis=0, tiled=True
    )
    grad_in_norm = (
        lax.dot_general(
            grad_query_rows, query_rows, contract_last, preferred_element_type=jnp.float32
        )
        + lax.dot_general(
            key_row_gradient, key_rows, contract_last, preferred_element_type=jnp.float32
        )
        + lax.dot_general(
            value_grad_b, value_rows_w, contract_last, preferred_element_type=jnp.float32
        )
    )
    in_grad = grad_resid + root_mean_backward(x_hat, norm_one, attn_gain, grad_in_norm)
    attn_gain_part = jnp.sum(grad_in_norm * x_hat, axis=0)
    grad_attn_gain, grad_mlp_gain, grad_query_gain, grad_key_gain = lax.psum(
        (attn_gain_part, mlp_gain_part, query_gain_part, key_gain_part), ("rep", "shard", "seq")
    )
    attn_grads = jnp.concatenate([grad_query_rows, key_row_gradient, value_grad_b], axis=1)
    d_share = model_width // rank_count
    in_own, resid_own, gate_own, up_own, hidden_own = (
        lax.all_to_all(normalized_input, ("shard", "seq"), split_axis=1, concat_axis=0, tiled=True),
        lax.all_to_all(grad_resid_b, ("shard", "seq"), split_axis=1, concat_axis=0, tiled=True),
        lax.all_to_all(gate_grad_store, ("shard", "seq"), split_axis=1, concat_axis=0, tiled=True),
        lax.all_to_all(up_grad_store, ("shard", "seq"), split_axis=1, concat_axis=0, tiled=True),
        lax.all_to_all(hidden_store, ("shard", "seq"), split_axis=1, concat_axis=0, tiled=True),
    )
    attn_piece = lax.all_gather(attn_grads, ("shard", "seq"), axis=0, tiled=True)
    mix_piece = lax.all_gather(head_mixture, ("shard", "seq"), axis=0, tiled=True)
    mid_piece = lax.all_gather(normed_mid, ("shard", "seq"), axis=0, tiled=True)
    grad_piece = lax.all_gather(out_grad, ("shard", "seq"), axis=0, tiled=True)
    span_rows = attn_piece.shape[0]
    in_cols = in_own
    resid_cols = resid_own
    attn_rows = jnp.concatenate(
        [
            lax.dot_general(
                in_cols, attn_piece, contract_first, preferred_element_type=jnp.float32
            ),
            lax.dot_general(
                resid_cols, mix_piece, contract_first, preferred_element_type=jnp.float32
            ),
        ],
        axis=1,
    )
    mlp_rows = jnp.concatenate(
        [
            lax.dot_general(
                gate_own, mid_piece, contract_first, preferred_element_type=jnp.float32
            ),
            lax.dot_general(up_own, mid_piece, contract_first, preferred_element_type=jnp.float32),
            lax.dot_general(
                hidden_own, grad_piece, contract_first, preferred_element_type=jnp.float32
            ),
        ],
        axis=1,
    )
    group_grads = jnp.concatenate([attn_rows, mlp_rows], axis=0)
    own_grads = lax.psum(group_grads, "rep")
    attn_block_grads = own_grads[:d_share]
    mlp_block_grads = own_grads[d_share:]
    grad_query = attn_block_grads[:, :query_width]
    grad_key = attn_block_grads[:, query_width : query_width + kv_width]
    grad_value = attn_block_grads[:, query_width + kv_width : query_width + 2 * kv_width]
    grad_output = attn_block_grads[:, query_width + 2 * kv_width :]
    grad_gate = mlp_block_grads[:, :model_width]
    grad_up = mlp_block_grads[:, model_width : 2 * model_width]
    grad_down = mlp_block_grads[:, 2 * model_width :]
    return (
        act_out,
        in_grad,
        grad_attn_gain,
        grad_query,
        grad_key,
        grad_value,
        grad_output,
        grad_query_gain,
        grad_key_gain,
        grad_mlp_gain,
        grad_gate,
        grad_up,
        grad_down,
    )


group_axes = ("shard", "seq")


def group_swap(values, mask):
    return lax.ppermute(values, group_axes, [(rank, rank ^ mask) for rank in range(8)])


def rep_swap(values, mask):
    return lax.ppermute(values, "rep", [(rank, rank ^ mask) for rank in range(4)])


xor_order = (0, 2, 4, 6, 1, 3, 5, 7)


def gather_near(own):
    return [own] + [group_swap(own, mask) for mask in (2, 4, 6)]


def gather_far(near):
    return [group_swap(piece, 1) for piece in near]


def after(values, marker):
    return lax.optimization_barrier((values, marker))[0]


def add_rounded(left, right):
    return (left.astype(jnp.float32) + right.astype(jnp.float32)).astype(jnp.bfloat16)


def scatter_sum(near_part, far_part):
    swapped = group_swap(far_part.astype(jnp.bfloat16), 1)
    width = near_part.shape[0] // 4
    halves = [
        near_part[at : at + width] + swapped[at : at + width].astype(jnp.float32)
        for at in range(0, 4 * width, width)
    ]
    total = halves[0]
    moved = [
        group_swap(half.astype(jnp.bfloat16), mask) for mask, half in zip((2, 4, 6), halves[1:])
    ]
    for piece in moved:
        total = total + piece.astype(jnp.float32)
    return total


def rep_halving_sum(values):
    place = lax.axis_index("rep")
    low = place % 2
    high = place // 2
    half = values.shape[0] // 2
    quarter = half // 2
    kept = lax.dynamic_slice_in_dim(values, low * half, half)
    sent = lax.dynamic_slice_in_dim(values, (1 - low) * half, half)
    part = add_rounded(kept, rep_swap(sent, 1))
    kept = lax.dynamic_slice_in_dim(part, high * quarter, quarter)
    sent = lax.dynamic_slice_in_dim(part, (1 - high) * quarter, quarter)
    part = add_rounded(kept, rep_swap(sent, 2))
    other = rep_swap(part, 2)
    part = jnp.where(
        high == 0, jnp.concatenate([part, other]), jnp.concatenate([other, part])
    )
    other = rep_swap(part, 1)
    return jnp.where(low == 0, jnp.concatenate([part, other]), jnp.concatenate([other, part]))


def sum_everywhere(values):
    for mask in (1, 2, 4):
        values = values + group_swap(values, mask)
    for mask in (1, 2):
        values = values + rep_swap(values, mask)
    return values


def lower_lanes(shape, width):
    return lax.broadcasted_iota(jnp.int32, shape, 1) % (2 * width) < width


def pair_scale(values, head_dim):
    lower = lower_lanes(values.shape, head_dim)
    low = jnp.sum(jnp.where(lower, values, 0.0), axis=1, keepdims=True)
    high = jnp.sum(jnp.where(lower, 0.0, values), axis=1, keepdims=True)
    return jnp.where(lower, low, high) * (1.0 / head_dim)


def swap_halves(values, head_dim):
    width = values.shape[1]
    half = head_dim // 2
    return jnp.where(
        lower_lanes(values.shape, half),
        pltpu.roll(values, width - half, 1),
        pltpu.roll(values, half, 1),
    )


def rotated_heads(raw, query_gain, key_gain, cosine, sine, head_dim):
    width = 2 * head_dim
    queries = raw[:, :width]
    keys = raw[:, width:]
    query_norm = lax.rsqrt(pair_scale(queries * queries, head_dim) + norm_eps)
    key_norm = lax.rsqrt(pair_scale(keys * keys, head_dim) + norm_eps)
    query_hat = queries * query_norm
    key_hat = keys * key_norm
    scaled = query_hat * query_gain
    query_rot = scaled * cosine + swap_halves(scaled, head_dim) * sine
    scaled = key_hat * key_gain
    key_rot = scaled * cosine + swap_halves(scaled, head_dim) * sine
    lower = lower_lanes(keys.shape, head_dim)
    key_twice = jnp.where(lower, key_rot, pltpu.roll(key_rot, head_dim, 1))
    value_twice = jnp.where(lower, pltpu.roll(keys, head_dim, 1), keys)
    return query_hat, query_norm, key_hat, key_norm, query_rot, key_twice, value_twice


def stack_heads(values, head_dim):
    lower = lower_lanes(values.shape, head_dim)
    zero = jnp.zeros_like(values)
    return jnp.concatenate(
        [jnp.where(lower, values, zero), jnp.where(lower, zero, values)], axis=0
    )


def join_heads(stacked, head_dim):
    rows = stacked.shape[0] // 2
    lower = lower_lanes((rows, stacked.shape[1]), head_dim)
    return jnp.where(lower, stacked[:rows], stacked[rows:])


def allowed_pairs(doc_column, doc_row, first, rows, span):
    row_index = first + lax.broadcasted_iota(jnp.int32, (rows, span), 0)
    key_index = lax.broadcasted_iota(jnp.int32, (rows, span), 1)
    return (doc_column == doc_row) & (key_index <= row_index)


def dot_last(left, right):
    return lax.dot_general(left, right, contract_last, preferred_element_type=jnp.float32)


def dot_first(left, right):
    return lax.dot_general(left, right, contract_first, preferred_element_type=jnp.float32)


def dot_plain(left, right):
    return jnp.dot(left, right, preferred_element_type=jnp.float32)


def scalar_spec():
    return pl.BlockSpec(memory_space=pltpu.SMEM)


def whole_spec():
    return pl.BlockSpec(memory_space=pltpu.VMEM)


def any_spec():
    return pl.BlockSpec(memory_space=pltpu.HBM)


def in_hbm(values):
    return [pltpu.with_memory_space_constraint(value, pltpu.HBM) for value in values]


def start_copies(copies, sems, first=0):
    handles = [
        pltpu.make_async_copy(source, target, sems.at[first + at])
        for at, (source, target) in enumerate(copies)
    ]
    for handle in handles:
        handle.start()
    return handles


def pack_heads(w_query, key_weight, value_weight, places, head_dim):
    rows = w_query.shape[0]
    width = 2 * head_dim

    def kernel(place_ref, query_ref, key_ref, value_ref, *out_refs):
        shard = place_ref[0]
        core = place_ref[1]
        for step, out_ref in enumerate(out_refs):
            other = shard ^ step
            out_ref[:, :width] = query_ref[
                :, pl.ds(pl.multiple_of((2 * other + core) * width, width), width)
            ]
            lanes = pl.ds(pl.multiple_of(other * width, width), width)
            keys = key_ref[:, lanes].astype(jnp.float32)
            values = value_ref[:, lanes].astype(jnp.float32)
            lower = lower_lanes(keys.shape, head_dim)
            first = jnp.where(lower, keys, pltpu.roll(values, head_dim, 1))
            second = jnp.where(lower, pltpu.roll(keys, head_dim, 1), values)
            out_ref[:, width:] = jnp.where(core == 0, first, second).astype(jnp.bfloat16)

    return pl.pallas_call(
        kernel,
        name="pack_heads",
        in_specs=[scalar_spec()] + [whole_spec()] * 3,
        out_shape=(jax.ShapeDtypeStruct((rows, 2 * width), jnp.bfloat16),) * 4,
    )(places, w_query, key_weight, value_weight)


def attention_forward(head_dim, block):
    score_scale = head_dim ** (-0.5)
    width = 2 * head_dim

    def kernel(
        place_ref, gain_ref, piece_0, piece_1, piece_2, piece_3, query_gain_ref,
        key_gain_ref, cos_hbm, sin_hbm, doc_col_hbm, doc_row_ref, *refs,
    ):
        x_refs = refs[:8]
        mix_ref, normed_out, raw_out, lse_out, weight_out = refs[8:13]
        query_scr, key_scr, value_scr, x_scr, sems = refs[13:18]
        cos_ref, sin_ref, doc_col_ref, normed_ref, raw_ref, lse_ref, weight_ref = refs[18:]
        total = cos_ref.shape[0]
        shard = place_ref[0]
        rank = 2 * shard + place_ref[1]
        piece_rows = piece_0.shape[0]
        own_rows = total // 8
        copies = []
        for step, piece in enumerate((piece_0, piece_1, piece_2, piece_3)):
            first = pl.multiple_of((shard ^ step) * piece_rows, piece_rows)
            copies.append((piece, weight_ref.at[pl.ds(first, piece_rows), :]))
        for step, x_ref in enumerate(x_refs):
            copies.append((x_ref, x_scr.at[pl.ds(step * own_rows, own_rows), :]))
        copies += [(cos_hbm, cos_ref), (sin_hbm, sin_ref), (doc_col_hbm, doc_col_ref)]
        handles = start_copies(copies, sems)
        for handle in handles:
            handle.wait()
        outward = start_copies([(weight_ref, weight_out)], sems, len(copies))
        for half in range(0, total, 4 * own_rows):
            for step in range(4):
                x = x_scr[pl.ds(half + step * own_rows, own_rows), :].astype(jnp.float32)
                normed_ref[pl.ds(half + step * own_rows, own_rows), :] = (
                    x * rms_scale(x) * gain_ref[...]
                ).astype(jnp.bfloat16)
            raw = dot_plain(normed_ref[pl.ds(half, 4 * own_rows), :], weight_ref[...])
            for step in range(4):
                mask = xor_order[half // own_rows + step]
                first = pl.multiple_of((rank ^ mask) * own_rows, own_rows)
                raw_ref[pl.ds(first, own_rows), :] = raw[step * own_rows : (step + 1) * own_rows]
        outward += start_copies(
            [(normed_ref, normed_out), (raw_ref, raw_out)], sems, len(copies) + 1
        )
        for first in range(0, total, block):
            rows = pl.ds(first, block)
            parts = rotated_heads(
                raw_ref[rows, :], query_gain_ref[...], key_gain_ref[...], cos_ref[rows, :],
                sin_ref[rows, :], head_dim,
            )
            query_scr[rows, :] = parts[4].astype(jnp.bfloat16)
            key_scr[rows, :] = parts[5].astype(jnp.bfloat16)
            value_scr[rows, :] = parts[6].astype(jnp.bfloat16)
        for first in range(0, total, block):
            rows = pl.ds(first, block)
            span = first + block
            stacked = stack_heads(query_scr[rows, :], head_dim)
            allowed = allowed_pairs(
                doc_col_ref[rows, :], doc_row_ref[:, :span], first, block, span
            )
            allowed = jnp.concatenate([allowed, allowed], axis=0)
            scores = dot_last(stacked, key_scr[:span, :]) * score_scale
            scores = jnp.where(allowed, scores, very_low)
            high = jnp.max(scores, axis=1, keepdims=True)
            powers = jnp.exp(scores - high)
            row_total = jnp.sum(powers, axis=1, keepdims=True)
            probs = (powers * (1.0 / row_total)).astype(jnp.bfloat16)
            mixed = dot_plain(probs, value_scr[:span, :])
            mix_ref[rows, :] = join_heads(mixed, head_dim).astype(jnp.bfloat16)
            lse_ref[pl.ds(2 * first, 2 * block), :] = high + jnp.log(row_total)
        outward += start_copies([(lse_ref, lse_out)], sems, len(copies) + 3)
        for handle in outward:
            handle.wait()

    def call(places, xs, gain, pieces, query_gain, key_gain, cosine, sine, doc_column, doc_row):
        total, model = cosine.shape[0], xs[0].shape[1]
        return pl.pallas_call(
            kernel,
            name="attention_forward",
            in_specs=[scalar_spec(), whole_spec()]
            + [any_spec()] * 4
            + [whole_spec()] * 2
            + [any_spec()] * 3
            + [whole_spec()]
            + [any_spec()] * 8,
            out_specs=(whole_spec(),) + (any_spec(),) * 4,
            compiler_params=pltpu.CompilerParams(vmem_limit_bytes=32 << 20),
            out_shape=(
                jax.ShapeDtypeStruct((total, width), jnp.bfloat16),
                pltpu.HBM((total, model), jnp.bfloat16),
                pltpu.HBM((total, 2 * width), jnp.float32),
                pltpu.HBM((2 * total, 1), jnp.float32),
                pltpu.HBM((model, 2 * width), jnp.bfloat16),
            ),
            scratch_shapes=[pltpu.VMEM((total, width), jnp.bfloat16)] * 3
            + [
                pltpu.VMEM((total, model), jnp.bfloat16),
                pltpu.SemaphoreType.DMA((19,)),
                pltpu.VMEM((total, width), jnp.float32),
                pltpu.VMEM((total, width), jnp.float32),
                pltpu.VMEM((total, 1), jnp.int32),
                pltpu.VMEM((total, model), jnp.bfloat16),
                pltpu.VMEM((total, 2 * width), jnp.float32),
                pltpu.VMEM((2 * total, 1), jnp.float32),
                pltpu.VMEM((model, 2 * width), jnp.bfloat16),
            ],
        )(
            places, gain, *in_hbm(pieces), query_gain, key_gain,
            *in_hbm((cosine, sine, doc_column)), doc_row, *in_hbm(xs),
        )

    return call


def residual_stage(places, mix_pieces, out_pieces, xs, mlp_gain):
    total, model = 8 * xs[0].shape[0], xs[0].shape[1]
    width = mix_pieces[0].shape[1]
    own_rows = out_pieces[0].shape[0]

    def kernel(place_ref, gain_ref, *refs):
        mix_refs = refs[:8]
        out_refs = refs[8:16]
        x_refs = refs[16:24]
        normed_ref, mixed_out, cols_out, resid_out, hat_out, scale_ref = refs[24:30]
        weight_scr, x_scr, sems, mixed_ref, cols_ref, resid_ref, hat_ref = refs[30:]
        rank = 2 * place_ref[0] + place_ref[1]
        copies = []
        for mask, ref in zip(xor_order, out_refs):
            first = pl.multiple_of((rank ^ mask) * own_rows, own_rows)
            copies.append((ref, weight_scr.at[pl.ds(first, own_rows), :]))
        for step, row_mask in enumerate(xor_order):
            first = pl.multiple_of((rank ^ row_mask) * own_rows, own_rows)
            for mask, ref in zip(xor_order, mix_refs):
                lanes = pl.ds(pl.multiple_of((rank ^ mask) * width, width), width)
                copies.append(
                    (
                        ref.at[pl.ds(first, own_rows), :],
                        mixed_ref.at[pl.ds(step * own_rows, own_rows), lanes],
                    )
                )
        for step, ref in enumerate(x_refs):
            copies.append((ref, x_scr.at[pl.ds(step * own_rows, own_rows), :]))
        handles = start_copies(copies, sems)
        for handle in handles:
            handle.wait()
        cols_ref[...] = weight_scr[:, pl.ds(pl.multiple_of(rank * width, width), width)]
        outward = start_copies(
            [(mixed_ref, mixed_out), (cols_ref, cols_out)], sems, len(copies)
        )
        for first in range(0, total, total // 4):
            rows = pl.ds(first, total // 4)
            resid = x_scr[rows, :].astype(jnp.float32) + dot_last(
                mixed_ref[rows, :], weight_scr[...]
            )
            scale = rms_scale(resid)
            hat = resid * scale
            normed_ref[rows, :] = (hat * gain_ref[...]).astype(jnp.bfloat16)
            if first == 0:
                resid_ref[...] = resid[:own_rows]
                hat_ref[...] = hat[:own_rows]
                scale_ref[...] = scale[:own_rows]
                outward += start_copies(
                    [(resid_ref, resid_out), (hat_ref, hat_out)], sems, len(copies) + 2
                )
        for handle in outward:
            handle.wait()

    return pl.pallas_call(
        kernel,
        name="residual_stage",
        in_specs=[scalar_spec(), whole_spec()] + [any_spec()] * 24,
        out_specs=(whole_spec(),) + (any_spec(),) * 4 + (whole_spec(),),
        compiler_params=pltpu.CompilerParams(vmem_limit_bytes=24 << 20),
        out_shape=(
            jax.ShapeDtypeStruct((total, model), jnp.bfloat16),
            pltpu.HBM((total, model), jnp.bfloat16),
            pltpu.HBM((model, width), jnp.bfloat16),
            pltpu.HBM((own_rows, model), jnp.float32),
            pltpu.HBM((own_rows, model), jnp.float32),
            jax.ShapeDtypeStruct((own_rows, 1), jnp.float32),
        ),
        scratch_shapes=[
            pltpu.VMEM((model, model), jnp.bfloat16),
            pltpu.VMEM((total, model), jnp.bfloat16),
            pltpu.SemaphoreType.DMA((84,)),
            pltpu.VMEM((total, model), jnp.bfloat16),
            pltpu.VMEM((model, width), jnp.bfloat16),
            pltpu.VMEM((own_rows, model), jnp.float32),
            pltpu.VMEM((own_rows, model), jnp.float32),
        ],
    )(places, mlp_gain, *in_hbm((*mix_pieces, *out_pieces, *xs)))


def stack_rows(pieces):
    rows, width = pieces[0].shape

    def kernel(*refs):
        out_ref, sems = refs[-2:]
        handles = start_copies(
            [(ref, out_ref.at[pl.ds(at * rows, rows), :]) for at, ref in enumerate(refs[:-2])],
            sems,
        )
        for handle in handles:
            handle.wait()

    return pl.pallas_call(
        kernel,
        name="stack_rows",
        in_specs=[any_spec()] * len(pieces),
        compiler_params=pltpu.CompilerParams(vmem_limit_bytes=8 << 20),
        scratch_shapes=[pltpu.SemaphoreType.DMA((len(pieces),))],
        out_shape=jax.ShapeDtypeStruct((rows * len(pieces), width), pieces[0].dtype),
    )(*pieces)


def attention_backward(head_dim, block):
    score_scale = head_dim ** (-0.5)
    width = 2 * head_dim

    def kernel(
        place_ref, raw_ref, mix_ref, out_cols_ref, lse_ref, query_gain_ref,
        key_gain_ref, cos_ref, sin_ref, doc_col_ref, doc_row_ref, normed_ref, *refs,
    ):
        resid_refs = refs[:8]
        grads_out_ref, query_part_ref, key_part_ref, resid_own_ref = refs[8:12]
        refs = refs[12:]
        piece_refs = refs[:8]
        query_scr, key_scr, value_scr, mix_grad_scr, grads_ref, key_sum, value_sum = refs[8:15]
        resid_scr, sems = refs[15:]
        total = raw_ref.shape[0]
        own_rows = total // 8
        rank = 2 * place_ref[0] + place_ref[1]
        handles = start_copies(
            [
                (ref, resid_scr.at[pl.ds(step * own_rows, own_rows), :])
                for step, ref in enumerate(resid_refs)
            ],
            sems,
        )
        for first in range(0, total, block):
            rows = pl.ds(first, block)
            parts = rotated_heads(
                raw_ref[rows, :], query_gain_ref[...], key_gain_ref[...], cos_ref[rows, :],
                sin_ref[rows, :], head_dim,
            )
            query_scr[rows, :] = parts[4].astype(jnp.bfloat16)
            key_scr[rows, :] = parts[5].astype(jnp.bfloat16)
            value_scr[rows, :] = parts[6].astype(jnp.bfloat16)
        for handle in handles:
            handle.wait()
        resid_own_ref[...] = resid_scr[:, pl.ds(pl.multiple_of(rank * width, width), width)]
        for half in range(0, total, 4 * own_rows):
            mix_grad = dot_plain(
                resid_scr[pl.ds(half, 4 * own_rows), :], out_cols_ref[...]
            ).astype(jnp.bfloat16)
            for step in range(4):
                mask = xor_order[half // own_rows + step]
                first = pl.multiple_of((rank ^ mask) * own_rows, own_rows)
                mix_grad_scr[pl.ds(first, own_rows), :] = mix_grad[
                    step * own_rows : (step + 1) * own_rows
                ]
        query_gain = query_gain_ref[...]
        key_gain = key_gain_ref[...]

        def heads_of(rows):
            return rotated_heads(
                raw_ref[rows, :], query_gain, key_gain, cos_ref[rows, :], sin_ref[rows, :],
                head_dim,
            )

        def unrotated(grad, rows):
            return grad * cos_ref[rows, :] - swap_halves(grad, head_dim) * sin_ref[rows, :]

        def norm_back(upstream, hat, norm, gain):
            scaled = upstream * gain
            return norm * (scaled - hat * pair_scale(scaled * hat, head_dim))

        key_sum[...] = jnp.zeros_like(key_sum)
        value_sum[...] = jnp.zeros_like(value_sum)
        query_part = jnp.zeros((1, width), jnp.float32)
        for first in range(0, total, block):
            rows = pl.ds(first, block)
            span = first + block
            stacked = stack_heads(query_scr[rows, :], head_dim)
            stacked_grad = stack_heads(mix_grad_scr[rows, :], head_dim)
            mixed = mix_ref[rows, :].astype(jnp.float32)
            delta = jnp.sum(
                stacked_grad.astype(jnp.float32) * jnp.concatenate([mixed, mixed], axis=0),
                axis=1,
                keepdims=True,
            )
            allowed = allowed_pairs(
                doc_col_ref[rows, :], doc_row_ref[:, :span], first, block, span
            )
            allowed = jnp.concatenate([allowed, allowed], axis=0)
            scores = dot_last(stacked, key_scr[:span, :]) * score_scale
            lse = lse_ref[pl.ds(2 * first, 2 * block), :]
            probs = jnp.exp(jnp.where(allowed, scores - lse, very_low))
            prob_grad = dot_last(stacked_grad, value_scr[:span, :])
            score_grad = (probs * (prob_grad - delta)).astype(jnp.bfloat16)
            rotated = join_heads(dot_plain(score_grad, key_scr[:span, :]), head_dim)
            key_sum[:span, :] += dot_first(score_grad, stacked)
            value_sum[:span, :] += dot_first(probs.astype(jnp.bfloat16), stacked_grad)
            query_hat, query_norm = heads_of(rows)[:2]
            straight = unrotated(rotated * score_scale, rows)
            query_part = query_part + jnp.sum(straight * query_hat, axis=0, keepdims=True)
            grads_ref[rows, :width] = norm_back(
                straight, query_hat, query_norm, query_gain
            ).astype(jnp.bfloat16)
        key_part = jnp.zeros((1, width), jnp.float32)
        for first in range(0, total, block):
            rows = pl.ds(first, block)
            key_hat, key_norm = heads_of(rows)[2:4]
            summed = key_sum[rows, :]
            summed = (summed + pltpu.roll(summed, head_dim, 1)) * score_scale
            values = value_sum[rows, :]
            values = values + pltpu.roll(values, head_dim, 1)
            straight = unrotated(summed, rows)
            key_part = key_part + jnp.sum(straight * key_hat, axis=0, keepdims=True)
            key_grad = norm_back(straight, key_hat, key_norm, key_gain)
            lower = lower_lanes(key_grad.shape, head_dim)
            grads_ref[rows, width:] = jnp.where(lower, key_grad, values).astype(jnp.bfloat16)
        query_part_ref[...] = query_part
        key_part_ref[...] = key_part
        for step, mask in enumerate(xor_order):
            first = pl.multiple_of((rank ^ mask) * own_rows, own_rows)
            grads_out_ref[pl.ds(step * own_rows, own_rows), :] = grads_ref[
                pl.ds(first, own_rows), :
            ]
        for mask, piece_ref in enumerate(piece_refs):
            lanes = pl.ds(pl.multiple_of((rank ^ mask) * width, width), width)
            piece_ref[...] = dot_first(normed_ref[:, lanes], grads_out_ref[...]).astype(
                jnp.bfloat16
            )

    def call(
        places, raw, mix, resids, out_cols, lse, query_gain, key_gain, cosine, sine, doc_col,
        doc_row, normed,
    ):
        total = raw.shape[0]
        return pl.pallas_call(
            kernel,
            name="attention_backward",
            in_specs=[scalar_spec()] + [whole_spec()] * 11 + [any_spec()] * 8,
            compiler_params=pltpu.CompilerParams(vmem_limit_bytes=36 << 20),
            out_shape=(
                jax.ShapeDtypeStruct((total, 2 * width), jnp.bfloat16),
                jax.ShapeDtypeStruct((1, width), jnp.float32),
                jax.ShapeDtypeStruct((1, width), jnp.float32),
                jax.ShapeDtypeStruct((total, width), jnp.bfloat16),
            )
            + (jax.ShapeDtypeStruct((width, 2 * width), jnp.bfloat16),) * 8,
            scratch_shapes=[pltpu.VMEM((total, width), jnp.bfloat16)] * 4
            + [pltpu.VMEM((total, 2 * width), jnp.bfloat16)]
            + [pltpu.VMEM((total, width), jnp.float32)] * 2
            + [pltpu.VMEM((total, normed.shape[1]), jnp.bfloat16), pltpu.SemaphoreType.DMA((8,))],
        )(
            places, raw, mix, out_cols, lse, query_gain, key_gain, cosine, sine, doc_col,
            doc_row, normed, *in_hbm(resids),
        )

    return call


def unpack_heads(places, summed, head_dim):
    rows = summed.shape[0]
    width = 2 * head_dim
    model = 8 * width

    def kernel(place_ref, sum_ref, query_ref, key_ref, value_ref, out_ref):
        shard = place_ref[0]
        core = place_ref[1]
        for step in range(4):
            other = shard ^ step
            first = sum_ref[:, pl.ds(4 * step * width, 2 * width)].astype(jnp.float32)
            second = sum_ref[:, pl.ds((4 * step + 2) * width, 2 * width)].astype(jnp.float32)
            even = jnp.where(core == 0, first, second)
            odd = jnp.where(core == 0, second, first)
            query_ref[:, pl.ds(pl.multiple_of(2 * other * width, width), width)] = even[:, :width]
            query_ref[:, pl.ds(pl.multiple_of((2 * other + 1) * width, width), width)] = odd[
                :, :width
            ]
            even = even[:, width:]
            odd = odd[:, width:]
            lower = lower_lanes(even.shape, head_dim)
            lanes = pl.ds(pl.multiple_of(other * width, width), width)
            key_ref[:, lanes] = jnp.where(lower, even, pltpu.roll(odd, head_dim, 1))
            value_ref[:, lanes] = jnp.where(lower, pltpu.roll(even, head_dim, 1), odd)
        out_ref[...] = sum_ref[:, 2 * model :].astype(jnp.float32)

    return pl.pallas_call(
        kernel,
        name="unpack_heads",
        in_specs=[scalar_spec(), whole_spec()],
        out_shape=(
            jax.ShapeDtypeStruct((rows, model), jnp.float32),
            jax.ShapeDtypeStruct((rows, model // 2), jnp.float32),
            jax.ShapeDtypeStruct((rows, model // 2), jnp.float32),
            jax.ShapeDtypeStruct((rows, summed.shape[1] - 2 * model), jnp.float32),
        ),
    )(places, summed)


def local_by_heads(
    tokens_in,
    doc_lengths,
    attn_gain,
    w_query,
    key_weight,
    value_weight,
    w_output,
    query_norm_gain,
    key_norm_gain,
    mlp_gain,
    w_gate,
    w_up,
    w_down,
    out_grad,
):
    row_count, model_width = tokens_in.shape
    head_dim = query_norm_gain.shape[0]
    pair_width = 2 * head_dim
    total = row_count * 8
    half_rows = total // 2
    block = 256
    core = lax.axis_index("seq")
    shard = lax.axis_index("shard")
    rank = shard * 2 + core
    places = jnp.stack([shard, core]).astype(jnp.int32)

    x_near = gather_near(tokens_in)
    head_pieces = pack_heads(w_query, key_weight, value_weight, places, head_dim)
    head_pieces = [head_pieces[0]] + [
        group_swap(head_pieces[step], 2 * step) for step in (1, 2, 3)
    ]
    x_far = gather_far(x_near)
    x_pieces = x_near + x_far

    out_near = lax.dynamic_slice_in_dim(w_output, core * row_count, row_count)
    out_local = lax.dynamic_slice_in_dim(w_output, (1 - core) * row_count, row_count)
    out_near = gather_near(after(out_near, x_near[1:]))
    out_pieces = out_near + [out_local] + gather_far(out_near[1:])

    index = jnp.arange(total, dtype=jnp.int32)
    docs, offsets = doc_info(doc_lengths[0], index)
    half_dim = head_dim // 2
    inverse_freq = rope_base ** (-(jnp.arange(half_dim, dtype=jnp.float32) * 2.0 / head_dim))
    angles = offsets.astype(jnp.float32)[:, None] * inverse_freq[None, :]
    cosine = jnp.cos(angles)
    sine = jnp.sin(angles)
    cosine = jnp.concatenate([cosine] * 4, axis=1)
    sine = jnp.concatenate([-sine, sine, -sine, sine], axis=1)
    doc_column = docs[:, None]
    doc_row = docs[None, :]
    query_gain = jnp.concatenate([query_norm_gain] * 2)[None, :]
    key_gain = jnp.concatenate([key_norm_gain] * 2)[None, :]

    mix, normed, raw, lse, head_weight = attention_forward(head_dim, block)(
        places, x_pieces, attn_gain[None, :], head_pieces, query_gain, key_gain, cosine, sine,
        doc_column, doc_row,
    )
    mix_near = gather_near(mix)
    mix_far = gather_far(mix_near)
    grad_near = gather_near(after(out_grad, mix_near[1:]))
    grad_all = stack_rows(grad_near + gather_far(grad_near))

    normed_mid, mix_all, out_cols, own_resid, own_hat, own_scale = residual_stage(
        places, mix_near + mix_far, out_pieces, x_pieces, mlp_gain[None, :]
    )

    hidden_rows = w_gate.shape[0] // 2

    def own_rows(weight):
        return lax.dynamic_slice_in_dim(weight, core * hidden_rows, hidden_rows)

    gate_rows = own_rows(w_gate)
    up_rows = own_rows(w_up)
    down_rows = own_rows(w_down)
    gate = dot_last(normed_mid, gate_rows)
    up = dot_last(normed_mid, up_rows)
    grad_hidden = dot_last(grad_all, down_rows)
    gate_sig = jax.nn.sigmoid(gate)
    hidden = (gate * gate_sig * up).astype(jnp.bfloat16)
    gate_grad = (grad_hidden * up * gate_sig * (1.0 + gate * (1.0 - gate_sig))).astype(jnp.bfloat16)
    up_grad = (grad_hidden * gate * gate_sig).astype(jnp.bfloat16)

    def mid_part(first):
        rows = slice(first, first + half_rows)
        return dot_plain(gate_grad[rows], gate_rows) + dot_plain(up_grad[rows], up_rows)

    grad_mid = scatter_sum(mid_part(0), mid_part(half_rows))
    grad_resid = out_grad.astype(jnp.float32) + root_mean_backward(
        own_hat, own_scale, mlp_gain, grad_mid
    )
    mlp_gain_part = jnp.sum(grad_mid * own_hat, axis=0)
    resid_near = gather_near(grad_resid.astype(jnp.bfloat16))
    resid_pieces = resid_near + gather_far(resid_near)

    mlp_grads = jnp.concatenate(
        [
            dot_first(hidden, grad_all).astype(jnp.bfloat16),
            dot_first(gate_grad, normed_mid).astype(jnp.bfloat16),
            dot_first(up_grad, normed_mid).astype(jnp.bfloat16),
        ],
        axis=0,
    )
    mlp_sums = lax.psum(mlp_grads, "rep").astype(jnp.float32)

    act_out = own_resid + scatter_sum(
        dot_plain(hidden[:half_rows], down_rows), dot_plain(hidden[half_rows:], down_rows)
    )

    backward = attention_backward(head_dim, block)(
        places, raw, mix, resid_pieces, out_cols, lse, query_gain, key_gain, cosine, sine,
        doc_column, doc_row, normed,
    )
    head_grads, query_part, key_part, resid_own = backward[:4]
    weight_pieces = backward[4:]
    weight_pieces = [weight_pieces[0]] + [
        group_swap(weight_pieces[mask], mask) for mask in range(1, 8)
    ]
    out_grads = dot_first(resid_own, mix_all).astype(jnp.bfloat16)
    attn_grads = rep_halving_sum(jnp.concatenate(weight_pieces + [out_grads], axis=1))
    grad_query, grad_key, grad_value, grad_output = unpack_heads(places, attn_grads, head_dim)

    grad_in_norm = scatter_sum(
        dot_last(head_grads[:half_rows], head_weight),
        dot_last(head_grads[half_rows:], head_weight),
    )
    own_x = tokens_in.astype(jnp.float32)
    own_norm = rms_scale(own_x)
    x_hat = own_x * own_norm
    in_grad = grad_resid + root_mean_backward(x_hat, own_norm, attn_gain, grad_in_norm)
    attn_gain_part = jnp.sum(grad_in_norm * x_hat, axis=0)
    query_gain_part = query_part[0, :head_dim] + query_part[0, head_dim:]
    gains = sum_everywhere(
        jnp.concatenate(
            [attn_gain_part, mlp_gain_part, query_gain_part, key_part[0, :head_dim]]
        )[None, :]
    )[0]
    return (
        act_out,
        in_grad,
        gains[:model_width],
        grad_query,
        grad_key,
        grad_value,
        grad_output,
        gains[2 * model_width : 2 * model_width + head_dim],
        gains[2 * model_width + head_dim :],
        gains[model_width : 2 * model_width],
        mlp_sums[hidden_rows : 2 * hidden_rows],
        mlp_sums[2 * hidden_rows :],
        mlp_sums[:hidden_rows],
    )


def solution(mesh):
    placed = (
        P(("rep", "shard", "seq"), None),
        P("rep", None),
        P(),
        P("shard", None),
        P("shard", None),
        P("shard", None),
        P("shard", None),
        P(),
        P(),
        P(),
        P("shard", None),
        P("shard", None),
        P("shard", None),
        P(("rep", "shard", "seq"), None),
    )
    sizes = dict(mesh.shape)
    by_heads = sizes["rep"] == 4 and sizes["shard"] == 4 and sizes["seq"] == 2
    return jax.shard_map(
        local_by_heads if by_heads else local,
        mesh=mesh,
        in_specs=placed,
        out_specs=(
            P(("rep", "shard", "seq"), None),
            P(("rep", "shard", "seq"), None),
            P(),
            P(("shard", "seq"), None),
            P(("shard", "seq"), None),
            P(("shard", "seq"), None),
            P(("shard", "seq"), None),
            P(),
            P(),
            P(),
            P(("shard", "seq"), None),
            P(("shard", "seq"), None),
            P(("shard", "seq"), None),
        ),
        check_vma=False,
    )
```

```python
import math

import jax
import jax.numpy as jnp
from jax import lax
from jax.experimental import pallas as pl
from jax.experimental.pallas import tpu as pltpu
from jax.sharding import PartitionSpec as P

norm_eps = 1e-05
rope_base = 1000000.0
very_low = -1e30
contract_last = (((1,), (1,)), ((), ()))
contract_first = (((0,), (0,)), ((), ()))


def rms_scale(values):
    return lax.rsqrt(jnp.mean(values * values, axis=-1, keepdims=True) + norm_eps)


def root_mean_backward(normed, factor, gain, upstream):
    scaled = upstream * gain
    return factor * (scaled - normed * jnp.mean(scaled * normed, axis=-1, keepdims=True))


def rope_tables(positions, head_dim):
    half_dim = head_dim // 2
    inverse_freq = rope_base ** (-(jnp.arange(half_dim, dtype=jnp.float32) * 2.0 / head_dim))
    angles = positions.astype(jnp.float32)[:, None] * inverse_freq[None, :]
    return (jnp.cos(angles)[:, None, :], jnp.sin(angles)[:, None, :])


def rotate_pairs(values, cosine_table, sine_values):
    half_dim = values.shape[-1] // 2
    lower_half = values[..., :half_dim]
    upper_half = values[..., half_dim:]
    return jnp.concatenate(
        [
            lower_half * cosine_table - upper_half * sine_values,
            upper_half * cosine_table + lower_half * sine_values,
        ],
        axis=-1,
    )


def rotate_back(grads, cosine_table, sine_values):
    half_dim = grads.shape[-1] // 2
    lower_half = grads[..., :half_dim]
    upper_half = grads[..., half_dim:]
    return jnp.concatenate(
        [
            lower_half * cosine_table + upper_half * sine_values,
            upper_half * cosine_table - lower_half * sine_values,
        ],
        axis=-1,
    )


def doc_info(lengths, positions):
    doc_ends = jnp.cumsum(lengths)
    finished = doc_ends[None, :] <= positions[:, None]
    doc_ids = jnp.sum(finished.astype(jnp.int32), axis=1)
    doc_first = jnp.sum(jnp.where(finished, lengths[None, :], 0), axis=1)
    return (doc_ids, positions - doc_first)


def local(
    tokens_in,
    doc_lengths,
    attn_gain,
    w_query,
    key_weight,
    value_weight,
    w_output,
    query_norm_gain,
    key_norm_gain,
    mlp_gain,
    w_gate,
    w_up,
    w_down,
    out_grad,
):
    row_count = tokens_in.shape[0]
    model_width = tokens_in.shape[1]
    head_dim = query_norm_gain.shape[0]
    query_width = w_query.shape[1]
    kv_width = key_weight.shape[1]
    kv_heads = kv_width // head_dim
    head_grouping = query_width // kv_width
    score_scale = head_dim ** (-0.5)
    rank_count = lax.axis_size("shard") * lax.axis_size("seq")
    group_rows = row_count * rank_count
    first_row = lax.axis_index(("shard", "seq")) * row_count
    key_block = min(512, group_rows)
    block_count = group_rows // key_block
    key_index = jnp.arange(group_rows, dtype=jnp.int32)
    key_docs, key_offset = doc_info(doc_lengths[0], key_index)
    query_index = first_row + jnp.arange(row_count, dtype=jnp.int32)
    query_docs = lax.dynamic_slice_in_dim(key_docs, first_row, row_count)
    query_offset = lax.dynamic_slice_in_dim(key_offset, first_row, row_count)
    cosine_table, sine_values = rope_tables(query_offset, head_dim)
    x_float = tokens_in.astype(jnp.float32)
    norm_one = rms_scale(x_float)
    x_hat = x_float * norm_one
    normalized_input = (x_hat * attn_gain).astype(jnp.bfloat16)
    pieces = (
        lax.all_gather(w_query, "shard", axis=0, tiled=True),
        lax.all_gather(key_weight, "shard", axis=0, tiled=True),
        lax.all_gather(value_weight, "shard", axis=0, tiled=True),
    )
    in_cols = normalized_input
    queries, key_proj, value_proj = tuple(
        (jnp.dot(in_cols, weight, preferred_element_type=jnp.float32) for weight in pieces)
    )
    query_heads = queries.reshape(row_count, query_width // head_dim, head_dim)
    query_norm = rms_scale(query_heads)
    query_normalized = query_heads * query_norm
    query_rotated = rotate_pairs(
        query_normalized * query_norm_gain, cosine_table, sine_values
    ).astype(jnp.bfloat16)
    key_head_rows = key_proj.reshape(row_count, kv_heads, head_dim)
    key_head_norm = rms_scale(key_head_rows)
    key_normalized = key_head_rows * key_head_norm
    key_rot = rotate_pairs(key_normalized * key_norm_gain, cosine_table, sine_values).astype(
        jnp.bfloat16
    )
    value_rows = value_proj.astype(jnp.bfloat16)
    key_all, value_all = (
        lax.all_gather(key_rot.reshape(row_count, kv_width), ("shard", "seq"), axis=0, tiled=True),
        lax.all_gather(value_rows, ("shard", "seq"), axis=0, tiled=True),
    )
    query_grouped = query_rotated.reshape(row_count, kv_heads, head_grouping, head_dim)

    def block_mask(offset, span_rows):
        docs_here = lax.dynamic_slice_in_dim(key_docs, offset, span_rows)
        index_here = offset + jnp.arange(span_rows, dtype=jnp.int32)
        return (query_docs[:, None] == docs_here[None, :]) & (
            index_here[None, :] <= query_index[:, None]
        )

    def block_scores(offset, span_rows, allowed):
        key_rows = lax.dynamic_slice_in_dim(key_all, offset, span_rows, 0).reshape(
            span_rows, kv_heads, head_dim
        )
        value_block = lax.dynamic_slice_in_dim(value_all, offset, span_rows, 0).reshape(
            span_rows, kv_heads, head_dim
        )
        scores = (
            jnp.einsum(
                "tgjd,rgd->gjtr", query_grouped, key_rows, preferred_element_type=jnp.float32
            )
            * score_scale
        )
        return (jnp.where(allowed, scores, very_low), key_rows, value_block)

    def total_block(block_index, running):
        offset = block_index * key_block
        allowed = block_mask(offset, key_block)

        def total_accumulate(softmax_state):
            row_high, row_total = softmax_state
            scores, _, _ = block_scores(offset, key_block, allowed)
            new_high = jnp.maximum(row_high, jnp.max(scores, axis=-1))
            exp_scores = jnp.where(allowed, jnp.exp(scores - new_high[..., None]), 0.0)
            row_total = row_total * jnp.exp(row_high - new_high) + jnp.sum(exp_scores, axis=-1)
            return (new_high, row_total)

        return lax.cond(
            jnp.any(allowed), total_accumulate, lambda softmax_state: softmax_state, running
        )

    softmax_init = (
        jnp.full((kv_heads, head_grouping, row_count), very_low, jnp.float32),
        jnp.zeros((kv_heads, head_grouping, row_count), jnp.float32),
    )
    row_high, row_total = lax.fori_loop(0, block_count, total_block, softmax_init)
    log_total = row_high + jnp.log(row_total)

    def mix_block(block_index, weighted):
        offset = block_index * key_block
        allowed = block_mask(offset, key_block)

        def mix_accumulate(current):
            scores, _, value_block = block_scores(offset, key_block, allowed)
            attn_prob = jnp.where(allowed, jnp.exp(scores - log_total[..., None]), 0.0).astype(
                jnp.bfloat16
            )
            return current + jnp.einsum(
                "gjtr,rgd->gjtd", attn_prob, value_block, preferred_element_type=jnp.float32
            )

        return lax.cond(jnp.any(allowed), mix_accumulate, lambda current: current, weighted)

    weighted = lax.fori_loop(
        0,
        block_count,
        mix_block,
        jnp.zeros((kv_heads, head_grouping, row_count, head_dim), jnp.float32),
    )
    head_mixture = (
        weighted.transpose(2, 0, 1, 3).reshape(row_count, query_width).astype(jnp.bfloat16)
    )
    attn_part = lax.dot_general(
        head_mixture,
        lax.all_gather(w_output, "shard", axis=0, tiled=True),
        contract_last,
        preferred_element_type=jnp.float32,
    )
    residual = x_float + attn_part
    norm_two = rms_scale(residual)
    resid_hat = residual * norm_two
    normed_mid = (resid_hat * mlp_gain).astype(jnp.bfloat16)
    gate_rows = lax.all_gather(w_gate, "shard", axis=0, tiled=True)
    up_rows = lax.all_gather(w_up, "shard", axis=0, tiled=True)
    down_rows = lax.all_gather(w_down, "shard", axis=0, tiled=True)
    gate_part = lax.dot_general(
        normed_mid, gate_rows, contract_last, preferred_element_type=jnp.float32
    )
    up_part = lax.dot_general(
        normed_mid, up_rows, contract_last, preferred_element_type=jnp.float32
    )
    hidden_part = (gate_part * jax.nn.sigmoid(gate_part) * up_part).astype(jnp.bfloat16)
    mlp_sum = jnp.dot(hidden_part, down_rows, preferred_element_type=jnp.float32)
    mlp_gate_store = gate_part
    mlp_up_store = up_part
    hidden_store = hidden_part
    mlp_sum, gate_store, up_store, hidden_store = (
        mlp_sum,
        mlp_gate_store,
        mlp_up_store,
        hidden_store,
    )
    act_out = residual + mlp_sum
    grad_float = out_grad.astype(jnp.float32)
    gate_rows = lax.all_gather(w_gate, "shard", axis=0, tiled=True)
    up_rows = lax.all_gather(w_up, "shard", axis=0, tiled=True)
    down_rows = lax.all_gather(w_down, "shard", axis=0, tiled=True)
    gate_part = gate_store
    up_part = up_store
    grad_hidden = lax.dot_general(
        out_grad, down_rows, contract_last, preferred_element_type=jnp.float32
    )
    gate_sig = jax.nn.sigmoid(gate_part)
    gate_grad = (grad_hidden * up_part * gate_sig * (1.0 + gate_part * (1.0 - gate_sig))).astype(
        jnp.bfloat16
    )
    up_grad = (grad_hidden * gate_part * gate_sig).astype(jnp.bfloat16)
    grad_mid = jnp.dot(gate_grad, gate_rows, preferred_element_type=jnp.float32) + jnp.dot(
        up_grad, up_rows, preferred_element_type=jnp.float32
    )
    gate_grad_store = gate_grad
    up_grad_store = up_grad
    grad_mid, gate_grad_store, up_grad_store = (grad_mid, gate_grad_store, up_grad_store)
    grad_resid = grad_float + root_mean_backward(resid_hat, norm_two, mlp_gain, grad_mid)
    mlp_gain_part = jnp.sum(grad_mid * resid_hat, axis=0)
    grad_resid_b = grad_resid.astype(jnp.bfloat16)
    resid_cols = grad_resid_b
    mixing_gradient = jnp.dot(
        resid_cols,
        lax.all_gather(w_output, "shard", axis=0, tiled=True),
        preferred_element_type=jnp.float32,
    ).astype(jnp.bfloat16)
    mix_grouped = mixing_gradient.reshape(row_count, kv_heads, head_grouping, head_dim)
    delta_row_values = jnp.sum(
        (mixing_gradient.astype(jnp.float32) * head_mixture.astype(jnp.float32)).reshape(
            row_count, kv_heads, head_grouping, head_dim
        ),
        axis=-1,
    ).transpose(1, 2, 0)

    def score_grads(offset, span_rows, allowed):
        scores, key_rows, value_block = block_scores(offset, span_rows, allowed)
        attn_prob = jnp.where(allowed, jnp.exp(scores - log_total[..., None]), 0.0)
        grad_prob = jnp.einsum(
            "tgjd,rgd->gjtr", mix_grouped, value_block, preferred_element_type=jnp.float32
        )
        grad_score = (attn_prob * (grad_prob - delta_row_values[..., None])).astype(jnp.bfloat16)
        return (attn_prob, grad_score, key_rows)

    def query_pass(block_index, grad_sum):
        offset = block_index * key_block
        allowed = block_mask(offset, key_block)

        def query_accumulate(current):
            _, grad_score, key_rows = score_grads(offset, key_block, allowed)
            return current + score_scale * jnp.einsum(
                "gjtr,rgd->tgjd", grad_score, key_rows, preferred_element_type=jnp.float32
            )

        return lax.cond(jnp.any(allowed), query_accumulate, lambda current: current, grad_sum)

    query_rot_grad = lax.fori_loop(
        0,
        block_count,
        query_pass,
        jnp.zeros((row_count, kv_heads, head_grouping, head_dim), jnp.float32),
    )

    def one_block(start_row):
        allowed = block_mask(start_row, key_block)

        def compute(unused):
            attn_prob, grad_score, _ = score_grads(start_row, key_block, allowed)
            key_grad = score_scale * jnp.einsum(
                "gjtr,tgjd->rgd", grad_score, query_grouped, preferred_element_type=jnp.float32
            )
            value_grad = jnp.einsum(
                "gjtr,tgjd->rgd",
                attn_prob.astype(jnp.bfloat16),
                mix_grouped,
                preferred_element_type=jnp.float32,
            )
            return jnp.concatenate(
                [key_grad.reshape(key_block, kv_width), value_grad.reshape(key_block, kv_width)],
                axis=1,
            )

        return lax.cond(
            jnp.any(allowed),
            compute,
            lambda unused: jnp.zeros((key_block, 2 * kv_width), jnp.float32),
            0,
        )

    starts = key_block * jnp.arange(
        row_count * lax.axis_size(("shard", "seq")) // key_block, dtype=jnp.int32
    )
    kv_summed = lax.psum_scatter(
        lax.map(one_block, starts).reshape(
            row_count * lax.axis_size(("shard", "seq")), 2 * kv_width
        ),
        ("shard", "seq"),
        scatter_dimension=0,
        tiled=True,
    )
    key_rot_grad = kv_summed[:, :kv_width].reshape(row_count, kv_heads, head_dim)
    value_grad_b = kv_summed[:, kv_width:].astype(jnp.bfloat16)
    key_unrotated = rotate_back(key_rot_grad, cosine_table, sine_values)
    key_gain_part = jnp.sum(key_unrotated * key_normalized, axis=(0, 1))
    key_row_gradient = (
        root_mean_backward(key_normalized, key_head_norm, key_norm_gain, key_unrotated)
        .reshape(row_count, kv_width)
        .astype(jnp.bfloat16)
    )
    query_unrot = rotate_back(
        query_rot_grad.reshape(row_count, query_width // head_dim, head_dim),
        cosine_table,
        sine_values,
    )
    query_gain_part = jnp.sum(query_unrot * query_normalized, axis=(0, 1))
    grad_query_rows = (
        root_mean_backward(query_normalized, query_norm, query_norm_gain, query_unrot)
        .reshape(row_count, query_width)
        .astype(jnp.bfloat16)
    )
    query_rows, key_rows, value_rows_w = lax.all_gather(
        (w_query, key_weight, value_weight), "shard", axis=0, tiled=True
    )
    grad_in_norm = (
        lax.dot_general(
            grad_query_rows, query_rows, contract_last, preferred_element_type=jnp.float32
        )
        + lax.dot_general(
            key_row_gradient, key_rows, contract_last, preferred_element_type=jnp.float32
        )
        + lax.dot_general(
            value_grad_b, value_rows_w, contract_last, preferred_element_type=jnp.float32
        )
    )
    in_grad = grad_resid + root_mean_backward(x_hat, norm_one, attn_gain, grad_in_norm)
    attn_gain_part = jnp.sum(grad_in_norm * x_hat, axis=0)
    grad_attn_gain, grad_mlp_gain, grad_query_gain, grad_key_gain = lax.psum(
        (attn_gain_part, mlp_gain_part, query_gain_part, key_gain_part), ("rep", "shard", "seq")
    )
    attn_grads = jnp.concatenate([grad_query_rows, key_row_gradient, value_grad_b], axis=1)
    d_share = model_width // rank_count
    in_own, resid_own, gate_own, up_own, hidden_own = (
        lax.all_to_all(normalized_input, ("shard", "seq"), split_axis=1, concat_axis=0, tiled=True),
        lax.all_to_all(grad_resid_b, ("shard", "seq"), split_axis=1, concat_axis=0, tiled=True),
        lax.all_to_all(gate_grad_store, ("shard", "seq"), split_axis=1, concat_axis=0, tiled=True),
        lax.all_to_all(up_grad_store, ("shard", "seq"), split_axis=1, concat_axis=0, tiled=True),
        lax.all_to_all(hidden_store, ("shard", "seq"), split_axis=1, concat_axis=0, tiled=True),
    )
    attn_piece = lax.all_gather(attn_grads, ("shard", "seq"), axis=0, tiled=True)
    mix_piece = lax.all_gather(head_mixture, ("shard", "seq"), axis=0, tiled=True)
    mid_piece = lax.all_gather(normed_mid, ("shard", "seq"), axis=0, tiled=True)
    grad_piece = lax.all_gather(out_grad, ("shard", "seq"), axis=0, tiled=True)
    in_cols = in_own
    resid_cols = resid_own
    attn_rows = jnp.concatenate(
        [
            lax.dot_general(
                in_cols, attn_piece, contract_first, preferred_element_type=jnp.float32
            ),
            lax.dot_general(
                resid_cols, mix_piece, contract_first, preferred_element_type=jnp.float32
            ),
        ],
        axis=1,
    )
    mlp_rows = jnp.concatenate(
        [
            lax.dot_general(
                gate_own, mid_piece, contract_first, preferred_element_type=jnp.float32
            ),
            lax.dot_general(up_own, mid_piece, contract_first, preferred_element_type=jnp.float32),
            lax.dot_general(
                hidden_own, grad_piece, contract_first, preferred_element_type=jnp.float32
            ),
        ],
        axis=1,
    )
    group_grads = jnp.concatenate([attn_rows, mlp_rows], axis=0)
    own_grads = lax.psum(group_grads, "rep")
    attn_block_grads = own_grads[:d_share]
    mlp_block_grads = own_grads[d_share:]
    grad_query = attn_block_grads[:, :query_width]
    grad_key = attn_block_grads[:, query_width : query_width + kv_width]
    grad_value = attn_block_grads[:, query_width + kv_width : query_width + 2 * kv_width]
    grad_output = attn_block_grads[:, query_width + 2 * kv_width :]
    grad_gate = mlp_block_grads[:, :model_width]
    grad_up = mlp_block_grads[:, model_width : 2 * model_width]
    grad_down = mlp_block_grads[:, 2 * model_width :]
    return (
        act_out,
        in_grad,
        grad_attn_gain,
        grad_query,
        grad_key,
        grad_value,
        grad_output,
        grad_query_gain,
        grad_key_gain,
        grad_mlp_gain,
        grad_gate,
        grad_up,
        grad_down,
    )


group_axes = ("shard", "seq")


def group_swap(values, mask):
    return lax.ppermute(values, group_axes, [(rank, rank ^ mask) for rank in range(8)])


def rep_swap(values, mask):
    return lax.ppermute(values, "rep", [(rank, rank ^ mask) for rank in range(4)])


xor_order = (0, 2, 4, 6, 1, 3, 5, 7)


def gather_near(own):
    return [own] + [group_swap(own, mask) for mask in (2, 4, 6)]


def gather_far(near):
    return [group_swap(piece, 1) for piece in near]


def after(values, marker):
    return lax.optimization_barrier((values, marker))[0]


def add_rounded(left, right):
    return (left.astype(jnp.float32) + right.astype(jnp.float32)).astype(jnp.bfloat16)


def scatter_sum(near_part, far_part):
    swapped = group_swap(far_part.astype(jnp.bfloat16), 1)
    width = near_part.shape[0] // 4
    halves = [
        near_part[at : at + width] + swapped[at : at + width].astype(jnp.float32)
        for at in range(0, 4 * width, width)
    ]
    total = halves[0]
    moved = [
        group_swap(half.astype(jnp.bfloat16), mask) for mask, half in zip((2, 4, 6), halves[1:])
    ]
    for piece in moved:
        total = total + piece.astype(jnp.float32)
    return total


def rep_halving_sum(values, first_marker, second_marker):
    place = lax.axis_index("rep")
    low = place % 2
    high = place // 2
    half = values.shape[0] // 2
    quarter = half // 2
    kept = lax.dynamic_slice_in_dim(values, low * half, half)
    sent = lax.dynamic_slice_in_dim(values, (1 - low) * half, half)
    part = add_rounded(*after((kept, rep_swap(sent, 1)), first_marker))
    kept = lax.dynamic_slice_in_dim(part, high * quarter, quarter)
    sent = lax.dynamic_slice_in_dim(part, (1 - high) * quarter, quarter)
    part = add_rounded(*after((kept, rep_swap(sent, 2)), second_marker))
    other = rep_swap(part, 2)
    part = jnp.where(
        high == 0, jnp.concatenate([part, other]), jnp.concatenate([other, part])
    )
    other = rep_swap(part, 1)
    return jnp.where(low == 0, jnp.concatenate([part, other]), jnp.concatenate([other, part]))


def sum_everywhere(values):
    for mask in (1, 2, 4):
        values = values + group_swap(values, mask)
    for mask in (1, 2):
        values = values + rep_swap(values, mask)
    return values


def lower_lanes(shape, width):
    return lax.broadcasted_iota(jnp.int32, shape, 1) % (2 * width) < width


def pair_scale(values, head_dim):
    lower = lower_lanes(values.shape, head_dim)
    low = jnp.sum(jnp.where(lower, values, 0.0), axis=1, keepdims=True)
    high = jnp.sum(jnp.where(lower, 0.0, values), axis=1, keepdims=True)
    return jnp.where(lower, low, high) * (1.0 / head_dim)


def swap_halves(values, head_dim):
    width = values.shape[1]
    half = head_dim // 2
    return jnp.where(
        lower_lanes(values.shape, half),
        pltpu.roll(values, width - half, 1),
        pltpu.roll(values, half, 1),
    )


def rotated_heads(raw, query_gain, key_gain, cosine, sine, head_dim):
    width = 2 * head_dim
    queries = raw[:, :width]
    keys = raw[:, width:]
    query_norm = lax.rsqrt(pair_scale(queries * queries, head_dim) + norm_eps)
    key_norm = lax.rsqrt(pair_scale(keys * keys, head_dim) + norm_eps)
    query_hat = queries * query_norm
    key_hat = keys * key_norm
    scaled = query_hat * query_gain
    query_rot = scaled * cosine + swap_halves(scaled, head_dim) * sine
    scaled = key_hat * key_gain
    key_rot = scaled * cosine + swap_halves(scaled, head_dim) * sine
    lower = lower_lanes(keys.shape, head_dim)
    key_twice = jnp.where(lower, key_rot, pltpu.roll(key_rot, head_dim, 1))
    value_twice = jnp.where(lower, pltpu.roll(keys, head_dim, 1), keys)
    return query_hat, query_norm, key_hat, key_norm, query_rot, key_twice, value_twice


def stack_heads(values, head_dim):
    lower = lower_lanes(values.shape, head_dim)
    zero = jnp.zeros_like(values)
    return jnp.concatenate(
        [jnp.where(lower, values, zero), jnp.where(lower, zero, values)], axis=0
    )


def join_heads(stacked, head_dim):
    rows = stacked.shape[0] // 2
    lower = lower_lanes((rows, stacked.shape[1]), head_dim)
    return jnp.where(lower, stacked[:rows], stacked[rows:])


def allowed_pairs(doc_column, doc_row, first, rows, span):
    row_index = first + lax.broadcasted_iota(jnp.int32, (rows, span), 0)
    key_index = lax.broadcasted_iota(jnp.int32, (rows, span), 1)
    return (doc_column == doc_row) & (key_index <= row_index)


def dot_last(left, right):
    return lax.dot_general(left, right, contract_last, preferred_element_type=jnp.float32)


def dot_first(left, right):
    return lax.dot_general(left, right, contract_first, preferred_element_type=jnp.float32)


def dot_plain(left, right):
    return jnp.dot(left, right, preferred_element_type=jnp.float32)


def scalar_spec():
    return pl.BlockSpec(memory_space=pltpu.SMEM)


def whole_spec():
    return pl.BlockSpec(memory_space=pltpu.VMEM)


def any_spec():
    return pl.BlockSpec(memory_space=pltpu.HBM)


def in_hbm(values):
    return [pltpu.with_memory_space_constraint(value, pltpu.HBM) for value in values]


def start_copies(copies, sems, first=0):
    handles = [
        pltpu.make_async_copy(source, target, sems.at[first + at])
        for at, (source, target) in enumerate(copies)
    ]
    for handle in handles:
        handle.start()
    return handles


def pack_heads(w_query, key_weight, value_weight, places, head_dim):
    rows = w_query.shape[0]
    width = 2 * head_dim

    def kernel(place_ref, query_ref, key_ref, value_ref, *out_refs):
        shard = place_ref[0]
        core = place_ref[1]
        for step, out_ref in enumerate(out_refs):
            other = shard ^ step
            out_ref[:, :width] = query_ref[
                :, pl.ds(pl.multiple_of((2 * other + core) * width, width), width)
            ]
            lanes = pl.ds(pl.multiple_of(other * width, width), width)
            keys = key_ref[:, lanes].astype(jnp.float32)
            values = value_ref[:, lanes].astype(jnp.float32)
            lower = lower_lanes(keys.shape, head_dim)
            first = jnp.where(lower, keys, pltpu.roll(values, head_dim, 1))
            second = jnp.where(lower, pltpu.roll(keys, head_dim, 1), values)
            out_ref[:, width:] = jnp.where(core == 0, first, second).astype(jnp.bfloat16)

    return pl.pallas_call(
        kernel,
        name="pack_heads",
        in_specs=[scalar_spec()] + [whole_spec()] * 3,
        out_shape=(jax.ShapeDtypeStruct((rows, 2 * width), jnp.bfloat16),) * 4,
    )(places, w_query, key_weight, value_weight)


def attention_forward(head_dim, block):
    score_scale = head_dim ** (-0.5)
    assert score_scale == 2.0 ** round(math.log2(score_scale))
    width = 2 * head_dim

    def kernel(
        place_ref, gain_ref, piece_0, piece_1, piece_2, piece_3, query_gain_ref,
        key_gain_ref, cos_hbm, sin_hbm, doc_col_hbm, doc_row_ref, *refs,
    ):
        x_refs = refs[:8]
        mix_ref, normed_out, raw_out, lse_out, weight_out = refs[8:13]
        query_scr, key_scr, value_scr, x_scr, sems = refs[13:18]
        cos_ref, sin_ref, doc_col_ref, normed_ref, raw_ref, lse_ref, weight_ref = refs[18:]
        total = cos_ref.shape[0]
        shard = place_ref[0]
        rank = 2 * shard + place_ref[1]
        piece_rows = piece_0.shape[0]
        own_rows = total // 8
        copies = []
        for step, piece in enumerate((piece_0, piece_1, piece_2, piece_3)):
            first = pl.multiple_of((shard ^ step) * piece_rows, piece_rows)
            copies.append((piece, weight_ref.at[pl.ds(first, piece_rows), :]))
        for step, x_ref in enumerate(x_refs):
            copies.append((x_ref, x_scr.at[pl.ds(step * own_rows, own_rows), :]))
        copies += [(cos_hbm, cos_ref), (sin_hbm, sin_ref), (doc_col_hbm, doc_col_ref)]
        handles = start_copies(copies, sems)
        for handle in handles:
            handle.wait()
        outward = start_copies([(weight_ref, weight_out)], sems, len(copies))

        def normalize(step, carry):
            rows = pl.ds(pl.multiple_of(step * own_rows, own_rows), own_rows)
            x = x_scr[rows, :].astype(jnp.float32)
            normed_ref[rows, :] = (x * rms_scale(x) * gain_ref[...]).astype(jnp.bfloat16)
            return carry

        lax.fori_loop(0, 8, normalize, 0)
        for half in range(0, total, 4 * own_rows):
            raw = dot_plain(normed_ref[pl.ds(half, 4 * own_rows), :], weight_ref[...])
            for step in range(4):
                mask = xor_order[half // own_rows + step]
                first = pl.multiple_of((rank ^ mask) * own_rows, own_rows)
                raw_ref[pl.ds(first, own_rows), :] = raw[step * own_rows : (step + 1) * own_rows]
        outward += start_copies(
            [(normed_ref, normed_out), (raw_ref, raw_out)], sems, len(copies) + 1
        )

        def rotate(step, carry):
            rows = pl.ds(pl.multiple_of(step * block, block), block)
            parts = rotated_heads(
                raw_ref[rows, :], query_gain_ref[...], key_gain_ref[...], cos_ref[rows, :],
                sin_ref[rows, :], head_dim,
            )
            query_scr[rows, :] = (parts[4].astype(jnp.bfloat16) * score_scale).astype(jnp.bfloat16)
            key_scr[rows, :] = parts[5].astype(jnp.bfloat16)
            value_scr[rows, :] = parts[6].astype(jnp.bfloat16)
            return carry

        lax.fori_loop(0, total // block, rotate, 0)
        for first in range(0, total, block):
            rows = pl.ds(first, block)
            span = first + block
            stacked = stack_heads(query_scr[rows, :], head_dim)
            allowed = allowed_pairs(
                doc_col_ref[rows, :], doc_row_ref[:, :span], first, block, span
            )
            allowed = jnp.concatenate([allowed, allowed], axis=0)
            scores = dot_last(stacked, key_scr[:span, :])
            powers = jnp.exp(jnp.where(allowed, scores, very_low))
            row_total = jnp.sum(powers, axis=1, keepdims=True)
            probs = (powers * (1.0 / row_total)).astype(jnp.bfloat16)
            mixed = dot_plain(probs, value_scr[:span, :])
            mix_ref[rows, :] = join_heads(mixed, head_dim).astype(jnp.bfloat16)
            lse_ref[pl.ds(2 * first, 2 * block), :] = jnp.log(row_total)
        outward += start_copies([(lse_ref, lse_out)], sems, len(copies) + 3)
        for handle in outward:
            handle.wait()

    def call(places, xs, gain, pieces, query_gain, key_gain, cosine, sine, doc_column, doc_row):
        total, model = cosine.shape[0], xs[0].shape[1]
        return pl.pallas_call(
            kernel,
            name="attention_forward",
            in_specs=[scalar_spec(), whole_spec()]
            + [any_spec()] * 4
            + [whole_spec()] * 2
            + [any_spec()] * 3
            + [whole_spec()]
            + [any_spec()] * 8,
            out_specs=(whole_spec(),) + (any_spec(),) * 4,
            compiler_params=pltpu.CompilerParams(vmem_limit_bytes=32 << 20),
            out_shape=(
                jax.ShapeDtypeStruct((total, width), jnp.bfloat16),
                pltpu.HBM((total, model), jnp.bfloat16),
                pltpu.HBM((total, 2 * width), jnp.float32),
                pltpu.HBM((2 * total, 1), jnp.float32),
                pltpu.HBM((model, 2 * width), jnp.bfloat16),
            ),
            scratch_shapes=[pltpu.VMEM((total, width), jnp.bfloat16)] * 3
            + [
                pltpu.VMEM((total, model), jnp.bfloat16),
                pltpu.SemaphoreType.DMA((19,)),
                pltpu.VMEM((total, width), jnp.float32),
                pltpu.VMEM((total, width), jnp.float32),
                pltpu.VMEM((total, 1), jnp.int32),
                pltpu.VMEM((total, model), jnp.bfloat16),
                pltpu.VMEM((total, 2 * width), jnp.float32),
                pltpu.VMEM((2 * total, 1), jnp.float32),
                pltpu.VMEM((model, 2 * width), jnp.bfloat16),
            ],
        )(
            places, gain, *in_hbm(pieces), query_gain, key_gain,
            *in_hbm((cosine, sine, doc_column)), doc_row, *in_hbm(xs),
        )

    return call


def residual_stage(places, mix_pieces, out_pieces, xs, mlp_gain):
    total, model = 8 * xs[0].shape[0], xs[0].shape[1]
    width = mix_pieces[0].shape[1]
    own_rows = out_pieces[0].shape[0]

    def kernel(place_ref, gain_ref, *refs):
        mix_refs = refs[:8]
        out_refs = refs[8:16]
        x_refs = refs[16:24]
        normed_ref, mixed_out, cols_out, resid_out, hat_out, scale_ref = refs[24:30]
        weight_scr, x_scr, sems, mixed_ref, cols_ref, resid_ref, hat_ref = refs[30:]
        rank = 2 * place_ref[0] + place_ref[1]
        copies = []
        for mask, ref in zip(xor_order, out_refs):
            first = pl.multiple_of((rank ^ mask) * own_rows, own_rows)
            copies.append((ref, weight_scr.at[pl.ds(first, own_rows), :]))
        for step, row_mask in enumerate(xor_order):
            first = pl.multiple_of((rank ^ row_mask) * own_rows, own_rows)
            for mask, ref in zip(xor_order, mix_refs):
                lanes = pl.ds(pl.multiple_of((rank ^ mask) * width, width), width)
                copies.append(
                    (
                        ref.at[pl.ds(first, own_rows), :],
                        mixed_ref.at[pl.ds(step * own_rows, own_rows), lanes],
                    )
                )
        for step, ref in enumerate(x_refs):
            copies.append((ref, x_scr.at[pl.ds(step * own_rows, own_rows), :]))
        handles = start_copies(copies, sems)
        for handle in handles:
            handle.wait()
        cols_ref[...] = weight_scr[:, pl.ds(pl.multiple_of(rank * width, width), width)]
        outward = start_copies(
            [(mixed_ref, mixed_out), (cols_ref, cols_out)], sems, len(copies)
        )
        for first in range(0, total, total // 4):
            rows = pl.ds(first, total // 4)
            resid = x_scr[rows, :].astype(jnp.float32) + dot_last(
                mixed_ref[rows, :], weight_scr[...]
            )
            scale = rms_scale(resid)
            hat = resid * scale
            normed_ref[rows, :] = (hat * gain_ref[...]).astype(jnp.bfloat16)
            if first == 0:
                resid_ref[...] = resid[:own_rows]
                hat_ref[...] = hat[:own_rows]
                scale_ref[...] = scale[:own_rows]
                outward += start_copies(
                    [(resid_ref, resid_out), (hat_ref, hat_out)], sems, len(copies) + 2
                )
        for handle in outward:
            handle.wait()

    return pl.pallas_call(
        kernel,
        name="residual_stage",
        in_specs=[scalar_spec(), whole_spec()] + [any_spec()] * 24,
        out_specs=(whole_spec(),) + (any_spec(),) * 4 + (whole_spec(),),
        compiler_params=pltpu.CompilerParams(vmem_limit_bytes=24 << 20),
        out_shape=(
            jax.ShapeDtypeStruct((total, model), jnp.bfloat16),
            pltpu.HBM((total, model), jnp.bfloat16),
            pltpu.HBM((model, width), jnp.bfloat16),
            pltpu.HBM((own_rows, model), jnp.float32),
            pltpu.HBM((own_rows, model), jnp.float32),
            jax.ShapeDtypeStruct((own_rows, 1), jnp.float32),
        ),
        scratch_shapes=[
            pltpu.VMEM((model, model), jnp.bfloat16),
            pltpu.VMEM((total, model), jnp.bfloat16),
            pltpu.SemaphoreType.DMA((84,)),
            pltpu.VMEM((total, model), jnp.bfloat16),
            pltpu.VMEM((model, width), jnp.bfloat16),
            pltpu.VMEM((own_rows, model), jnp.float32),
            pltpu.VMEM((own_rows, model), jnp.float32),
        ],
    )(places, mlp_gain, *in_hbm((*mix_pieces, *out_pieces, *xs)))


def stack_rows(pieces):
    rows, width = pieces[0].shape

    def kernel(*refs):
        out_ref, sems = refs[-2:]
        handles = start_copies(
            [(ref, out_ref.at[pl.ds(at * rows, rows), :]) for at, ref in enumerate(refs[:-2])],
            sems,
        )
        for handle in handles:
            handle.wait()

    return pl.pallas_call(
        kernel,
        name="stack_rows",
        in_specs=[any_spec()] * len(pieces),
        compiler_params=pltpu.CompilerParams(vmem_limit_bytes=8 << 20),
        scratch_shapes=[pltpu.SemaphoreType.DMA((len(pieces),))],
        out_shape=jax.ShapeDtypeStruct((rows * len(pieces), width), pieces[0].dtype),
    )(*pieces)


def attention_backward(head_dim, block):
    score_scale = head_dim ** (-0.5)
    assert score_scale == 2.0 ** round(math.log2(score_scale))
    width = 2 * head_dim

    def kernel(
        place_ref, raw_ref, mix_ref, out_cols_ref, lse_ref, query_gain_ref,
        key_gain_ref, cos_ref, sin_ref, doc_col_ref, doc_row_ref, normed_ref, *refs,
    ):
        resid_refs = refs[:8]
        grads_out_ref, query_part_ref, key_part_ref, resid_own_ref = refs[8:12]
        refs = refs[12:]
        piece_refs = refs[:8]
        query_scr, key_scr, value_scr, mix_grad_scr, grads_ref, key_sum, value_sum = refs[8:15]
        resid_scr, sems = refs[15:]
        total = raw_ref.shape[0]
        own_rows = total // 8
        rank = 2 * place_ref[0] + place_ref[1]
        handles = start_copies(
            [
                (ref, resid_scr.at[pl.ds(step * own_rows, own_rows), :])
                for step, ref in enumerate(resid_refs)
            ],
            sems,
        )

        def rotate(step, carry):
            rows = pl.ds(pl.multiple_of(step * block, block), block)
            parts = rotated_heads(
                raw_ref[rows, :], query_gain_ref[...], key_gain_ref[...], cos_ref[rows, :],
                sin_ref[rows, :], head_dim,
            )
            query_scr[rows, :] = (parts[4].astype(jnp.bfloat16) * score_scale).astype(jnp.bfloat16)
            key_scr[rows, :] = parts[5].astype(jnp.bfloat16)
            value_scr[rows, :] = parts[6].astype(jnp.bfloat16)
            return carry

        lax.fori_loop(0, total // block, rotate, 0)
        for handle in handles:
            handle.wait()
        resid_own_ref[...] = resid_scr[:, pl.ds(pl.multiple_of(rank * width, width), width)]
        for half in range(0, total, 4 * own_rows):
            mix_grad = dot_plain(
                resid_scr[pl.ds(half, 4 * own_rows), :], out_cols_ref[...]
            ).astype(jnp.bfloat16)
            for step in range(4):
                mask = xor_order[half // own_rows + step]
                first = pl.multiple_of((rank ^ mask) * own_rows, own_rows)
                mix_grad_scr[pl.ds(first, own_rows), :] = mix_grad[
                    step * own_rows : (step + 1) * own_rows
                ]
        query_gain = query_gain_ref[...]
        key_gain = key_gain_ref[...]

        def heads_of(rows):
            return rotated_heads(
                raw_ref[rows, :], query_gain, key_gain, cos_ref[rows, :], sin_ref[rows, :],
                head_dim,
            )

        def unrotated(grad, rows):
            return grad * cos_ref[rows, :] - swap_halves(grad, head_dim) * sin_ref[rows, :]

        def norm_back(upstream, hat, norm, gain):
            scaled = upstream * gain
            return norm * (scaled - hat * pair_scale(scaled * hat, head_dim))

        key_sum[...] = jnp.zeros_like(key_sum)
        value_sum[...] = jnp.zeros_like(value_sum)
        wide = 2 * block

        def query_block(step, query_part):
            first = pl.multiple_of(step * block, block)
            rows = pl.ds(first, block)
            stacked = stack_heads(query_scr[rows, :], head_dim)
            stacked_grad = stack_heads(mix_grad_scr[rows, :], head_dim)
            mixed = mix_ref[rows, :].astype(jnp.float32)
            delta = jnp.sum(
                stacked_grad.astype(jnp.float32) * jnp.concatenate([mixed, mixed], axis=0),
                axis=1,
                keepdims=True,
            )
            lse = lse_ref[pl.ds(pl.multiple_of(2 * first, 2 * block), 2 * block), :]
            doc_column = doc_col_ref[rows, :]

            def key_block(at, rotated):
                begin = pl.multiple_of(at * wide, wide)
                keys = pl.ds(begin, wide)
                allowed = allowed_pairs(
                    doc_column, doc_row_ref[:, keys], first - begin, block, wide
                )
                allowed = jnp.concatenate([allowed, allowed], axis=0)
                scores = dot_last(stacked, key_scr[keys, :])
                probs = jnp.exp(jnp.where(allowed, scores - lse, very_low))
                prob_grad = dot_last(stacked_grad, value_scr[keys, :])
                score_grad = (probs * (prob_grad - delta)).astype(jnp.bfloat16)
                key_sum[keys, :] += dot_first(score_grad, stacked)
                value_sum[keys, :] += dot_first(probs.astype(jnp.bfloat16), stacked_grad)
                return rotated + dot_plain(score_grad, key_scr[keys, :])

            rotated = lax.fori_loop(
                0, step // 2 + 1, key_block, jnp.zeros((2 * block, width), jnp.float32)
            )
            query_hat, query_norm = heads_of(rows)[:2]
            straight = unrotated(join_heads(rotated, head_dim) * score_scale, rows)
            grads_ref[rows, :width] = norm_back(
                straight, query_hat, query_norm, query_gain
            ).astype(jnp.bfloat16)
            return query_part + jnp.sum(straight * query_hat, axis=0, keepdims=True)

        zero_part = jnp.zeros((1, width), jnp.float32)
        query_part = lax.fori_loop(0, total // block, query_block, zero_part)

        def finish_keys(step, key_part):
            rows = pl.ds(pl.multiple_of(step * block, block), block)
            key_hat, key_norm = heads_of(rows)[2:4]
            summed = key_sum[rows, :]
            summed = summed + pltpu.roll(summed, head_dim, 1)
            values = value_sum[rows, :]
            values = values + pltpu.roll(values, head_dim, 1)
            straight = unrotated(summed, rows)
            key_grad = norm_back(straight, key_hat, key_norm, key_gain)
            lower = lower_lanes(key_grad.shape, head_dim)
            grads_ref[rows, width:] = jnp.where(lower, key_grad, values).astype(jnp.bfloat16)
            return key_part + jnp.sum(straight * key_hat, axis=0, keepdims=True)

        key_part = lax.fori_loop(0, total // block, finish_keys, zero_part)
        query_part_ref[...] = query_part
        key_part_ref[...] = key_part
        for step, mask in enumerate(xor_order):
            first = pl.multiple_of((rank ^ mask) * own_rows, own_rows)
            grads_out_ref[pl.ds(step * own_rows, own_rows), :] = grads_ref[
                pl.ds(first, own_rows), :
            ]
        for mask, piece_ref in enumerate(piece_refs):
            lanes = pl.ds(pl.multiple_of((rank ^ mask) * width, width), width)
            piece_ref[...] = dot_first(normed_ref[:, lanes], grads_out_ref[...]).astype(
                jnp.bfloat16
            )

    def call(
        places, raw, mix, resids, out_cols, lse, query_gain, key_gain, cosine, sine, doc_col,
        doc_row, normed,
    ):
        total = raw.shape[0]
        return pl.pallas_call(
            kernel,
            name="attention_backward",
            in_specs=[scalar_spec()] + [whole_spec()] * 11 + [any_spec()] * 8,
            compiler_params=pltpu.CompilerParams(vmem_limit_bytes=36 << 20),
            out_shape=(
                jax.ShapeDtypeStruct((total, 2 * width), jnp.bfloat16),
                jax.ShapeDtypeStruct((1, width), jnp.float32),
                jax.ShapeDtypeStruct((1, width), jnp.float32),
                jax.ShapeDtypeStruct((total, width), jnp.bfloat16),
            )
            + (jax.ShapeDtypeStruct((width, 2 * width), jnp.bfloat16),) * 8,
            scratch_shapes=[pltpu.VMEM((total, width), jnp.bfloat16)] * 4
            + [pltpu.VMEM((total, 2 * width), jnp.bfloat16)]
            + [pltpu.VMEM((total, width), jnp.float32)] * 2
            + [pltpu.VMEM((total, normed.shape[1]), jnp.bfloat16), pltpu.SemaphoreType.DMA((8,))],
        )(
            places, raw, mix, out_cols, lse, query_gain, key_gain, cosine, sine, doc_col,
            doc_row, normed, *in_hbm(resids),
        )

    return call


def unpack_heads(places, summed, head_dim):
    rows = summed.shape[0]
    width = 2 * head_dim
    model = 8 * width

    def kernel(place_ref, sum_ref, query_ref, key_ref, value_ref, out_ref):
        shard = place_ref[0]
        core = place_ref[1]
        for step in range(4):
            other = shard ^ step
            first = sum_ref[:, pl.ds(4 * step * width, 2 * width)].astype(jnp.float32)
            second = sum_ref[:, pl.ds((4 * step + 2) * width, 2 * width)].astype(jnp.float32)
            even = jnp.where(core == 0, first, second)
            odd = jnp.where(core == 0, second, first)
            query_ref[:, pl.ds(pl.multiple_of(2 * other * width, width), width)] = even[:, :width]
            query_ref[:, pl.ds(pl.multiple_of((2 * other + 1) * width, width), width)] = odd[
                :, :width
            ]
            even = even[:, width:]
            odd = odd[:, width:]
            lower = lower_lanes(even.shape, head_dim)
            lanes = pl.ds(pl.multiple_of(other * width, width), width)
            key_ref[:, lanes] = jnp.where(lower, even, pltpu.roll(odd, head_dim, 1))
            value_ref[:, lanes] = jnp.where(lower, pltpu.roll(even, head_dim, 1), odd)
        out_ref[...] = sum_ref[:, 2 * model :].astype(jnp.float32)

    return pl.pallas_call(
        kernel,
        name="unpack_heads",
        in_specs=[scalar_spec(), whole_spec()],
        out_shape=(
            jax.ShapeDtypeStruct((rows, model), jnp.float32),
            jax.ShapeDtypeStruct((rows, model // 2), jnp.float32),
            jax.ShapeDtypeStruct((rows, model // 2), jnp.float32),
            jax.ShapeDtypeStruct((rows, summed.shape[1] - 2 * model), jnp.float32),
        ),
    )(places, summed)


def heads_body(
    tokens_in,
    doc_lengths,
    attn_gain,
    w_query,
    key_weight,
    value_weight,
    w_output,
    query_norm_gain,
    key_norm_gain,
    mlp_gain,
    w_gate,
    w_up,
    w_down,
    out_grad,
):
    row_count, model_width = tokens_in.shape
    head_dim = query_norm_gain.shape[0]
    total = row_count * 8
    half_rows = total // 2
    block = 256
    core = lax.axis_index("seq")
    shard = lax.axis_index("shard")
    places = jnp.stack([shard, core]).astype(jnp.int32)

    x_near = gather_near(tokens_in)
    head_pieces = pack_heads(w_query, key_weight, value_weight, places, head_dim)
    head_pieces = [head_pieces[0]] + [
        group_swap(head_pieces[step], 2 * step) for step in (1, 2, 3)
    ]
    x_far = gather_far(x_near)
    x_pieces = x_near + x_far

    out_near = lax.dynamic_slice_in_dim(w_output, core * row_count, row_count)
    out_local = lax.dynamic_slice_in_dim(w_output, (1 - core) * row_count, row_count)
    out_own = after(out_near, x_near[1:])
    out_near = [out_own]
    for mask in (2, 4, 6):
        out_near.append(group_swap(out_own, mask))
    out_pieces = out_near + [out_local] + gather_far(out_near[1:])

    index = jnp.arange(total, dtype=jnp.int32)
    docs, offsets = doc_info(doc_lengths[0], index)
    half_dim = head_dim // 2
    inverse_freq = rope_base ** (-(jnp.arange(half_dim, dtype=jnp.float32) * 2.0 / head_dim))
    angles = offsets.astype(jnp.float32)[:, None] * jnp.tile(inverse_freq, 4)[None, :]
    cosine = jnp.cos(angles)
    sine = jnp.where(lower_lanes(angles.shape, half_dim), -1.0, 1.0) * jnp.sin(angles)
    doc_column = docs[:, None]
    doc_row = docs[None, :]
    query_gain = jnp.concatenate([query_norm_gain] * 2)[None, :]
    key_gain = jnp.concatenate([key_norm_gain] * 2)[None, :]

    mix, normed, raw, lse, head_weight = attention_forward(head_dim, block)(
        places, x_pieces, attn_gain[None, :], head_pieces, query_gain, key_gain, cosine, sine,
        doc_column, doc_row,
    )
    mix_near = gather_near(mix)
    mix_far = gather_far(mix_near)
    grad_near = gather_near(after(out_grad, mix_near[1:]))
    grad_all = stack_rows(grad_near + gather_far(grad_near))

    normed_mid, mix_all, out_cols, own_resid, own_hat, own_scale = residual_stage(
        places, mix_near + mix_far, out_pieces, x_pieces, mlp_gain[None, :]
    )

    hidden_rows = w_gate.shape[0] // 2

    def own_rows(weight):
        return lax.dynamic_slice_in_dim(weight, core * hidden_rows, hidden_rows)

    gate_rows = own_rows(w_gate)
    up_rows = own_rows(w_up)
    down_rows = own_rows(w_down)
    gate = dot_last(normed_mid, gate_rows)
    up = dot_last(normed_mid, up_rows)
    grad_hidden = dot_last(grad_all, down_rows)
    gate_sig = jax.nn.sigmoid(gate)
    hidden = (gate * gate_sig * up).astype(jnp.bfloat16)
    gate_grad = (grad_hidden * up * gate_sig * (1.0 + gate * (1.0 - gate_sig))).astype(jnp.bfloat16)
    up_grad = (grad_hidden * gate * gate_sig).astype(jnp.bfloat16)

    def mid_part(first):
        rows = slice(first, first + half_rows)
        return dot_plain(gate_grad[rows], gate_rows) + dot_plain(up_grad[rows], up_rows)

    mlp_grads = jnp.concatenate(
        [
            dot_first(hidden, grad_all).astype(jnp.bfloat16),
            dot_first(gate_grad, normed_mid).astype(jnp.bfloat16),
            dot_first(up_grad, normed_mid).astype(jnp.bfloat16),
        ],
        axis=0,
    )
    mlp_sums = lax.psum(mlp_grads, "rep").astype(jnp.float32)

    gate_grad, up_grad = after((gate_grad, up_grad), mlp_grads)
    grad_mid = scatter_sum(mid_part(0), mid_part(half_rows))
    grad_resid = out_grad.astype(jnp.float32) + root_mean_backward(
        own_hat, own_scale, mlp_gain, grad_mid
    )
    mlp_gain_part = jnp.sum(grad_mid * own_hat, axis=0)
    resid_near = gather_near(grad_resid.astype(jnp.bfloat16))
    resid_pieces = resid_near + gather_far(resid_near)

    act_out = own_resid + scatter_sum(
        dot_plain(hidden[:half_rows], down_rows), dot_plain(hidden[half_rows:], down_rows)
    )

    backward = attention_backward(head_dim, block)(
        places, raw, mix, resid_pieces, out_cols, lse, query_gain, key_gain, cosine, sine,
        doc_column, doc_row, normed,
    )
    head_grads, query_part, key_part, resid_own = backward[:4]
    weight_pieces = backward[4:]
    weight_pieces = [weight_pieces[0]] + [
        group_swap(weight_pieces[mask], mask) for mask in range(1, 8)
    ]
    out_grads = dot_first(resid_own, mix_all).astype(jnp.bfloat16)
    grad_in_norm = scatter_sum(
        dot_last(head_grads[:half_rows], head_weight),
        dot_last(head_grads[half_rows:], head_weight),
    )
    own_x = tokens_in.astype(jnp.float32)
    own_norm = rms_scale(own_x)
    x_hat = own_x * own_norm
    in_grad = grad_resid + root_mean_backward(x_hat, own_norm, attn_gain, grad_in_norm)
    attn_gain_part = jnp.sum(grad_in_norm * x_hat, axis=0)
    query_gain_part = query_part[0, :head_dim] + query_part[0, head_dim:]
    gains = sum_everywhere(
        jnp.concatenate(
            [attn_gain_part, mlp_gain_part, query_gain_part, key_part[0, :head_dim]]
        )[None, :]
    )[0]
    attn_grads = rep_halving_sum(
        jnp.concatenate(weight_pieces + [out_grads], axis=1), grad_in_norm, gains
    )
    grad_query, grad_key, grad_value, grad_output = unpack_heads(places, attn_grads, head_dim)
    return (
        act_out,
        in_grad,
        gains[:model_width],
        grad_query,
        grad_key,
        grad_value,
        grad_output,
        gains[2 * model_width : 2 * model_width + head_dim],
        gains[2 * model_width + head_dim :],
        gains[model_width : 2 * model_width],
        mlp_sums[hidden_rows : 2 * hidden_rows],
        mlp_sums[2 * hidden_rows :],
        mlp_sums[:hidden_rows],
    )


def local_by_heads(*arrays):
    return heads_body(*arrays)


def solution(mesh):
    placed = (
        P(("rep", "shard", "seq"), None),
        P("rep", None),
        P(),
        P("shard", None),
        P("shard", None),
        P("shard", None),
        P("shard", None),
        P(),
        P(),
        P(),
        P("shard", None),
        P("shard", None),
        P("shard", None),
        P(("rep", "shard", "seq"), None),
    )
    sizes = dict(mesh.shape)
    by_heads = sizes["rep"] == 4 and sizes["shard"] == 4 and sizes["seq"] == 2
    return jax.shard_map(
        local_by_heads if by_heads else local,
        mesh=mesh,
        in_specs=placed,
        out_specs=(
            P(("rep", "shard", "seq"), None),
            P(("rep", "shard", "seq"), None),
            P(),
            P(("shard", "seq"), None),
            P(("shard", "seq"), None),
            P(("shard", "seq"), None),
            P(("shard", "seq"), None),
            P(),
            P(),
            P(),
            P(("shard", "seq"), None),
            P(("shard", "seq"), None),
            P(("shard", "seq"), None),
        ),
        check_vma=False,
    )
```

```python
import math

import jax
import jax.numpy as jnp
from jax import lax
from jax.experimental import pallas as pl
from jax.experimental.pallas import tpu as pltpu
from jax.sharding import PartitionSpec as P

norm_eps = 1e-05
rope_base = 1000000.0
very_low = -1e30
contract_last = (((1,), (1,)), ((), ()))
contract_first = (((0,), (0,)), ((), ()))


def rms_scale(values):
    return lax.rsqrt(jnp.mean(values * values, axis=-1, keepdims=True) + norm_eps)


def root_mean_backward(normed, factor, gain, upstream):
    scaled = upstream * gain
    return factor * (scaled - normed * jnp.mean(scaled * normed, axis=-1, keepdims=True))


def rope_tables(positions, head_dim):
    half_dim = head_dim // 2
    inverse_freq = rope_base ** (-(jnp.arange(half_dim, dtype=jnp.float32) * 2.0 / head_dim))
    angles = positions.astype(jnp.float32)[:, None] * inverse_freq[None, :]
    return (jnp.cos(angles)[:, None, :], jnp.sin(angles)[:, None, :])


def rotate_pairs(values, cosine_table, sine_values):
    half_dim = values.shape[-1] // 2
    lower_half = values[..., :half_dim]
    upper_half = values[..., half_dim:]
    return jnp.concatenate(
        [
            lower_half * cosine_table - upper_half * sine_values,
            upper_half * cosine_table + lower_half * sine_values,
        ],
        axis=-1,
    )


def rotate_back(grads, cosine_table, sine_values):
    half_dim = grads.shape[-1] // 2
    lower_half = grads[..., :half_dim]
    upper_half = grads[..., half_dim:]
    return jnp.concatenate(
        [
            lower_half * cosine_table + upper_half * sine_values,
            upper_half * cosine_table - lower_half * sine_values,
        ],
        axis=-1,
    )


def doc_info(lengths, positions):
    doc_ends = jnp.cumsum(lengths)
    finished = doc_ends[None, :] <= positions[:, None]
    doc_ids = jnp.sum(finished.astype(jnp.int32), axis=1)
    doc_first = jnp.sum(jnp.where(finished, lengths[None, :], 0), axis=1)
    return (doc_ids, positions - doc_first)


def local(
    tokens_in,
    doc_lengths,
    attn_gain,
    w_query,
    key_weight,
    value_weight,
    w_output,
    query_norm_gain,
    key_norm_gain,
    mlp_gain,
    w_gate,
    w_up,
    w_down,
    out_grad,
):
    row_count = tokens_in.shape[0]
    model_width = tokens_in.shape[1]
    head_dim = query_norm_gain.shape[0]
    query_width = w_query.shape[1]
    kv_width = key_weight.shape[1]
    kv_heads = kv_width // head_dim
    head_grouping = query_width // kv_width
    score_scale = head_dim ** (-0.5)
    rank_count = lax.axis_size("shard") * lax.axis_size("seq")
    group_rows = row_count * rank_count
    first_row = lax.axis_index(("shard", "seq")) * row_count
    key_block = min(512, group_rows)
    block_count = group_rows // key_block
    key_index = jnp.arange(group_rows, dtype=jnp.int32)
    key_docs, key_offset = doc_info(doc_lengths[0], key_index)
    query_index = first_row + jnp.arange(row_count, dtype=jnp.int32)
    query_docs = lax.dynamic_slice_in_dim(key_docs, first_row, row_count)
    query_offset = lax.dynamic_slice_in_dim(key_offset, first_row, row_count)
    cosine_table, sine_values = rope_tables(query_offset, head_dim)
    x_float = tokens_in.astype(jnp.float32)
    norm_one = rms_scale(x_float)
    x_hat = x_float * norm_one
    normalized_input = (x_hat * attn_gain).astype(jnp.bfloat16)
    pieces = (
        lax.all_gather(w_query, "shard", axis=0, tiled=True),
        lax.all_gather(key_weight, "shard", axis=0, tiled=True),
        lax.all_gather(value_weight, "shard", axis=0, tiled=True),
    )
    in_cols = normalized_input
    queries, key_proj, value_proj = tuple(
        (jnp.dot(in_cols, weight, preferred_element_type=jnp.float32) for weight in pieces)
    )
    query_heads = queries.reshape(row_count, query_width // head_dim, head_dim)
    query_norm = rms_scale(query_heads)
    query_normalized = query_heads * query_norm
    query_rotated = rotate_pairs(
        query_normalized * query_norm_gain, cosine_table, sine_values
    ).astype(jnp.bfloat16)
    key_head_rows = key_proj.reshape(row_count, kv_heads, head_dim)
    key_head_norm = rms_scale(key_head_rows)
    key_normalized = key_head_rows * key_head_norm
    key_rot = rotate_pairs(key_normalized * key_norm_gain, cosine_table, sine_values).astype(
        jnp.bfloat16
    )
    value_rows = value_proj.astype(jnp.bfloat16)
    key_all, value_all = (
        lax.all_gather(key_rot.reshape(row_count, kv_width), ("shard", "seq"), axis=0, tiled=True),
        lax.all_gather(value_rows, ("shard", "seq"), axis=0, tiled=True),
    )
    query_grouped = query_rotated.reshape(row_count, kv_heads, head_grouping, head_dim)

    def block_mask(offset, span_rows):
        docs_here = lax.dynamic_slice_in_dim(key_docs, offset, span_rows)
        index_here = offset + jnp.arange(span_rows, dtype=jnp.int32)
        return (query_docs[:, None] == docs_here[None, :]) & (
            index_here[None, :] <= query_index[:, None]
        )

    def block_scores(offset, span_rows, allowed):
        key_rows = lax.dynamic_slice_in_dim(key_all, offset, span_rows, 0).reshape(
            span_rows, kv_heads, head_dim
        )
        value_block = lax.dynamic_slice_in_dim(value_all, offset, span_rows, 0).reshape(
            span_rows, kv_heads, head_dim
        )
        scores = (
            jnp.einsum(
                "tgjd,rgd->gjtr", query_grouped, key_rows, preferred_element_type=jnp.float32
            )
            * score_scale
        )
        return (jnp.where(allowed, scores, very_low), key_rows, value_block)

    def total_block(block_index, running):
        offset = block_index * key_block
        allowed = block_mask(offset, key_block)

        def total_accumulate(softmax_state):
            row_high, row_total = softmax_state
            scores, _, _ = block_scores(offset, key_block, allowed)
            new_high = jnp.maximum(row_high, jnp.max(scores, axis=-1))
            exp_scores = jnp.where(allowed, jnp.exp(scores - new_high[..., None]), 0.0)
            row_total = row_total * jnp.exp(row_high - new_high) + jnp.sum(exp_scores, axis=-1)
            return (new_high, row_total)

        return lax.cond(
            jnp.any(allowed), total_accumulate, lambda softmax_state: softmax_state, running
        )

    softmax_init = (
        jnp.full((kv_heads, head_grouping, row_count), very_low, jnp.float32),
        jnp.zeros((kv_heads, head_grouping, row_count), jnp.float32),
    )
    row_high, row_total = lax.fori_loop(0, block_count, total_block, softmax_init)
    log_total = row_high + jnp.log(row_total)

    def mix_block(block_index, weighted):
        offset = block_index * key_block
        allowed = block_mask(offset, key_block)

        def mix_accumulate(current):
            scores, _, value_block = block_scores(offset, key_block, allowed)
            attn_prob = jnp.where(allowed, jnp.exp(scores - log_total[..., None]), 0.0).astype(
                jnp.bfloat16
            )
            return current + jnp.einsum(
                "gjtr,rgd->gjtd", attn_prob, value_block, preferred_element_type=jnp.float32
            )

        return lax.cond(jnp.any(allowed), mix_accumulate, lambda current: current, weighted)

    weighted = lax.fori_loop(
        0,
        block_count,
        mix_block,
        jnp.zeros((kv_heads, head_grouping, row_count, head_dim), jnp.float32),
    )
    head_mixture = (
        weighted.transpose(2, 0, 1, 3).reshape(row_count, query_width).astype(jnp.bfloat16)
    )
    attn_part = lax.dot_general(
        head_mixture,
        lax.all_gather(w_output, "shard", axis=0, tiled=True),
        contract_last,
        preferred_element_type=jnp.float32,
    )
    residual = x_float + attn_part
    norm_two = rms_scale(residual)
    resid_hat = residual * norm_two
    normed_mid = (resid_hat * mlp_gain).astype(jnp.bfloat16)
    gate_rows = lax.all_gather(w_gate, "shard", axis=0, tiled=True)
    up_rows = lax.all_gather(w_up, "shard", axis=0, tiled=True)
    down_rows = lax.all_gather(w_down, "shard", axis=0, tiled=True)
    gate_part = lax.dot_general(
        normed_mid, gate_rows, contract_last, preferred_element_type=jnp.float32
    )
    up_part = lax.dot_general(
        normed_mid, up_rows, contract_last, preferred_element_type=jnp.float32
    )
    hidden_part = (gate_part * jax.nn.sigmoid(gate_part) * up_part).astype(jnp.bfloat16)
    mlp_sum = jnp.dot(hidden_part, down_rows, preferred_element_type=jnp.float32)
    mlp_gate_store = gate_part
    mlp_up_store = up_part
    hidden_store = hidden_part
    mlp_sum, gate_store, up_store, hidden_store = (
        mlp_sum,
        mlp_gate_store,
        mlp_up_store,
        hidden_store,
    )
    act_out = residual + mlp_sum
    grad_float = out_grad.astype(jnp.float32)
    gate_rows = lax.all_gather(w_gate, "shard", axis=0, tiled=True)
    up_rows = lax.all_gather(w_up, "shard", axis=0, tiled=True)
    down_rows = lax.all_gather(w_down, "shard", axis=0, tiled=True)
    gate_part = gate_store
    up_part = up_store
    grad_hidden = lax.dot_general(
        out_grad, down_rows, contract_last, preferred_element_type=jnp.float32
    )
    gate_sig = jax.nn.sigmoid(gate_part)
    gate_grad = (grad_hidden * up_part * gate_sig * (1.0 + gate_part * (1.0 - gate_sig))).astype(
        jnp.bfloat16
    )
    up_grad = (grad_hidden * gate_part * gate_sig).astype(jnp.bfloat16)
    grad_mid = jnp.dot(gate_grad, gate_rows, preferred_element_type=jnp.float32) + jnp.dot(
        up_grad, up_rows, preferred_element_type=jnp.float32
    )
    gate_grad_store = gate_grad
    up_grad_store = up_grad
    grad_mid, gate_grad_store, up_grad_store = (grad_mid, gate_grad_store, up_grad_store)
    grad_resid = grad_float + root_mean_backward(resid_hat, norm_two, mlp_gain, grad_mid)
    mlp_gain_part = jnp.sum(grad_mid * resid_hat, axis=0)
    grad_resid_b = grad_resid.astype(jnp.bfloat16)
    resid_cols = grad_resid_b
    mixing_gradient = jnp.dot(
        resid_cols,
        lax.all_gather(w_output, "shard", axis=0, tiled=True),
        preferred_element_type=jnp.float32,
    ).astype(jnp.bfloat16)
    mix_grouped = mixing_gradient.reshape(row_count, kv_heads, head_grouping, head_dim)
    delta_row_values = jnp.sum(
        (mixing_gradient.astype(jnp.float32) * head_mixture.astype(jnp.float32)).reshape(
            row_count, kv_heads, head_grouping, head_dim
        ),
        axis=-1,
    ).transpose(1, 2, 0)

    def score_grads(offset, span_rows, allowed):
        scores, key_rows, value_block = block_scores(offset, span_rows, allowed)
        attn_prob = jnp.where(allowed, jnp.exp(scores - log_total[..., None]), 0.0)
        grad_prob = jnp.einsum(
            "tgjd,rgd->gjtr", mix_grouped, value_block, preferred_element_type=jnp.float32
        )
        grad_score = (attn_prob * (grad_prob - delta_row_values[..., None])).astype(jnp.bfloat16)
        return (attn_prob, grad_score, key_rows)

    def query_pass(block_index, grad_sum):
        offset = block_index * key_block
        allowed = block_mask(offset, key_block)

        def query_accumulate(current):
            _, grad_score, key_rows = score_grads(offset, key_block, allowed)
            return current + score_scale * jnp.einsum(
                "gjtr,rgd->tgjd", grad_score, key_rows, preferred_element_type=jnp.float32
            )

        return lax.cond(jnp.any(allowed), query_accumulate, lambda current: current, grad_sum)

    query_rot_grad = lax.fori_loop(
        0,
        block_count,
        query_pass,
        jnp.zeros((row_count, kv_heads, head_grouping, head_dim), jnp.float32),
    )

    def one_block(start_row):
        allowed = block_mask(start_row, key_block)

        def compute(unused):
            attn_prob, grad_score, _ = score_grads(start_row, key_block, allowed)
            key_grad = score_scale * jnp.einsum(
                "gjtr,tgjd->rgd", grad_score, query_grouped, preferred_element_type=jnp.float32
            )
            value_grad = jnp.einsum(
                "gjtr,tgjd->rgd",
                attn_prob.astype(jnp.bfloat16),
                mix_grouped,
                preferred_element_type=jnp.float32,
            )
            return jnp.concatenate(
                [key_grad.reshape(key_block, kv_width), value_grad.reshape(key_block, kv_width)],
                axis=1,
            )

        return lax.cond(
            jnp.any(allowed),
            compute,
            lambda unused: jnp.zeros((key_block, 2 * kv_width), jnp.float32),
            0,
        )

    starts = key_block * jnp.arange(
        row_count * lax.axis_size(("shard", "seq")) // key_block, dtype=jnp.int32
    )
    kv_summed = lax.psum_scatter(
        lax.map(one_block, starts).reshape(
            row_count * lax.axis_size(("shard", "seq")), 2 * kv_width
        ),
        ("shard", "seq"),
        scatter_dimension=0,
        tiled=True,
    )
    key_rot_grad = kv_summed[:, :kv_width].reshape(row_count, kv_heads, head_dim)
    value_grad_b = kv_summed[:, kv_width:].astype(jnp.bfloat16)
    key_unrotated = rotate_back(key_rot_grad, cosine_table, sine_values)
    key_gain_part = jnp.sum(key_unrotated * key_normalized, axis=(0, 1))
    key_row_gradient = (
        root_mean_backward(key_normalized, key_head_norm, key_norm_gain, key_unrotated)
        .reshape(row_count, kv_width)
        .astype(jnp.bfloat16)
    )
    query_unrot = rotate_back(
        query_rot_grad.reshape(row_count, query_width // head_dim, head_dim),
        cosine_table,
        sine_values,
    )
    query_gain_part = jnp.sum(query_unrot * query_normalized, axis=(0, 1))
    grad_query_rows = (
        root_mean_backward(query_normalized, query_norm, query_norm_gain, query_unrot)
        .reshape(row_count, query_width)
        .astype(jnp.bfloat16)
    )
    query_rows, key_rows, value_rows_w = lax.all_gather(
        (w_query, key_weight, value_weight), "shard", axis=0, tiled=True
    )
    grad_in_norm = (
        lax.dot_general(
            grad_query_rows, query_rows, contract_last, preferred_element_type=jnp.float32
        )
        + lax.dot_general(
            key_row_gradient, key_rows, contract_last, preferred_element_type=jnp.float32
        )
        + lax.dot_general(
            value_grad_b, value_rows_w, contract_last, preferred_element_type=jnp.float32
        )
    )
    in_grad = grad_resid + root_mean_backward(x_hat, norm_one, attn_gain, grad_in_norm)
    attn_gain_part = jnp.sum(grad_in_norm * x_hat, axis=0)
    grad_attn_gain, grad_mlp_gain, grad_query_gain, grad_key_gain = lax.psum(
        (attn_gain_part, mlp_gain_part, query_gain_part, key_gain_part), ("rep", "shard", "seq")
    )
    attn_grads = jnp.concatenate([grad_query_rows, key_row_gradient, value_grad_b], axis=1)
    d_share = model_width // rank_count
    in_own, resid_own, gate_own, up_own, hidden_own = (
        lax.all_to_all(normalized_input, ("shard", "seq"), split_axis=1, concat_axis=0, tiled=True),
        lax.all_to_all(grad_resid_b, ("shard", "seq"), split_axis=1, concat_axis=0, tiled=True),
        lax.all_to_all(gate_grad_store, ("shard", "seq"), split_axis=1, concat_axis=0, tiled=True),
        lax.all_to_all(up_grad_store, ("shard", "seq"), split_axis=1, concat_axis=0, tiled=True),
        lax.all_to_all(hidden_store, ("shard", "seq"), split_axis=1, concat_axis=0, tiled=True),
    )
    attn_piece = lax.all_gather(attn_grads, ("shard", "seq"), axis=0, tiled=True)
    mix_piece = lax.all_gather(head_mixture, ("shard", "seq"), axis=0, tiled=True)
    mid_piece = lax.all_gather(normed_mid, ("shard", "seq"), axis=0, tiled=True)
    grad_piece = lax.all_gather(out_grad, ("shard", "seq"), axis=0, tiled=True)
    in_cols = in_own
    resid_cols = resid_own
    attn_rows = jnp.concatenate(
        [
            lax.dot_general(
                in_cols, attn_piece, contract_first, preferred_element_type=jnp.float32
            ),
            lax.dot_general(
                resid_cols, mix_piece, contract_first, preferred_element_type=jnp.float32
            ),
        ],
        axis=1,
    )
    mlp_rows = jnp.concatenate(
        [
            lax.dot_general(
                gate_own, mid_piece, contract_first, preferred_element_type=jnp.float32
            ),
            lax.dot_general(up_own, mid_piece, contract_first, preferred_element_type=jnp.float32),
            lax.dot_general(
                hidden_own, grad_piece, contract_first, preferred_element_type=jnp.float32
            ),
        ],
        axis=1,
    )
    group_grads = jnp.concatenate([attn_rows, mlp_rows], axis=0)
    own_grads = lax.psum(group_grads, "rep")
    attn_block_grads = own_grads[:d_share]
    mlp_block_grads = own_grads[d_share:]
    grad_query = attn_block_grads[:, :query_width]
    grad_key = attn_block_grads[:, query_width : query_width + kv_width]
    grad_value = attn_block_grads[:, query_width + kv_width : query_width + 2 * kv_width]
    grad_output = attn_block_grads[:, query_width + 2 * kv_width :]
    grad_gate = mlp_block_grads[:, :model_width]
    grad_up = mlp_block_grads[:, model_width : 2 * model_width]
    grad_down = mlp_block_grads[:, 2 * model_width :]
    return (
        act_out,
        in_grad,
        grad_attn_gain,
        grad_query,
        grad_key,
        grad_value,
        grad_output,
        grad_query_gain,
        grad_key_gain,
        grad_mlp_gain,
        grad_gate,
        grad_up,
        grad_down,
    )


group_axes = ("shard", "seq")


def group_swap(values, mask):
    return lax.ppermute(values, group_axes, [(rank, rank ^ mask) for rank in range(8)])


def rep_swap(values, mask):
    return lax.ppermute(values, "rep", [(rank, rank ^ mask) for rank in range(4)])


xor_order = (0, 2, 4, 6, 1, 3, 5, 7)


def gather_near(own):
    return [own] + [group_swap(own, mask) for mask in (2, 4, 6)]


def gather_far(near):
    return [group_swap(piece, 1) for piece in near]


def after(values, marker):
    return lax.optimization_barrier((values, marker))[0]


def add_rounded(left, right):
    return (left.astype(jnp.float32) + right.astype(jnp.float32)).astype(jnp.bfloat16)


def scatter_sum(near_part, far_part):
    swapped = group_swap(far_part.astype(jnp.bfloat16), 1)
    width = near_part.shape[0] // 4
    halves = [
        near_part[at : at + width] + swapped[at : at + width].astype(jnp.float32)
        for at in range(0, 4 * width, width)
    ]
    total = halves[0]
    moved = [
        group_swap(half.astype(jnp.bfloat16), mask) for mask, half in zip((2, 4, 6), halves[1:])
    ]
    for piece in moved:
        total = total + piece.astype(jnp.float32)
    return total


def rep_halving_sum(values, first_marker, second_marker):
    place = lax.axis_index("rep")
    low = place % 2
    high = place // 2
    half = values.shape[0] // 2
    quarter = half // 2
    kept = lax.dynamic_slice_in_dim(values, low * half, half)
    sent = lax.dynamic_slice_in_dim(values, (1 - low) * half, half)
    part = add_rounded(*after((kept, rep_swap(sent, 1)), first_marker))
    kept = lax.dynamic_slice_in_dim(part, high * quarter, quarter)
    sent = lax.dynamic_slice_in_dim(part, (1 - high) * quarter, quarter)
    part = add_rounded(*after((kept, rep_swap(sent, 2)), second_marker))
    other = rep_swap(part, 2)
    part = jnp.where(
        high == 0, jnp.concatenate([part, other]), jnp.concatenate([other, part])
    )
    other = rep_swap(part, 1)
    return jnp.where(low == 0, jnp.concatenate([part, other]), jnp.concatenate([other, part]))


def sum_everywhere(values):
    for mask in (1, 2, 4):
        values = values + group_swap(values, mask)
    for mask in (1, 2):
        values = values + rep_swap(values, mask)
    return values


def lower_lanes(shape, width):
    return lax.broadcasted_iota(jnp.int32, shape, 1) % (2 * width) < width


def pair_scale(values, head_dim):
    lower = lower_lanes(values.shape, head_dim)
    low = jnp.sum(jnp.where(lower, values, 0.0), axis=1, keepdims=True)
    high = jnp.sum(jnp.where(lower, 0.0, values), axis=1, keepdims=True)
    return jnp.where(lower, low, high) * (1.0 / head_dim)


def swap_halves(values, head_dim):
    width = values.shape[1]
    half = head_dim // 2
    return jnp.where(
        lower_lanes(values.shape, half),
        pltpu.roll(values, width - half, 1),
        pltpu.roll(values, half, 1),
    )


def rotated_heads(raw, query_gain, key_gain, cosine, sine, head_dim):
    width = 2 * head_dim
    queries = raw[:, :width]
    keys = raw[:, width:]
    query_norm = lax.rsqrt(pair_scale(queries * queries, head_dim) + norm_eps)
    key_norm = lax.rsqrt(pair_scale(keys * keys, head_dim) + norm_eps)
    query_hat = queries * query_norm
    key_hat = keys * key_norm
    scaled = query_hat * query_gain
    query_rot = scaled * cosine + swap_halves(scaled, head_dim) * sine
    scaled = key_hat * key_gain
    key_rot = scaled * cosine + swap_halves(scaled, head_dim) * sine
    lower = lower_lanes(keys.shape, head_dim)
    key_twice = jnp.where(lower, key_rot, pltpu.roll(key_rot, head_dim, 1))
    value_twice = jnp.where(lower, pltpu.roll(keys, head_dim, 1), keys)
    return query_hat, query_norm, key_hat, key_norm, query_rot, key_twice, value_twice


def stack_heads(values, head_dim):
    lower = lower_lanes(values.shape, head_dim)
    zero = jnp.zeros_like(values)
    return jnp.concatenate(
        [jnp.where(lower, values, zero), jnp.where(lower, zero, values)], axis=0
    )


def join_heads(stacked, head_dim):
    rows = stacked.shape[0] // 2
    lower = lower_lanes((rows, stacked.shape[1]), head_dim)
    return jnp.where(lower, stacked[:rows], stacked[rows:])


def allowed_pairs(doc_column, doc_row, first, rows, span):
    row_index = first + lax.broadcasted_iota(jnp.int32, (rows, span), 0)
    key_index = lax.broadcasted_iota(jnp.int32, (rows, span), 1)
    return (doc_column == doc_row) & (key_index <= row_index)


def dot_last(left, right):
    return lax.dot_general(left, right, contract_last, preferred_element_type=jnp.float32)


def dot_first(left, right):
    return lax.dot_general(left, right, contract_first, preferred_element_type=jnp.float32)


def dot_plain(left, right):
    return jnp.dot(left, right, preferred_element_type=jnp.float32)


def scalar_spec():
    return pl.BlockSpec(memory_space=pltpu.SMEM)


def whole_spec():
    return pl.BlockSpec(memory_space=pltpu.VMEM)


def any_spec():
    return pl.BlockSpec(memory_space=pltpu.HBM)


def in_hbm(values):
    return [pltpu.with_memory_space_constraint(value, pltpu.HBM) for value in values]


def start_copies(copies, sems, first=0):
    handles = [
        pltpu.make_async_copy(source, target, sems.at[first + at])
        for at, (source, target) in enumerate(copies)
    ]
    for handle in handles:
        handle.start()
    return handles


def pack_heads(w_query, key_weight, value_weight, places, head_dim):
    rows = w_query.shape[0]
    width = 2 * head_dim

    def kernel(place_ref, query_ref, key_ref, value_ref, *out_refs):
        shard = place_ref[0]
        core = place_ref[1]
        for step, out_ref in enumerate(out_refs):
            other = shard ^ step
            out_ref[:, :width] = query_ref[
                :, pl.ds(pl.multiple_of((2 * other + core) * width, width), width)
            ]
            lanes = pl.ds(pl.multiple_of(other * width, width), width)
            keys = key_ref[:, lanes].astype(jnp.float32)
            values = value_ref[:, lanes].astype(jnp.float32)
            lower = lower_lanes(keys.shape, head_dim)
            first = jnp.where(lower, keys, pltpu.roll(values, head_dim, 1))
            second = jnp.where(lower, pltpu.roll(keys, head_dim, 1), values)
            out_ref[:, width:] = jnp.where(core == 0, first, second).astype(jnp.bfloat16)

    return pl.pallas_call(
        kernel,
        name="pack_heads",
        in_specs=[scalar_spec()] + [whole_spec()] * 3,
        out_shape=(jax.ShapeDtypeStruct((rows, 2 * width), jnp.bfloat16),) * 4,
    )(places, w_query, key_weight, value_weight)


def attention_forward(head_dim, block):
    score_scale = head_dim ** (-0.5)
    assert score_scale == 2.0 ** round(math.log2(score_scale))
    width = 2 * head_dim

    def kernel(
        place_ref, gain_ref, piece_0, piece_1, piece_2, piece_3, query_gain_ref,
        key_gain_ref, cos_hbm, sin_hbm, doc_col_hbm, doc_row_ref, *refs,
    ):
        x_refs = refs[:8]
        mix_ref, normed_out, raw_out, lse_out, weight_out = refs[8:13]
        query_scr, key_scr, value_scr, x_scr, sems = refs[13:18]
        cos_ref, sin_ref, doc_col_ref, normed_ref, raw_ref, lse_ref, weight_ref = refs[18:]
        total = cos_ref.shape[0]
        shard = place_ref[0]
        rank = 2 * shard + place_ref[1]
        piece_rows = piece_0.shape[0]
        own_rows = total // 8
        copies = []
        for step, piece in enumerate((piece_0, piece_1, piece_2, piece_3)):
            first = pl.multiple_of((shard ^ step) * piece_rows, piece_rows)
            copies.append((piece, weight_ref.at[pl.ds(first, piece_rows), :]))
        for step, x_ref in enumerate(x_refs):
            copies.append((x_ref, x_scr.at[pl.ds(step * own_rows, own_rows), :]))
        copies += [(cos_hbm, cos_ref), (sin_hbm, sin_ref), (doc_col_hbm, doc_col_ref)]
        handles = start_copies(copies, sems)
        for handle in handles:
            handle.wait()
        outward = start_copies([(weight_ref, weight_out)], sems, len(copies))

        def normalize(step, carry):
            rows = pl.ds(pl.multiple_of(step * own_rows, own_rows), own_rows)
            x = x_scr[rows, :].astype(jnp.float32)
            normed_ref[rows, :] = (x * rms_scale(x) * gain_ref[...]).astype(jnp.bfloat16)
            return carry

        lax.fori_loop(0, 8, normalize, 0)
        for half in range(0, total, 4 * own_rows):
            raw = dot_plain(normed_ref[pl.ds(half, 4 * own_rows), :], weight_ref[...])
            for step in range(4):
                mask = xor_order[half // own_rows + step]
                first = pl.multiple_of((rank ^ mask) * own_rows, own_rows)
                raw_ref[pl.ds(first, own_rows), :] = raw[step * own_rows : (step + 1) * own_rows]
        outward += start_copies(
            [(normed_ref, normed_out), (raw_ref, raw_out)], sems, len(copies) + 1
        )

        def rotate(step, carry):
            rows = pl.ds(pl.multiple_of(step * block, block), block)
            parts = rotated_heads(
                raw_ref[rows, :], query_gain_ref[...], key_gain_ref[...], cos_ref[rows, :],
                sin_ref[rows, :], head_dim,
            )
            query_scr[rows, :] = (parts[4].astype(jnp.bfloat16) * score_scale).astype(jnp.bfloat16)
            key_scr[rows, :] = parts[5].astype(jnp.bfloat16)
            value_scr[rows, :] = parts[6].astype(jnp.bfloat16)
            return carry

        lax.fori_loop(0, total // block, rotate, 0)
        for first in range(0, total, block):
            rows = pl.ds(first, block)
            span = first + block
            stacked = stack_heads(query_scr[rows, :], head_dim)
            allowed = allowed_pairs(
                doc_col_ref[rows, :], doc_row_ref[:, :span], first, block, span
            )
            allowed = jnp.concatenate([allowed, allowed], axis=0)
            scores = dot_last(stacked, key_scr[:span, :])
            powers = jnp.exp(jnp.where(allowed, scores, very_low))
            row_total = jnp.sum(powers, axis=1, keepdims=True)
            probs = (powers * (1.0 / row_total)).astype(jnp.bfloat16)
            mixed = dot_plain(probs, value_scr[:span, :])
            mix_ref[rows, :] = join_heads(mixed, head_dim).astype(jnp.bfloat16)
            lse_ref[pl.ds(2 * first, 2 * block), :] = jnp.log(row_total)
        outward += start_copies([(lse_ref, lse_out)], sems, len(copies) + 3)
        for handle in outward:
            handle.wait()

    def call(places, xs, gain, pieces, query_gain, key_gain, cosine, sine, doc_column, doc_row):
        total, model = cosine.shape[0], xs[0].shape[1]
        return pl.pallas_call(
            kernel,
            name="attention_forward",
            in_specs=[scalar_spec(), whole_spec()]
            + [any_spec()] * 4
            + [whole_spec()] * 2
            + [any_spec()] * 3
            + [whole_spec()]
            + [any_spec()] * 8,
            out_specs=(whole_spec(),) + (any_spec(),) * 4,
            compiler_params=pltpu.CompilerParams(vmem_limit_bytes=32 << 20),
            out_shape=(
                jax.ShapeDtypeStruct((total, width), jnp.bfloat16),
                pltpu.HBM((total, model), jnp.bfloat16),
                pltpu.HBM((total, 2 * width), jnp.float32),
                pltpu.HBM((2 * total, 1), jnp.float32),
                pltpu.HBM((model, 2 * width), jnp.bfloat16),
            ),
            scratch_shapes=[pltpu.VMEM((total, width), jnp.bfloat16)] * 3
            + [
                pltpu.VMEM((total, model), jnp.bfloat16),
                pltpu.SemaphoreType.DMA((19,)),
                pltpu.VMEM((total, width), jnp.float32),
                pltpu.VMEM((total, width), jnp.float32),
                pltpu.VMEM((total, 1), jnp.int32),
                pltpu.VMEM((total, model), jnp.bfloat16),
                pltpu.VMEM((total, 2 * width), jnp.float32),
                pltpu.VMEM((2 * total, 1), jnp.float32),
                pltpu.VMEM((model, 2 * width), jnp.bfloat16),
            ],
        )(
            places, gain, *in_hbm(pieces), query_gain, key_gain,
            *in_hbm((cosine, sine, doc_column)), doc_row, *in_hbm(xs),
        )

    return call


def residual_stage(places, mix_pieces, out_pieces, xs, mlp_gain):
    total, model = 8 * xs[0].shape[0], xs[0].shape[1]
    width = mix_pieces[0].shape[1]
    own_rows = out_pieces[0].shape[0]

    def kernel(place_ref, gain_ref, *refs):
        mix_refs = refs[:8]
        out_refs = refs[8:16]
        x_refs = refs[16:24]
        normed_ref, mixed_out, cols_out, resid_out, hat_out, scale_ref = refs[24:30]
        weight_scr, x_scr, sems, mixed_ref, cols_ref, resid_ref, hat_ref = refs[30:]
        rank = 2 * place_ref[0] + place_ref[1]
        copies = []
        for mask, ref in zip(xor_order, out_refs):
            first = pl.multiple_of((rank ^ mask) * own_rows, own_rows)
            copies.append((ref, weight_scr.at[pl.ds(first, own_rows), :]))
        for step, row_mask in enumerate(xor_order):
            first = pl.multiple_of((rank ^ row_mask) * own_rows, own_rows)
            for mask, ref in zip(xor_order, mix_refs):
                lanes = pl.ds(pl.multiple_of((rank ^ mask) * width, width), width)
                copies.append(
                    (
                        ref.at[pl.ds(first, own_rows), :],
                        mixed_ref.at[pl.ds(step * own_rows, own_rows), lanes],
                    )
                )
        for step, ref in enumerate(x_refs):
            copies.append((ref, x_scr.at[pl.ds(step * own_rows, own_rows), :]))
        handles = start_copies(copies, sems)
        for handle in handles:
            handle.wait()
        cols_ref[...] = weight_scr[:, pl.ds(pl.multiple_of(rank * width, width), width)]
        outward = start_copies(
            [(mixed_ref, mixed_out), (cols_ref, cols_out)], sems, len(copies)
        )
        for first in range(0, total, total // 4):
            rows = pl.ds(first, total // 4)
            resid = x_scr[rows, :].astype(jnp.float32) + dot_last(
                mixed_ref[rows, :], weight_scr[...]
            )
            scale = rms_scale(resid)
            hat = resid * scale
            normed_ref[rows, :] = (hat * gain_ref[...]).astype(jnp.bfloat16)
            if first == 0:
                resid_ref[...] = resid[:own_rows]
                hat_ref[...] = hat[:own_rows]
                scale_ref[...] = scale[:own_rows]
                outward += start_copies(
                    [(resid_ref, resid_out), (hat_ref, hat_out)], sems, len(copies) + 2
                )
        for handle in outward:
            handle.wait()

    return pl.pallas_call(
        kernel,
        name="residual_stage",
        in_specs=[scalar_spec(), whole_spec()] + [any_spec()] * 24,
        out_specs=(whole_spec(),) + (any_spec(),) * 4 + (whole_spec(),),
        compiler_params=pltpu.CompilerParams(vmem_limit_bytes=24 << 20),
        out_shape=(
            jax.ShapeDtypeStruct((total, model), jnp.bfloat16),
            pltpu.HBM((total, model), jnp.bfloat16),
            pltpu.HBM((model, width), jnp.bfloat16),
            pltpu.HBM((own_rows, model), jnp.float32),
            pltpu.HBM((own_rows, model), jnp.float32),
            jax.ShapeDtypeStruct((own_rows, 1), jnp.float32),
        ),
        scratch_shapes=[
            pltpu.VMEM((model, model), jnp.bfloat16),
            pltpu.VMEM((total, model), jnp.bfloat16),
            pltpu.SemaphoreType.DMA((84,)),
            pltpu.VMEM((total, model), jnp.bfloat16),
            pltpu.VMEM((model, width), jnp.bfloat16),
            pltpu.VMEM((own_rows, model), jnp.float32),
            pltpu.VMEM((own_rows, model), jnp.float32),
        ],
    )(places, mlp_gain, *in_hbm((*mix_pieces, *out_pieces, *xs)))


def stack_rows(pieces):
    rows, width = pieces[0].shape

    def kernel(*refs):
        out_ref, sems = refs[-2:]
        handles = start_copies(
            [(ref, out_ref.at[pl.ds(at * rows, rows), :]) for at, ref in enumerate(refs[:-2])],
            sems,
        )
        for handle in handles:
            handle.wait()

    return pl.pallas_call(
        kernel,
        name="stack_rows",
        in_specs=[any_spec()] * len(pieces),
        compiler_params=pltpu.CompilerParams(vmem_limit_bytes=8 << 20),
        scratch_shapes=[pltpu.SemaphoreType.DMA((len(pieces),))],
        out_shape=jax.ShapeDtypeStruct((rows * len(pieces), width), pieces[0].dtype),
    )(*pieces)


def attention_backward(head_dim, block):
    score_scale = head_dim ** (-0.5)
    assert score_scale == 2.0 ** round(math.log2(score_scale))
    width = 2 * head_dim

    def kernel(
        place_ref, raw_ref, mix_ref, out_cols_ref, lse_ref, query_gain_ref,
        key_gain_ref, cos_ref, sin_ref, doc_col_ref, doc_row_ref, normed_ref, *refs,
    ):
        resid_refs = refs[:8]
        grads_out_ref, query_part_ref, key_part_ref, resid_own_ref = refs[8:12]
        refs = refs[12:]
        piece_refs = refs[:8]
        query_scr, key_scr, value_scr, mix_grad_scr, grads_ref, key_sum, value_sum = refs[8:15]
        resid_scr, sems = refs[15:]
        total = raw_ref.shape[0]
        own_rows = total // 8
        rank = 2 * place_ref[0] + place_ref[1]
        handles = start_copies(
            [
                (ref, resid_scr.at[pl.ds(step * own_rows, own_rows), :])
                for step, ref in enumerate(resid_refs)
            ],
            sems,
        )

        def rotate(step, carry):
            rows = pl.ds(pl.multiple_of(step * block, block), block)
            parts = rotated_heads(
                raw_ref[rows, :], query_gain_ref[...], key_gain_ref[...], cos_ref[rows, :],
                sin_ref[rows, :], head_dim,
            )
            query_scr[rows, :] = (parts[4].astype(jnp.bfloat16) * score_scale).astype(jnp.bfloat16)
            key_scr[rows, :] = parts[5].astype(jnp.bfloat16)
            value_scr[rows, :] = parts[6].astype(jnp.bfloat16)
            return carry

        lax.fori_loop(0, total // block, rotate, 0)
        for handle in handles:
            handle.wait()
        resid_own_ref[...] = resid_scr[:, pl.ds(pl.multiple_of(rank * width, width), width)]
        for half in range(0, total, 4 * own_rows):
            mix_grad = dot_plain(
                resid_scr[pl.ds(half, 4 * own_rows), :], out_cols_ref[...]
            ).astype(jnp.bfloat16)
            for step in range(4):
                mask = xor_order[half // own_rows + step]
                first = pl.multiple_of((rank ^ mask) * own_rows, own_rows)
                mix_grad_scr[pl.ds(first, own_rows), :] = mix_grad[
                    step * own_rows : (step + 1) * own_rows
                ]
        query_gain = query_gain_ref[...]
        key_gain = key_gain_ref[...]

        def heads_of(rows):
            return rotated_heads(
                raw_ref[rows, :], query_gain, key_gain, cos_ref[rows, :], sin_ref[rows, :],
                head_dim,
            )

        def unrotated(grad, rows):
            return grad * cos_ref[rows, :] - swap_halves(grad, head_dim) * sin_ref[rows, :]

        def norm_back(upstream, hat, norm, gain):
            scaled = upstream * gain
            return norm * (scaled - hat * pair_scale(scaled * hat, head_dim))

        key_sum[...] = jnp.zeros_like(key_sum)
        value_sum[...] = jnp.zeros_like(value_sum)
        wide = 2 * block

        def query_block(step, query_part):
            first = pl.multiple_of(step * block, block)
            rows = pl.ds(first, block)
            stacked = stack_heads(query_scr[rows, :], head_dim)
            stacked_grad = stack_heads(mix_grad_scr[rows, :], head_dim)
            mixed = mix_ref[rows, :].astype(jnp.float32)
            delta = jnp.sum(
                stacked_grad.astype(jnp.float32) * jnp.concatenate([mixed, mixed], axis=0),
                axis=1,
                keepdims=True,
            )
            lse = lse_ref[pl.ds(pl.multiple_of(2 * first, 2 * block), 2 * block), :]
            doc_column = doc_col_ref[rows, :]

            def key_block(at, rotated):
                begin = pl.multiple_of(at * wide, wide)
                keys = pl.ds(begin, wide)
                allowed = allowed_pairs(
                    doc_column, doc_row_ref[:, keys], first - begin, block, wide
                )
                allowed = jnp.concatenate([allowed, allowed], axis=0)
                scores = dot_last(stacked, key_scr[keys, :])
                probs = jnp.exp(jnp.where(allowed, scores - lse, very_low))
                prob_grad = dot_last(stacked_grad, value_scr[keys, :])
                score_grad = (probs * (prob_grad - delta)).astype(jnp.bfloat16)
                key_sum[keys, :] += dot_first(score_grad, stacked)
                value_sum[keys, :] += dot_first(probs.astype(jnp.bfloat16), stacked_grad)
                return rotated + dot_plain(score_grad, key_scr[keys, :])

            rotated = lax.fori_loop(
                0, step // 2 + 1, key_block, jnp.zeros((2 * block, width), jnp.float32)
            )
            query_hat, query_norm = heads_of(rows)[:2]
            straight = unrotated(join_heads(rotated, head_dim) * score_scale, rows)
            grads_ref[rows, :width] = norm_back(
                straight, query_hat, query_norm, query_gain
            ).astype(jnp.bfloat16)
            return query_part + jnp.sum(straight * query_hat, axis=0, keepdims=True)

        zero_part = jnp.zeros((1, width), jnp.float32)
        query_part = lax.fori_loop(0, total // block, query_block, zero_part)

        def finish_keys(step, key_part):
            rows = pl.ds(pl.multiple_of(step * block, block), block)
            key_hat, key_norm = heads_of(rows)[2:4]
            summed = key_sum[rows, :]
            summed = summed + pltpu.roll(summed, head_dim, 1)
            values = value_sum[rows, :]
            values = values + pltpu.roll(values, head_dim, 1)
            straight = unrotated(summed, rows)
            key_grad = norm_back(straight, key_hat, key_norm, key_gain)
            lower = lower_lanes(key_grad.shape, head_dim)
            grads_ref[rows, width:] = jnp.where(lower, key_grad, values).astype(jnp.bfloat16)
            return key_part + jnp.sum(straight * key_hat, axis=0, keepdims=True)

        key_part = lax.fori_loop(0, total // block, finish_keys, zero_part)
        query_part_ref[...] = query_part
        key_part_ref[...] = key_part
        for step, mask in enumerate(xor_order):
            first = pl.multiple_of((rank ^ mask) * own_rows, own_rows)
            grads_out_ref[pl.ds(step * own_rows, own_rows), :] = grads_ref[
                pl.ds(first, own_rows), :
            ]
        for mask, piece_ref in enumerate(piece_refs):
            lanes = pl.ds(pl.multiple_of((rank ^ mask) * width, width), width)
            piece_ref[...] = dot_first(normed_ref[:, lanes], grads_out_ref[...]).astype(
                jnp.bfloat16
            )

    def call(
        places, raw, mix, resids, out_cols, lse, query_gain, key_gain, cosine, sine, doc_col,
        doc_row, normed,
    ):
        total = raw.shape[0]
        return pl.pallas_call(
            kernel,
            name="attention_backward",
            in_specs=[scalar_spec()] + [whole_spec()] * 11 + [any_spec()] * 8,
            compiler_params=pltpu.CompilerParams(vmem_limit_bytes=36 << 20),
            out_shape=(
                jax.ShapeDtypeStruct((total, 2 * width), jnp.bfloat16),
                jax.ShapeDtypeStruct((1, width), jnp.float32),
                jax.ShapeDtypeStruct((1, width), jnp.float32),
                jax.ShapeDtypeStruct((total, width), jnp.bfloat16),
            )
            + (jax.ShapeDtypeStruct((width, 2 * width), jnp.bfloat16),) * 8,
            scratch_shapes=[pltpu.VMEM((total, width), jnp.bfloat16)] * 4
            + [pltpu.VMEM((total, 2 * width), jnp.bfloat16)]
            + [pltpu.VMEM((total, width), jnp.float32)] * 2
            + [pltpu.VMEM((total, normed.shape[1]), jnp.bfloat16), pltpu.SemaphoreType.DMA((8,))],
        )(
            places, raw, mix, out_cols, lse, query_gain, key_gain, cosine, sine, doc_col,
            doc_row, normed, *in_hbm(resids),
        )

    return call


def unpack_heads(places, summed, head_dim):
    rows = summed.shape[0]
    width = 2 * head_dim
    model = 8 * width

    def kernel(place_ref, sum_ref, query_ref, key_ref, value_ref, out_ref):
        shard = place_ref[0]
        core = place_ref[1]
        for step in range(4):
            other = shard ^ step
            first = sum_ref[:, pl.ds(4 * step * width, 2 * width)].astype(jnp.float32)
            second = sum_ref[:, pl.ds((4 * step + 2) * width, 2 * width)].astype(jnp.float32)
            even = jnp.where(core == 0, first, second)
            odd = jnp.where(core == 0, second, first)
            query_ref[:, pl.ds(pl.multiple_of(2 * other * width, width), width)] = even[:, :width]
            query_ref[:, pl.ds(pl.multiple_of((2 * other + 1) * width, width), width)] = odd[
                :, :width
            ]
            even = even[:, width:]
            odd = odd[:, width:]
            lower = lower_lanes(even.shape, head_dim)
            lanes = pl.ds(pl.multiple_of(other * width, width), width)
            key_ref[:, lanes] = jnp.where(lower, even, pltpu.roll(odd, head_dim, 1))
            value_ref[:, lanes] = jnp.where(lower, pltpu.roll(even, head_dim, 1), odd)
        out_ref[...] = sum_ref[:, 2 * model :].astype(jnp.float32)

    return pl.pallas_call(
        kernel,
        name="unpack_heads",
        in_specs=[scalar_spec(), whole_spec()],
        out_shape=(
            jax.ShapeDtypeStruct((rows, model), jnp.float32),
            jax.ShapeDtypeStruct((rows, model // 2), jnp.float32),
            jax.ShapeDtypeStruct((rows, model // 2), jnp.float32),
            jax.ShapeDtypeStruct((rows, summed.shape[1] - 2 * model), jnp.float32),
        ),
    )(places, summed)


def heads_body(
    tokens_in,
    doc_lengths,
    attn_gain,
    w_query,
    key_weight,
    value_weight,
    w_output,
    query_norm_gain,
    key_norm_gain,
    mlp_gain,
    w_gate,
    w_up,
    w_down,
    out_grad,
):
    row_count, model_width = tokens_in.shape
    head_dim = query_norm_gain.shape[0]
    total = row_count * 8
    half_rows = total // 2
    block = 256
    core = lax.axis_index("seq")
    shard = lax.axis_index("shard")
    places = jnp.stack([shard, core]).astype(jnp.int32)

    x_near = gather_near(tokens_in)
    head_pieces = pack_heads(w_query, key_weight, value_weight, places, head_dim)
    head_pieces = [head_pieces[0]] + [
        group_swap(head_pieces[step], 2 * step) for step in (1, 2, 3)
    ]
    x_far = gather_far(x_near)
    x_pieces = x_near + x_far

    out_near = lax.dynamic_slice_in_dim(w_output, core * row_count, row_count)
    out_local = lax.dynamic_slice_in_dim(w_output, (1 - core) * row_count, row_count)
    out_own = after(out_near, x_near[1:])
    out_near = [out_own]
    for mask in (2, 4, 6):
        out_near.append(group_swap(out_own, mask))
    out_pieces = out_near + [out_local] + gather_far(out_near[1:])

    index = jnp.arange(total, dtype=jnp.int32)
    docs, offsets = doc_info(doc_lengths[0], index)
    half_dim = head_dim // 2
    inverse_freq = rope_base ** (-(jnp.arange(half_dim, dtype=jnp.float32) * 2.0 / head_dim))
    angles = offsets.astype(jnp.float32)[:, None] * jnp.tile(inverse_freq, 4)[None, :]
    cosine = jnp.cos(angles)
    sine = jnp.where(lower_lanes(angles.shape, half_dim), -1.0, 1.0) * jnp.sin(angles)
    doc_column = docs[:, None]
    doc_row = docs[None, :]
    query_gain = jnp.concatenate([query_norm_gain] * 2)[None, :]
    key_gain = jnp.concatenate([key_norm_gain] * 2)[None, :]

    mix, normed, raw, lse, head_weight = attention_forward(head_dim, block)(
        places, x_pieces, attn_gain[None, :], head_pieces, query_gain, key_gain, cosine, sine,
        doc_column, doc_row,
    )
    mix_near = gather_near(mix)
    mix_far = gather_far(mix_near)
    grad_own = after(out_grad, mix_near[1:])
    grad_near = [grad_own]
    for mask in (2, 4, 6):
        grad_near.append(group_swap(grad_own, mask))
    grad_all = stack_rows(grad_near + gather_far(grad_near))

    normed_mid, mix_all, out_cols, own_resid, own_hat, own_scale = residual_stage(
        places, mix_near + mix_far, out_pieces, x_pieces, mlp_gain[None, :]
    )

    hidden_rows = w_gate.shape[0] // 2

    def own_rows(weight):
        return lax.dynamic_slice_in_dim(weight, core * hidden_rows, hidden_rows)

    gate_rows = own_rows(w_gate)
    up_rows = own_rows(w_up)
    down_rows = own_rows(w_down)
    gate = dot_last(normed_mid, gate_rows)
    up = dot_last(normed_mid, up_rows)
    grad_hidden = dot_last(grad_all, down_rows)
    gate_sig = jax.nn.sigmoid(gate)
    hidden = (gate * gate_sig * up).astype(jnp.bfloat16)
    gate_grad = (grad_hidden * up * gate_sig * (1.0 + gate * (1.0 - gate_sig))).astype(jnp.bfloat16)
    up_grad = (grad_hidden * gate * gate_sig).astype(jnp.bfloat16)

    def mid_part(first):
        rows = slice(first, first + half_rows)
        return dot_plain(gate_grad[rows], gate_rows) + dot_plain(up_grad[rows], up_rows)

    mlp_grads = jnp.concatenate(
        [
            dot_first(hidden, grad_all).astype(jnp.bfloat16),
            dot_first(gate_grad, normed_mid).astype(jnp.bfloat16),
            dot_first(up_grad, normed_mid).astype(jnp.bfloat16),
        ],
        axis=0,
    )
    mlp_sums = lax.psum(mlp_grads, "rep").astype(jnp.float32)

    gate_grad, up_grad = after((gate_grad, up_grad), mlp_grads)
    grad_mid = scatter_sum(mid_part(0), mid_part(half_rows))
    grad_resid = out_grad.astype(jnp.float32) + root_mean_backward(
        own_hat, own_scale, mlp_gain, grad_mid
    )
    mlp_gain_part = jnp.sum(grad_mid * own_hat, axis=0)
    resid_near = gather_near(grad_resid.astype(jnp.bfloat16))
    resid_pieces = resid_near + gather_far(resid_near)

    act_out = own_resid + scatter_sum(
        dot_plain(hidden[:half_rows], down_rows), dot_plain(hidden[half_rows:], down_rows)
    )

    backward = attention_backward(head_dim, block)(
        places, raw, mix, resid_pieces, out_cols, lse, query_gain, key_gain, cosine, sine,
        doc_column, doc_row, normed,
    )
    head_grads, query_part, key_part, resid_own = backward[:4]
    weight_pieces = backward[4:]
    weight_pieces = [weight_pieces[0]] + [
        group_swap(weight_pieces[mask], mask) for mask in range(1, 8)
    ]
    out_grads = dot_first(resid_own, mix_all).astype(jnp.bfloat16)
    grad_in_norm = scatter_sum(
        dot_last(head_grads[:half_rows], head_weight),
        dot_last(head_grads[half_rows:], head_weight),
    )
    own_x = tokens_in.astype(jnp.float32)
    own_norm = rms_scale(own_x)
    x_hat = own_x * own_norm
    in_grad = grad_resid + root_mean_backward(x_hat, own_norm, attn_gain, grad_in_norm)
    attn_gain_part = jnp.sum(grad_in_norm * x_hat, axis=0)
    query_gain_part = query_part[0, :head_dim] + query_part[0, head_dim:]
    gains = sum_everywhere(
        jnp.concatenate(
            [attn_gain_part, mlp_gain_part, query_gain_part, key_part[0, :head_dim]]
        )[None, :]
    )[0]
    attn_grads = rep_halving_sum(
        jnp.concatenate(weight_pieces + [out_grads], axis=1), grad_in_norm, gains
    )
    grad_query, grad_key, grad_value, grad_output = unpack_heads(places, attn_grads, head_dim)
    return (
        act_out,
        in_grad,
        gains[:model_width],
        grad_query,
        grad_key,
        grad_value,
        grad_output,
        gains[2 * model_width : 2 * model_width + head_dim],
        gains[2 * model_width + head_dim :],
        gains[model_width : 2 * model_width],
        mlp_sums[hidden_rows : 2 * hidden_rows],
        mlp_sums[2 * hidden_rows :],
        mlp_sums[:hidden_rows],
    )


def local_by_heads(*arrays):
    return heads_body(*arrays)


def solution(mesh):
    placed = (
        P(("rep", "shard", "seq"), None),
        P("rep", None),
        P(),
        P("shard", None),
        P("shard", None),
        P("shard", None),
        P("shard", None),
        P(),
        P(),
        P(),
        P("shard", None),
        P("shard", None),
        P("shard", None),
        P(("rep", "shard", "seq"), None),
    )
    sizes = dict(mesh.shape)
    by_heads = sizes["rep"] == 4 and sizes["shard"] == 4 and sizes["seq"] == 2
    return jax.shard_map(
        local_by_heads if by_heads else local,
        mesh=mesh,
        in_specs=placed,
        out_specs=(
            P(("rep", "shard", "seq"), None),
            P(("rep", "shard", "seq"), None),
            P(),
            P(("shard", "seq"), None),
            P(("shard", "seq"), None),
            P(("shard", "seq"), None),
            P(("shard", "seq"), None),
            P(),
            P(),
            P(),
            P(("shard", "seq"), None),
            P(("shard", "seq"), None),
            P(("shard", "seq"), None),
        ),
        check_vma=False,
    )
```
